32 devices in a mesh: dp: 8 (over z, y), tensor: 4 (over x, core).
Axes of the slice: x: 2, y: 2, z: 4, core: 2. Of those that a mesh axis runs over, the one named last changes fastest.
Arguments:
- tokens_long: bfloat16 [8, 1024, 1152], P('dp'), may hold values from -6 to 6
- tokens_short: bfloat16 [8, 256, 1152], P('dp'), may hold values from -6 to 6
- cond_long: bfloat16 [8, 1152], P('dp'), may hold values from -6 to 6
- cond_short: bfloat16 [8, 1152], P('dp'), may hold values from -6 to 6
- perm_long: int32 [8, 1024], P('dp'), may hold values from 0 to 1023, each once within a row
- perm_short: int32 [8, 256], P('dp'), may hold values from 0 to 255, each once within a row
- ada_weight: bfloat16 [2, 1152, 6912], P(None, None, 'dp'), may hold values from -0.09375 to 0.09375
- ada_bias: bfloat16 [2, 6912], P(None, 'dp'), may hold values from -1.5 to 1.5
- qkv_weight: bfloat16 [2, 1152, 3, 1152], P(None, None, None, 'tensor'), may hold values from -0.1875 to 0.1875
- qv_bias: bfloat16 [2, 2, 1152], P(None, None, 'tensor'), may hold values from -0.59765625 to 0.59765625
- proj_weight: bfloat16 [2, 1152, 1152], P(None, 'tensor'), may hold values from -0.375 to 0.375
- proj_bias: bfloat16 [2, 1152], replicated, may hold values from -1.796875 to 1.796875
- up_weight: bfloat16 [2, 1152, 4608], P(None, None, 'tensor'), may hold values from -0.1875 to 0.1875
- up_bias: bfloat16 [2, 4608], P(None, 'tensor'), may hold values from -3 to 3
- down_weight: bfloat16 [2, 4608, 1152], P(None, 'tensor'), may hold values from -0.09375 to 0.09375
- down_bias: bfloat16 [2, 1152], replicated, may hold values from -1.796875 to 1.796875
- mask_token: bfloat16 [1152], replicated, may hold values from -6 to 6
- cot_long: bfloat16 [8, 1024, 1152], P('dp'), may hold values from -6 to 6
- cot_short: bfloat16 [8, 256, 1152], P('dp'), may hold values from -6 to 6
Outputs:
- result_long: bfloat16 [8, 1024, 1152], P('dp')
- result_short: bfloat16 [8, 256, 1152], P('dp')
- dtok_long: bfloat16 [8, 1024, 1152], P('dp')
- dtok_short: bfloat16 [8, 256, 1152], P('dp')
- dcond_long: bfloat16 [8, 1152], P('dp')
- dcond_short: bfloat16 [8, 1152], P('dp')
- grad_ada_weight: float32 [2, 1152, 6912], P(None, None, 'dp')
- grad_ada_bias: float32 [2, 6912], P(None, 'dp')
- grad_qkv_weight: float32 [2, 1152, 3, 1152], P(None, 'dp', None, 'tensor')
- grad_qv_bias: float32 [2, 2, 1152], P(None, None, 'tensor')
- grad_proj_weight: float32 [2, 1152, 1152], P(None, 'tensor', 'dp')
- grad_proj_bias: float32 [2, 1152], replicated
- grad_up_weight: float32 [2, 1152, 4608], P(None, 'dp', 'tensor')
- grad_up_bias: float32 [2, 4608], P(None, 'tensor')
- grad_down_weight: float32 [2, 4608, 1152], P(None, 'tensor', 'dp')
- grad_down_bias: float32 [2, 1152], replicated
- grad_mask_token: float32 [1152], replicated
The draws below stay inside these ranges and needn't reach their ends.
Inputs may be any that keep to these rules, and one draw needn't show every extreme that they name: `perm_long`: each row lists every position of its latent once; its first 512 entries are the kept positions. `perm_short`: each row lists every position of its latent once; its first 128 entries are the kept positions.
All inputs are finite; a program needn't handle non-finite values.
Results may differ from the reference program's by a relative error of at most 0.029.
Values may be sent and summed in bfloat16 or wider, within the bound.
No kernel may reach another device: no remote copies, remote signals or barrier semaphores. Data moves between devices by JAX's collectives and lax.ppermute only.
A program may use at most 320 MiB of HBM per device.

```python
import math
import jax
import jax.numpy as jnp
from jax import lax

D = 1152
HEADS = 16
HEAD_DIM = 72
FF = 4608
LONG_LEN = 1024
SHORT_LEN = 256
N_LONG = 8
N_SHORT = 8
N_TENSOR = 4


def levels(own_key, extent, cuts, low, largest):
    def one(dim, shards_of):
        heights = jax.random.uniform(jax.random.fold_in(jax.random.fold_in(own_key, 6), dim), (shards_of,), jnp.float32, low / len(cuts), largest / len(cuts))
        return jnp.repeat(jnp.exp(heights), extent[dim] // shards_of).reshape((-1,) + (1,) * (len(extent) - dim - 1))

    loudness = one(*cuts[0])
    for cut in cuts[1:]:
        loudness = loudness * one(*cut)
    return loudness


def centred(stream_key, shape, width, limit, shards=(), kind=jnp.bfloat16):
    drawn = width * jax.random.normal(stream_key, shape, jnp.float32)
    if shards:
        drawn = drawn * levels(stream_key, shape, shards, -0.22, 0.18)
    return jnp.clip(drawn, -limit, limit).astype(kind)


def setup_inputs(seed: int = 0) -> dict:
    keys = jax.random.split(jax.random.key(seed), 20)
    return {
        "tokens_long": centred(keys[0], (N_LONG, LONG_LEN, D), 1.0, 6.0, ((0, 8),)),
        "tokens_short": centred(keys[1], (N_SHORT, SHORT_LEN, D), 1.0, 6.0, ((0, 8),)),
        "cond_long": centred(keys[2], (N_LONG, D), 1.0, 6.0, ((0, 8),)),
        "cond_short": centred(keys[3], (N_SHORT, D), 1.0, 6.0, ((0, 8),)),
        "perm_long": jax.vmap(lambda own: jax.random.permutation(own, LONG_LEN))(jax.random.split(keys[4], N_LONG)).reshape((N_LONG, LONG_LEN)).astype(jnp.int32),
        "perm_short": jax.vmap(lambda own: jax.random.permutation(own, SHORT_LEN))(jax.random.split(keys[5], N_SHORT)).reshape((N_SHORT, SHORT_LEN)).astype(jnp.int32),
        "ada_weight": centred(keys[6], (2, D, 6 * D), (4 * D) ** -0.5, 0.09375, ((2, 8),)),
        "ada_bias": centred(keys[7], (2, 6 * D), 0.25, 1.5, ((1, 8),)),
        "qkv_weight": centred(keys[8], (2, D, 3, D), D ** -0.5, 0.1875, ((3, 4),)),
        "qv_bias": centred(keys[9], (2, 2, D), 0.1, 0.59765625, ((2, 4),)),
        "proj_weight": centred(keys[10], (2, D, D), (D // 4) ** -0.5, 0.375, ((1, 4),)),
        "proj_bias": centred(keys[11], (2, D), 0.3, 1.796875),
        "up_weight": centred(keys[12], (2, D, FF), D ** -0.5, 0.1875, ((2, 4),)),
        "up_bias": centred(keys[13], (2, FF), 0.5, 3.0, ((1, 4),)),
        "down_weight": centred(keys[14], (2, FF, D), FF ** -0.5, 0.09375, ((1, 4),)),
        "down_bias": centred(keys[15], (2, D), 0.3, 1.796875),
        "mask_token": centred(keys[16], (D,), 1.0, 6.0),
        "cot_long": centred(keys[17], (N_LONG, LONG_LEN, D), 1.0, 6.0, ((0, 8),)),
        "cot_short": centred(keys[18], (N_SHORT, SHORT_LEN, D), 1.0, 6.0, ((0, 8),)),
    }


HIGHEST = lax.Precision.HIGHEST
EPSILON = 1e-06

@jax.custom_vjp
def low(v):
    return lax.optimization_barrier(v.astype(jnp.bfloat16)).astype(jnp.float32)

@jax.custom_vjp
def low_back(v):
    return v

def low_keep(v):
    return (low(v), None)

def low_pass(kept, grad):
    return (grad,)

def back_keep(v):
    return (v, None)

def back_low(kept, grad):
    return (low(grad),)
low.defvjp(low_keep, low_pass)
low_back.defvjp(back_keep, back_low)

def layer_norm(values):
    center = values - lax.optimization_barrier(jnp.mean(values, axis=-1, keepdims=True))
    spread = lax.optimization_barrier(jnp.mean(center * center, axis=-1, keepdims=True))
    return center * lax.rsqrt(spread + EPSILON)

def sincos_table(grid_side, features):
    quarter = features // 4
    frequency = 1.0 / 10000.0 ** (jnp.arange(quarter, dtype=jnp.float32) / quarter)
    places = jnp.arange(grid_side * grid_side, dtype=jnp.int32)
    row_angle = (places // grid_side).astype(jnp.float32)[:, None] * frequency[None, :]
    col_angle = (places % grid_side).astype(jnp.float32)[:, None] * frequency[None, :]
    return jnp.concatenate([jnp.sin(row_angle), jnp.cos(row_angle), jnp.sin(col_angle), jnp.cos(col_angle)], axis=1)

def attention_plain(queries, keys_all, values_all):
    scores = low_back(jnp.einsum('qhe,khe->hqk', queries, keys_all, precision=HIGHEST) * HEAD_DIM ** (-0.5))
    normer = jax.nn.logsumexp(scores, axis=-1, keepdims=True)
    weight_tree = low(jnp.exp(scores - normer))
    return jnp.einsum('hqk,khe->qhe', weight_tree, values_all, precision=HIGHEST)
attention_saved = jax.checkpoint(attention_plain)

def transformer_block(residual_stream, modulation_vector, weight_tree):
    qkv_weight, qv_bias, proj_weight, proj_bias, up_weight, up_bias, down_weight, down_bias = weight_tree
    length, features = residual_stream.shape
    shift_attn, scale_attn, gate_attn, shift_mlp, scale_mlp, gate_mlp = [modulation_vector[position] for position in range(6)]
    normed = low(layer_norm(residual_stream) * (1.0 + scale_attn) + shift_attn)
    bias_rows = jnp.stack([qv_bias[0], jnp.zeros_like(qv_bias[0]), qv_bias[1]])
    merged = jnp.einsum('ld,dte->lte', normed, qkv_weight, precision=HIGHEST) + bias_rows
    merged = low(low_back(merged))
    heads_shape = (length, HEADS, HEAD_DIM)
    attended = attention_saved(merged[:, 0].reshape(heads_shape), merged[:, 1].reshape(heads_shape), merged[:, 2].reshape(heads_shape))
    attended = low(low_back(attended.reshape(length, features)))
    group_width = features // N_TENSOR
    pieces = jnp.einsum('lgi,gio->glo', attended.reshape(length, N_TENSOR, group_width), proj_weight.reshape(N_TENSOR, group_width, features), precision=HIGHEST)
    branch = low_back(lax.optimization_barrier(jnp.sum(low(pieces), axis=0)) + proj_bias)
    residual_stream = residual_stream + gate_attn * branch
    normed = low(layer_norm(residual_stream) * (1.0 + scale_mlp) + shift_mlp)
    hidden = low_back(jnp.dot(normed, up_weight, precision=HIGHEST) + up_bias)
    active = low(jax.nn.gelu(hidden, approximate=True))
    unit_width = active.shape[1] // N_TENSOR
    pieces = jnp.einsum('lgi,gio->glo', active.reshape(length, N_TENSOR, unit_width), down_weight.reshape(N_TENSOR, unit_width, features), precision=HIGHEST)
    branch = low_back(lax.optimization_barrier(jnp.sum(low(pieces), axis=0)) + down_bias)
    return residual_stream + gate_mlp * branch

def latent_pass(token_rows, condition, token_ordering, params):
    ada_weight, ada_bias, qkv_weight, qv_bias, proj_weight, proj_bias, up_weight, up_bias, down_weight, down_bias, mask_token = params
    length, features = token_rows.shape
    visible_count = length // 2
    activated = low(jax.nn.silu(condition))
    modulation_vectors = [low_back(jnp.dot(activated, ada_weight[block_index], precision=HIGHEST) + ada_bias[block_index]).reshape(6, features) for block_index in range(2)]
    stacks = (qkv_weight, qv_bias, proj_weight, proj_bias, up_weight, up_bias, down_weight, down_bias)
    block_parameters = [tuple((stacked[block_index] for stacked in stacks)) for block_index in range(2)]
    encoder_result = transformer_block(jnp.take(token_rows, token_ordering[:visible_count], axis=0), modulation_vectors[0], block_parameters[0])
    inverse = jnp.zeros((length,), jnp.int32).at[token_ordering].set(jnp.arange(length, dtype=jnp.int32))
    filler = jnp.broadcast_to(mask_token, (length - visible_count, features))
    decoder_entry = jnp.take(jnp.concatenate([encoder_result, filler], axis=0), inverse, axis=0) + sincos_table(math.isqrt(length), features)
    return transformer_block(decoder_entry, modulation_vectors[1], block_parameters[1])

def reference(tokens_long, tokens_short, cond_long, cond_short, perm_long, perm_short, ada_weight, ada_bias, qkv_weight, qv_bias, proj_weight, proj_bias, up_weight, up_bias, down_weight, down_bias, mask_token, cot_long, cot_short):
    params = tuple((stacked.astype(jnp.float32) for stacked in (ada_weight, ada_bias, qkv_weight, qv_bias, proj_weight, proj_bias, up_weight, up_bias, down_weight, down_bias, mask_token)))

    def run_group(totals, token_rows, conditions, orderings, cotangents):

        def one_latent(carry, latent):
            tokens_one, cond_one, order_one, cot_one = latent

            def forward(tok_in, cond_in, param_in):
                return latent_pass(tok_in, cond_in, order_one, param_in)
            outcome, pullback = jax.vjp(forward, tokens_one.astype(jnp.float32), cond_one.astype(jnp.float32), params)
            d_tokens, d_cond, d_params = pullback(cot_one.astype(jnp.float32))
            carry = jax.tree.map(jnp.add, carry, d_params)
            return (carry, (outcome.astype(jnp.bfloat16), d_tokens.astype(jnp.bfloat16), d_cond.astype(jnp.bfloat16)))
        return lax.scan(one_latent, totals, (token_rows, conditions, orderings, cotangents))
    zeros = jax.tree.map(jnp.zeros_like, params)
    totals, (res_long, dtok_long, dcond_long) = run_group(zeros, tokens_long, cond_long, perm_long, cot_long)
    totals, (res_short, dtok_short, dcond_short) = run_group(totals, tokens_short, cond_short, perm_short, cot_short)
    return (res_long, res_short, dtok_long, dtok_short, dcond_long, dcond_short, totals[0], totals[1], totals[2], totals[3], totals[4], totals[5], totals[6], totals[7], totals[8], totals[9], totals[10])
```

```python
import math

import jax
import jax.numpy as jnp
from jax import lax
from jax.sharding import PartitionSpec as P

HEAD_DIM = 72
EPSILON = 1e-06
BF16 = jnp.bfloat16
F32 = jnp.float32


def dot(left, right, dims, out=F32):
    result = lax.dot_general(left, right, (dims, ((), ())), preferred_element_type=F32)
    return result.astype(out)


def rows_by(left, right, out=F32):
    return dot(left, right, ((1,), (0,)), out)


def rows_by_t(left, right, out=F32):
    return dot(left, right, ((1,), (1,)), out)


def rows_summed(left, right, out=F32):
    return dot(left, right, ((0,), (0,)), out)


def partners(size, bit):
    return [(index, index ^ bit) for index in range(size)]


def bits_of(size):
    bits = []
    while (1 << len(bits)) < size:
        bits.append(1 << len(bits))
    assert (1 << len(bits)) == size
    return bits


class Links:
    def __init__(self, dp_size, tensor_size):
        self.dp_size = dp_size
        self.tensor_size = tensor_size
        self.dp_bits = bits_of(dp_size)
        self.me = lax.axis_index("dp")
        self.core = lax.rem(lax.axis_index("tensor"), 2)

    def swap(self, value):
        return lax.ppermute(value, "tensor", partners(self.tensor_size, 1))

    def cross(self, value):
        return lax.ppermute(value, "tensor", partners(self.tensor_size, 2))

    def dp_move(self, value, bit):
        return lax.ppermute(value, "dp", partners(self.dp_size, bit))

    def my_bit(self, bit):
        return lax.rem(self.me // bit, 2)

    def gather_relative(self, value):
        held = value[None]
        for bit in self.dp_bits:
            held = jnp.concatenate([held, self.dp_move(held, bit)], axis=0)
        return held

    def exchange_relative(self, value):
        held = value
        for bit in self.dp_bits:
            shaped = held.reshape((self.dp_size // (2 * bit), 2, bit) + held.shape[1:])
            moved = self.dp_move(shaped[:, 1], bit)
            held = jnp.stack([shaped[:, 0], moved], axis=1).reshape(held.shape)
        return held

    def sum_relative(self, value):
        held = value
        for bit in reversed(self.dp_bits):
            moved = self.dp_move(held[bit:].astype(BF16), bit)
            held = held[:bit].astype(F32) + moved.astype(F32)
        return held[0]

    def reorder(self, value):
        held = value
        for bit in self.dp_bits:
            shaped = held.reshape((self.dp_size // (2 * bit), 2, bit) + held.shape[1:])
            flipped = jnp.where(self.my_bit(bit) == 1, shaped[:, ::-1], shaped)
            held = flipped.reshape(held.shape)
        return held

    def scatter_sum(self, value, axis):
        lead, rest = value.shape[:axis], value.shape[axis + 1 :]
        held = value.reshape(lead + (2,) * len(self.dp_bits) + rest)
        for done, bit in enumerate(self.dp_bits):
            place = axis + len(self.dp_bits) - 1 - done
            mine = self.my_bit(bit)
            away = lax.dynamic_index_in_dim(held, 1 - mine, place, keepdims=False)
            kept = lax.dynamic_index_in_dim(held, mine, place, keepdims=False)
            moved = self.dp_move(away, bit)
            held = (kept.astype(F32) + moved.astype(F32)).astype(BF16)
        return held

    def sum_all(self, value):
        held = value
        for bit in self.dp_bits:
            held = held + self.dp_move(held, bit)
        return held


def norm_of(values):
    center = values - jnp.mean(values, axis=-1, keepdims=True)
    spread = jnp.mean(center * center, axis=-1, keepdims=True)
    scale = lax.rsqrt(spread + EPSILON)
    return center * scale, scale


def norm_back(normed, scale, grad):
    return scale * (
        grad
        - jnp.mean(grad, axis=-1, keepdims=True)
        - normed * jnp.mean(grad * normed, axis=-1, keepdims=True)
    )


GELU_A = math.sqrt(2.0 / math.pi)
GELU_B = 0.044715


def gelu(hidden):
    return 0.5 * hidden * (1.0 + jnp.tanh(GELU_A * (hidden + GELU_B * hidden * hidden * hidden)))


def gelu_slope(hidden):
    squared = hidden * hidden
    bent = jnp.tanh(GELU_A * (hidden + GELU_B * hidden * squared))
    return 0.5 * (1.0 + bent) + 0.5 * hidden * (1.0 - bent * bent) * GELU_A * (
        1.0 + 3.0 * GELU_B * squared
    )


def heads_of(part):
    return part.reshape(part.shape[0], -1, HEAD_DIM)


def attend(queries, keys_all, values_all):
    scores = jnp.einsum(
        "qhe,khe->hqk", heads_of(queries), heads_of(keys_all), preferred_element_type=F32
    ) * HEAD_DIM ** (-0.5)
    highest = jnp.max(scores, axis=-1, keepdims=True)
    normer = highest + jnp.log(jnp.sum(jnp.exp(scores - highest), axis=-1, keepdims=True))
    probs = jnp.exp(scores - normer).astype(BF16)
    attended = jnp.einsum(
        "hqk,khe->qhe", probs, heads_of(values_all), preferred_element_type=F32
    )
    return attended.reshape(queries.shape).astype(BF16), normer


def attend_back(queries, keys_all, values_all, normer, d_attended):
    scaling = HEAD_DIM ** (-0.5)
    width = queries.shape[1]
    queries, keys_all, values_all, d_attended = (
        heads_of(part) for part in (queries, keys_all, values_all, d_attended)
    )
    scores = jnp.einsum("qhe,khe->hqk", queries, keys_all, preferred_element_type=F32) * scaling
    probs = jnp.exp(scores - normer)
    d_probs = jnp.einsum("qhe,khe->hqk", d_attended, values_all, preferred_element_type=F32)
    d_scores = (
        probs * (d_probs - jnp.sum(probs * d_probs, axis=-1, keepdims=True))
    ).astype(BF16)
    d_values = jnp.einsum("hqk,qhe->khe", probs.astype(BF16), d_attended, preferred_element_type=F32)
    d_queries = (
        jnp.einsum("hqk,khe->qhe", d_scores, keys_all, preferred_element_type=F32) * scaling
    )
    d_keys = jnp.einsum("hqk,qhe->khe", d_scores, queries, preferred_element_type=F32) * scaling
    return tuple(part.reshape(-1, width) for part in (d_queries, d_keys, d_values))


SHIFT_ATTN, SCALE_ATTN, GATE_ATTN, SHIFT_MLP, SCALE_MLP, GATE_MLP = range(6)


class Block:
    def __init__(self, links, weights, mods, owners):
        self.links = links
        (
            self.qkv_weight,
            self.qv_bias,
            self.proj_weight,
            self.proj_bias,
            self.up_weight,
            self.up_bias,
            self.down_weight,
            self.down_bias,
        ) = weights
        self.mods = mods
        self.owners = owners
        self.width = self.qkv_weight.shape[2]
        bias = self.qv_bias.astype(F32)
        self.qkv_bias = jnp.concatenate([bias[0], jnp.zeros_like(bias[0]), bias[1]])

    def mod(self, chunk, part):
        return self.mods[self.owners[chunk]][part][None]

    def joined(self, part_other, own_of):
        moved = self.links.swap(part_other)
        mine = (own_of() + moved.astype(F32)).astype(BF16)
        far = self.links.cross(mine)
        return mine.astype(F32) + far.astype(F32)

    def members(self, latent):
        return [chunk for chunk, owner in enumerate(self.owners) if owner == latent]

    def qkv_of(self, normed):
        features = normed.shape[1]
        flat = self.qkv_weight.reshape(features, 3 * self.width)
        return (rows_by(normed, flat) + self.qkv_bias[None]).astype(BF16)

    def parts(self, merged):
        return [merged[:, part * self.width : (part + 1) * self.width] for part in range(3)]

    def forward(self, streams):
        swap = self.links.swap
        chunks = range(len(streams))
        saved = [dict() for _ in chunks]
        for c in chunks:
            keep = saved[c]
            keep["x"] = streams[c]
            normed, _ = norm_of(streams[c])
            own = (normed * (1.0 + self.mod(c, SCALE_ATTN)) + self.mod(c, SHIFT_ATTN)).astype(BF16)
            keep["normed_attn"] = (own, swap(own))
            keep["qkv"] = tuple(self.qkv_of(half) for half in keep["normed_attn"])
        outputs = [None] * len(streams)
        for latent in sorted(set(self.owners)):
            halves = [half for c in self.members(latent) for half in saved[c]["qkv"]]
            keys_all = jnp.concatenate([self.parts(half)[1] for half in halves])
            values_all = jnp.concatenate([self.parts(half)[2] for half in halves])
            for c in self.members(latent):
                keep = saved[c]
                keep["keys"], keep["values"] = keys_all, values_all
                other, normer_other = attend(self.parts(keep["qkv"][1])[0], keys_all, values_all)
                part_other = rows_by(other, self.proj_weight, BF16)
                own, normer_own = attend(self.parts(keep["qkv"][0])[0], keys_all, values_all)
                keep["attended"] = (own, other)
                keep["normer"] = (normer_own, normer_other)
                branch = self.joined(
                    part_other, lambda own=own: rows_by(own, self.proj_weight)
                ) + self.proj_bias.astype(F32)
                keep["branch_attn"] = branch
                middle = keep["x"] + self.mod(c, GATE_ATTN) * branch
                keep["middle"] = middle
                normed, _ = norm_of(middle)
                normed = (normed * (1.0 + self.mod(c, SCALE_MLP)) + self.mod(c, SHIFT_MLP)).astype(
                    BF16
                )
                keep["normed_mlp"] = (normed, swap(normed))
                hidden, active = [], []
                for half in keep["normed_mlp"]:
                    raw = rows_by(half, self.up_weight) + self.up_bias.astype(F32)
                    hidden.append(raw)
                    active.append(gelu(raw).astype(BF16))
                keep["hidden"], keep["active"] = tuple(hidden), tuple(active)
                branch = self.joined(
                    rows_by(active[1], self.down_weight, BF16),
                    lambda half=active[0]: rows_by(half, self.down_weight),
                ) + self.down_bias.astype(F32)
                keep["branch_mlp"] = branch
                outputs[c] = middle + self.mod(c, GATE_MLP) * branch
        self.saved = saved
        return outputs

    def backward(self, d_outputs):
        swap = self.links.swap
        saved = self.saved
        chunks = range(len(d_outputs))
        sums = [[0.0] * 6 for _ in set(self.owners)]
        proj_sum, down_sum = 0.0, 0.0

        def add(chunk, part, value):
            sums[self.owners[chunk]][part] = sums[self.owners[chunk]][part] + value

        for c in chunks:
            keep = saved[c]
            d_out = d_outputs[c]
            add(c, GATE_MLP, jnp.sum(d_out * keep["branch_mlp"], axis=0))
            own = (self.mod(c, GATE_MLP) * d_out).astype(BF16)
            down_sum = down_sum + jnp.sum(own.astype(F32), axis=0)
            keep["d_branch_mlp"] = (own, swap(own))
            d_hidden = []
            for grad, hidden in zip(keep["d_branch_mlp"], keep["hidden"]):
                d_active = rows_by_t(grad, self.down_weight)
                d_hidden.append((d_active * gelu_slope(hidden)).astype(BF16))
            keep["d_hidden"] = tuple(d_hidden)
            d_normed = self.joined(
                rows_by_t(d_hidden[1], self.up_weight, BF16),
                lambda half=d_hidden[0]: rows_by_t(half, self.up_weight),
            )
            normed, scale = norm_of(keep["middle"])
            add(c, SCALE_MLP, jnp.sum(d_normed * normed, axis=0))
            add(c, SHIFT_MLP, jnp.sum(d_normed, axis=0))
            d_middle = d_out + norm_back(
                normed, scale, d_normed * (1.0 + self.mod(c, SCALE_MLP))
            )
            keep["d_middle"] = d_middle
            add(c, GATE_ATTN, jnp.sum(d_middle * keep["branch_attn"], axis=0))
            own = (self.mod(c, GATE_ATTN) * d_middle).astype(BF16)
            proj_sum = proj_sum + jnp.sum(own.astype(F32), axis=0)
            keep["d_branch_attn"] = (own, swap(own))
            keep["d_attended"] = tuple(
                rows_by_t(half, self.proj_weight, BF16) for half in keep["d_branch_attn"]
            )
        d_inputs = [None] * len(d_outputs)
        for latent in sorted(set(self.owners)):
            members = self.members(latent)
            d_queries = {}
            d_keys, d_values = 0.0, 0.0
            for c in members:
                keep = saved[c]
                for side in (1, 0):
                    query_grad, key_grad, value_grad = attend_back(
                        self.parts(keep["qkv"][side])[0],
                        keep["keys"],
                        keep["values"],
                        keep["normer"][side],
                        keep["d_attended"][side],
                    )
                    d_queries[c, side] = query_grad.astype(BF16)
                    d_keys = d_keys + key_grad
                    d_values = d_values + value_grad
            d_keys, d_values = d_keys.astype(BF16), d_values.astype(BF16)
            first = 0
            for c in members:
                keep = saved[c]
                halves = []
                for side in (0, 1):
                    count = d_queries[c, side].shape[0]
                    halves.append(
                        jnp.concatenate(
                            [
                                d_queries[c, side],
                                d_keys[first : first + count],
                                d_values[first : first + count],
                            ],
                            axis=1,
                        )
                    )
                    first += count
                keep["d_qkv"] = tuple(halves)
                features = self.qkv_weight.shape[0]
                flat = self.qkv_weight.reshape(features, 3 * self.width)
                d_normed = self.joined(
                    rows_by_t(halves[1], flat, BF16), lambda half=halves[0]: rows_by_t(half, flat)
                )
                normed, scale = norm_of(keep["x"])
                add(c, SCALE_ATTN, jnp.sum(d_normed * normed, axis=0))
                add(c, SHIFT_ATTN, jnp.sum(d_normed, axis=0))
                d_inputs[c] = keep["d_middle"] + norm_back(
                    normed, scale, d_normed * (1.0 + self.mod(c, SCALE_ATTN))
                )
        d_mods = jnp.stack([jnp.stack(rows) for rows in sums])
        return d_inputs, d_mods, proj_sum, down_sum

    def all_rows(self, name):
        return jnp.concatenate([half for keep in self.saved for half in keep[name]])

    def weight_grads(self):
        links = self.links
        blocks = links.dp_size

        def scattered(value):
            lead = value.shape[:-2]
            shaped = value.reshape(lead + (blocks, value.shape[-2] // blocks, value.shape[-1]))
            return links.scatter_sum(shaped, len(lead)).astype(F32)

        d_hidden = self.all_rows("d_hidden")
        down = scattered(rows_summed(self.all_rows("d_branch_mlp"), self.all_rows("active"), BF16))
        up = scattered(rows_summed(self.all_rows("normed_mlp"), d_hidden, BF16))
        proj = scattered(
            rows_summed(self.all_rows("d_branch_attn"), self.all_rows("attended"), BF16)
        )
        normed = self.all_rows("normed_attn")
        d_qkv = self.all_rows("d_qkv")
        qkv = scattered(
            jnp.stack([rows_summed(normed, part, BF16) for part in self.parts(d_qkv)])
        )
        qkv_sums = jnp.sum(d_qkv.astype(F32), axis=0)
        return {
            "qkv": jnp.transpose(qkv, (1, 0, 2)),
            "proj": proj.T,
            "up": up,
            "down": down.T,
            "qv_bias": jnp.stack([qkv_sums[: self.width], qkv_sums[2 * self.width :]]),
            "up_bias": jnp.sum(d_hidden.astype(F32), axis=0),
        }


def pick_matrix(places, length):
    return (places[:, None] == jnp.arange(length, dtype=jnp.int32)[None, :]).astype(BF16)


def table_rows(places, length, features):
    side = math.isqrt(length)
    quarter = features // 4
    frequency = 1.0 / 10000.0 ** (jnp.arange(quarter, dtype=F32) / quarter)
    angle = jnp.arange(side, dtype=jnp.int32).astype(F32)[:, None] * frequency[None, :]
    small = jnp.concatenate([jnp.sin(angle), jnp.cos(angle)], axis=1)
    steps = jnp.arange(side, dtype=jnp.int32)[None, :]
    row_pick = (places[:, None] // side == steps).astype(F32)
    col_pick = (places[:, None] % side == steps).astype(F32)
    return jnp.concatenate(
        [
            jnp.dot(row_pick, small, precision=lax.Precision.HIGHEST),
            jnp.dot(col_pick, small, precision=lax.Precision.HIGHEST),
        ],
        axis=1,
    )


def on_device(dp_size, tensor_size, *arguments):
    (
        tokens_long,
        tokens_short,
        cond_long,
        cond_short,
        perm_long,
        perm_short,
        ada_weight,
        ada_bias,
        qkv_weight,
        qv_bias,
        proj_weight,
        proj_bias,
        up_weight,
        up_bias,
        down_weight,
        down_bias,
        mask_token,
        cot_long,
        cot_short,
    ) = arguments
    assert tokens_long.shape[0] == 1 and tokens_short.shape[0] == 1
    links = Links(dp_size, tensor_size)
    features = tokens_long.shape[2]
    tokens = (tokens_long[0], tokens_short[0])
    cots = (cot_long[0], cot_short[0])
    perms = (perm_long[0], perm_short[0])
    lengths = tuple(rows.shape[0] for rows in tokens)
    kept = tuple(length // 2 for length in lengths)

    cond = jnp.concatenate([cond_long, cond_short]).astype(F32)
    acts = links.gather_relative(jax.nn.silu(cond).astype(BF16))
    flat_acts = acts.reshape(-1, features)
    columns = jnp.einsum("nd,ldm->nlm", flat_acts, ada_weight, preferred_element_type=F32)
    columns = (columns + ada_bias.astype(F32)[None]).astype(BF16)
    columns = columns.reshape((dp_size, 2) + columns.shape[1:])
    mods = links.reorder(links.exchange_relative(columns)).astype(F32)
    mods = jnp.transpose(mods, (2, 1, 0, 3)).reshape(2, 2, 6, features)

    def own_places(latent, first):
        half = kept[latent] // 2
        mine = lax.dynamic_slice_in_dim(perms[latent], first + links.core * half, half)
        other = lax.dynamic_slice_in_dim(perms[latent], first + (1 - links.core) * half, half)
        return mine, other

    kept_places = [own_places(latent, 0) for latent in (0, 1)]
    masked_places = [own_places(latent, kept[latent]) for latent in (0, 1)]

    def weights_of(block):
        return tuple(
            stacked[block]
            for stacked in (
                qkv_weight,
                qv_bias,
                proj_weight,
                proj_bias,
                up_weight,
                up_bias,
                down_weight,
                down_bias,
            )
        )

    encoder = Block(links, weights_of(0), mods[0], (0, 1))
    decoder = Block(links, weights_of(1), mods[1], (0, 0, 1))
    enc_in = [
        rows_by(pick_matrix(kept_places[latent][0], lengths[latent]), tokens[latent])
        for latent in (0, 1)
    ]
    encoded = encoder.forward(enc_in)
    filler = mask_token.astype(F32)[None]
    dec_places = [
        kept_places[0],
        masked_places[0],
        tuple(jnp.concatenate(pair) for pair in zip(kept_places[1], masked_places[1])),
    ]
    chunk_latents = (0, 0, 1)
    table = [
        table_rows(places[0], lengths[latent], features)
        for places, latent in zip(dec_places, chunk_latents)
    ]
    half_short = kept[1] // 2
    dec_in = [
        encoded[0] + table[0],
        filler + table[1],
        jnp.concatenate([encoded[1], jnp.broadcast_to(filler, (half_short, features))]) + table[2],
    ]
    decoded = decoder.forward(dec_in)

    def placed(rows, places, length):
        pick = pick_matrix(jnp.concatenate(places), length)
        return dot(pick, jnp.concatenate(rows), ((0,), (0,)), BF16)

    swapped = []
    for rows in decoded:
        own = rows.astype(BF16)
        swapped.append((own, links.swap(own)))
    results = [
        placed(
            swapped[0] + swapped[1], dec_places[0] + dec_places[1], lengths[0]
        ),
        placed(swapped[2], dec_places[2], lengths[1]),
    ]

    d_decoded = [
        rows_by(pick_matrix(places[0], lengths[latent]), cots[latent])
        for places, latent in zip(dec_places, chunk_latents)
    ]
    d_dec_in, d_mods_dec, proj_dec, down_dec = decoder.backward(d_decoded)
    mask_sum = jnp.sum(d_dec_in[1], axis=0) + jnp.sum(d_dec_in[2][half_short:], axis=0)
    d_encoded = [d_dec_in[0], d_dec_in[2][:half_short]]
    d_enc_in, d_mods_enc, proj_enc, down_enc = encoder.backward(d_encoded)
    d_tokens = []
    for latent in (0, 1):
        own = d_enc_in[latent].astype(BF16)
        d_tokens.append(placed((own, links.swap(own)), kept_places[latent], lengths[latent]))

    grads_dec = decoder.weight_grads()
    grads_enc = encoder.weight_grads()

    own_sums = jnp.concatenate(
        [
            d_mods_enc.reshape(12, features),
            d_mods_dec.reshape(12, features),
            jnp.stack([proj_enc, proj_dec, down_enc, down_dec, mask_sum]),
        ]
    )
    own_sums = own_sums + links.swap(own_sums)
    d_mods = own_sums[:24].reshape(2, 2, dp_size, -1).astype(BF16)
    mine = links.exchange_relative(links.reorder(jnp.transpose(d_mods, (2, 1, 0, 3))))
    flat_mine = mine.reshape((-1,) + mine.shape[2:])
    grad_ada = jnp.einsum("nd,nlm->ldm", flat_acts, flat_mine, preferred_element_type=F32)
    grad_ada_bias = jnp.sum(flat_mine.astype(F32), axis=0)
    d_acts = jnp.einsum("nlm,ldm->nd", flat_mine, ada_weight, preferred_element_type=F32)
    d_act = links.sum_relative(d_acts.reshape(dp_size, 2, features))
    gate = jax.nn.sigmoid(cond)
    d_cond = (d_act * gate * (1.0 + cond * (1.0 - gate))).astype(BF16)

    small = jnp.concatenate(
        [
            own_sums[24:].reshape(-1),
            grads_enc["up_bias"],
            grads_dec["up_bias"],
            grads_enc["qv_bias"].reshape(-1),
            grads_dec["qv_bias"].reshape(-1),
        ]
    )
    small = links.sum_all(small)
    wide = up_bias.shape[1]
    local = qv_bias.shape[2]
    proj_out = small[: 2 * features].reshape(2, features)
    down_out = small[2 * features : 4 * features].reshape(2, features)
    mask_out = small[4 * features : 5 * features]
    first = 5 * features
    up_out = small[first : first + 2 * wide].reshape(2, wide)
    first += 2 * wide
    qv_out = small[first : first + 4 * local].reshape(2, 2, local)

    def both(name):
        return jnp.stack([grads_enc[name], grads_dec[name]])

    return (
        results[0][None],
        results[1][None],
        d_tokens[0][None],
        d_tokens[1][None],
        d_cond[:1],
        d_cond[1:],
        grad_ada,
        grad_ada_bias,
        both("qkv").reshape(2, -1, 3, local),
        qv_out,
        both("proj"),
        proj_out,
        both("up"),
        up_out,
        both("down"),
        down_out,
        mask_out,
    )


def solution(mesh):
    in_specs = (
        P("dp", None, None),
        P("dp", None, None),
        P("dp", None),
        P("dp", None),
        P("dp", None),
        P("dp", None),
        P(None, None, "dp"),
        P(None, "dp"),
        P(None, None, None, "tensor"),
        P(None, None, "tensor"),
        P(None, "tensor", None),
        P(),
        P(None, None, "tensor"),
        P(None, "tensor"),
        P(None, "tensor", None),
        P(),
        P(),
        P("dp", None, None),
        P("dp", None, None),
    )
    out_specs = (
        P("dp", None, None),
        P("dp", None, None),
        P("dp", None, None),
        P("dp", None, None),
        P("dp", None),
        P("dp", None),
        P(None, None, "dp"),
        P(None, "dp"),
        P(None, "dp", None, "tensor"),
        P(None, None, "tensor"),
        P(None, "tensor", "dp"),
        P(),
        P(None, "dp", "tensor"),
        P(None, "tensor"),
        P(None, "tensor", "dp"),
        P(),
        P(),
    )

    def step(*arguments):
        return on_device(mesh.shape["dp"], mesh.shape["tensor"], *arguments)

    return jax.shard_map(
        step, mesh=mesh, in_specs=in_specs, out_specs=out_specs, check_vma=False
    )
```

```python
import math

import jax
import jax.numpy as jnp
from jax import lax
from jax.experimental import pallas as pl
from jax.experimental.pallas import tpu as pltpu
from jax.sharding import PartitionSpec as P

HEAD_DIM = 72
EPSILON = 1e-06
BF16 = jnp.bfloat16
F32 = jnp.float32
MIB = 1 << 20
SCALING = HEAD_DIM**-0.5
EXPONENT = SCALING * math.log2(math.e)
GELU_A = math.sqrt(2.0 / math.pi)
GELU_B = 0.044715

SHIFT_ATTN, SCALE_ATTN, GATE_ATTN, SHIFT_MLP, SCALE_MLP, GATE_MLP = range(6)
PROJ_BIAS, DOWN_BIAS, UP_BIAS, QKV_BIAS = 0, 2, 4, 6


def nn(left, right):
    return lax.dot_general(left, right, (((1,), (0,)), ((), ())), preferred_element_type=F32)


def nt(left, right):
    return lax.dot_general(left, right, (((1,), (1,)), ((), ())), preferred_element_type=F32)


def tn(left, right):
    return lax.dot_general(left, right, (((0,), (0,)), ((), ())), preferred_element_type=F32)


def shaped(shape, dtype=BF16):
    return jax.ShapeDtypeStruct(shape, dtype)


def bytes_of(value):
    return math.prod(value.shape) * value.dtype.itemsize


def call(body, operands, outs, name, scalars=(), scratch=(), flops=0, limit=16):
    fast = pl.BlockSpec(memory_space=pltpu.VMEM)
    small = pl.BlockSpec(memory_space=pltpu.SMEM)
    moved = sum(bytes_of(value) for value in operands) + sum(bytes_of(value) for value in outs)
    return pl.pallas_call(
        body,
        in_specs=[small] * len(scalars) + [fast] * len(operands),
        out_specs=[fast] * len(outs),
        out_shape=list(outs),
        scratch_shapes=list(scratch),
        cost_estimate=pl.CostEstimate(
            flops=int(flops), transcendentals=0, bytes_accessed=int(moved)
        ),
        compiler_params=pltpu.CompilerParams(vmem_limit_bytes=limit * MIB),
        name=name,
    )(
        *scalars,
        *[pltpu.with_memory_space_constraint(value, pltpu.VMEM) for value in operands],
    )


def normed_of(values):
    center = values - jnp.mean(values, axis=-1, keepdims=True)
    spread = jnp.mean(center * center, axis=-1, keepdims=True)
    scale = lax.rsqrt(spread + EPSILON)
    return center * scale, scale


def modulate(values, mods_ref, at, scale_part, shift_part):
    block, latent = at
    scale = mods_ref[block, latent, scale_part : scale_part + 1, :]
    shift = mods_ref[block, latent, shift_part : shift_part + 1, :]
    return (normed_of(values)[0] * (1.0 + scale) + shift).astype(BF16)


def ln_open(stream, mods, at):
    rows, features = stream.shape

    def body(x_ref, mods_ref, out_ref):
        out_ref[...] = modulate(x_ref[...], mods_ref, at, SCALE_ATTN, SHIFT_ATTN)

    return call(body, [stream, mods], [shaped((rows, features))], "ln_open", flops=20 * rows * features)[0]


def merge_attn(stream, near, far, small, mods, at):
    rows, features = stream.shape
    block, latent = at

    def body(x_ref, near_ref, far_ref, small_ref, mods_ref, mid_ref, out_ref):
        bias = small_ref[PROJ_BIAS + block : PROJ_BIAS + block + 1, :features]
        branch = near_ref[...].astype(F32) + far_ref[...].astype(F32) + bias
        middle = x_ref[...] + mods_ref[block, latent, GATE_ATTN : GATE_ATTN + 1, :] * branch
        mid_ref[...] = middle
        out_ref[...] = modulate(middle, mods_ref, at, SCALE_MLP, SHIFT_MLP)

    return call(
        body,
        [stream, near, far, small, mods],
        [shaped((rows, features), F32), shaped((rows, features))],
        "merge_attn",
        flops=25 * rows * features,
    )


def merge_mlp(middle, near, far, small, mods, at, table, tail):
    rows, features = middle.shape
    block, latent = at
    total = rows + (0 if tail is None else tail.shape[0])
    following = (block + 1, latent)

    def body(mid_ref, near_ref, far_ref, table_ref, small_ref, mods_ref, *rest):
        x_ref, out_ref = rest[-2:]
        bias = small_ref[DOWN_BIAS + block : DOWN_BIAS + block + 1, :features]
        branch = near_ref[...].astype(F32) + far_ref[...].astype(F32) + bias
        gate = mods_ref[block, latent, GATE_MLP : GATE_MLP + 1, :]
        stream = mid_ref[...] + gate * branch + table_ref[...]
        x_ref[:rows, :] = stream
        out_ref[:rows, :] = modulate(stream, mods_ref, following, SCALE_ATTN, SHIFT_ATTN)
        if tail is not None:
            stream = rest[0][...]
            x_ref[rows:, :] = stream
            out_ref[rows:, :] = modulate(stream, mods_ref, following, SCALE_ATTN, SHIFT_ATTN)

    return call(
        body,
        [middle, near, far, table, small, mods] + ([] if tail is None else [tail]),
        [shaped((total, features), F32), shaped((total, features))],
        "merge_mlp",
        flops=25 * total * features,
    )


def qkv_forward(own, other, weight, small, block):
    rows, features = own.shape
    width = weight.shape[1]

    def body(own_ref, other_ref, w_ref, small_ref, out_ref):
        bias = small_ref[QKV_BIAS + block : QKV_BIAS + block + 1, :width]
        both = jnp.concatenate([own_ref[...], other_ref[...]], axis=0)
        out = (nt(both, w_ref[block]) + bias).astype(BF16)
        out_ref[0] = out[:rows]
        out_ref[1] = out[rows:]

    return call(
        body,
        [own, other, weight, small],
        [shaped((2, rows, width))],
        "qkv_forward",
        flops=4 * rows * features * width,
    )[0]


def qkv_backward(grads, weight, block):
    _, rows, width = grads.shape
    features = weight.shape[2]

    def body(g_ref, w_ref, own_ref, other_ref):
        both = jnp.concatenate([g_ref[0], g_ref[1]], axis=0)
        out = nn(both, w_ref[block]).astype(BF16)
        own_ref[...] = out[:rows]
        other_ref[...] = out[rows:]

    return call(
        body,
        [grads, weight],
        [shaped((rows, features)), shaped((rows, features))],
        "qkv_backward",
        flops=4 * rows * features * width,
    )


def mlp_forward(own, other, up_weight, down_weight, small, block):
    rows, features = own.shape
    wide = up_weight.shape[2]

    def body(own_ref, other_ref, up_ref, down_ref, small_ref, own_out, other_out, act_ref, slope_ref):
        bias = small_ref[UP_BIAS + block : UP_BIAS + block + 1, :wide]
        both = jnp.concatenate([own_ref[...], other_ref[...]], axis=0)
        hidden = nn(both, up_ref[block]) + bias
        squared = hidden * hidden
        bent = jnp.tanh(GELU_A * hidden * (1.0 + GELU_B * squared))
        half = 0.5 + 0.5 * bent
        active = (hidden * half).astype(BF16)
        slope = half + 0.5 * hidden * (1.0 - bent * bent) * (
            GELU_A + 3.0 * GELU_A * GELU_B * squared
        )
        act_ref[...] = active
        slope_ref[...] = slope.astype(BF16)
        out = nn(active, down_ref[block]).astype(BF16)
        own_out[...] = out[:rows]
        other_out[...] = out[rows:]

    return call(
        body,
        [own, other, up_weight, down_weight, small],
        [
            shaped((rows, features)),
            shaped((rows, features)),
            shaped((2 * rows, wide)),
            shaped((2 * rows, wide)),
        ],
        "mlp_forward",
        flops=8 * rows * features * wide,
    )


def mlp_backward(own, other, slope, up_weight, down_weight, block):
    rows, features = own.shape
    wide = up_weight.shape[2]

    def body(own_ref, other_ref, slope_ref, up_ref, down_ref, own_out, other_out, hid_ref):
        both = jnp.concatenate([own_ref[...], other_ref[...]], axis=0)
        d_active = nt(both, down_ref[block])
        d_hidden = (d_active * slope_ref[...].astype(F32)).astype(BF16)
        hid_ref[...] = d_hidden
        out = nt(d_hidden, up_ref[block]).astype(BF16)
        own_out[...] = out[:rows]
        other_out[...] = out[rows:]

    return call(
        body,
        [own, other, slope, up_weight, down_weight],
        [shaped((rows, features)), shaped((rows, features)), shaped((2 * rows, wide))],
        "mlp_backward",
        flops=8 * rows * features * wide,
    )


def ln_back(near, far, stream, d_out, mods, at, scale_part, branch=None, cut=None, narrow=False):
    rows, features = stream.shape
    cut = rows if cut is None else cut
    operands = [near, far, stream, d_out, mods]
    outs = [shaped((rows, features), BF16 if narrow else F32), shaped((8, features), F32)]
    if branch is not None:
        branch_near, branch_far, small, bias_row, gate_at, gate_part = branch
        operands += [branch_near, branch_far, small]
        outs.append(shaped((cut, features)))

    def body(near_ref, far_ref, x_ref, d_ref, mods_ref, *rest):
        scale = mods_ref[at[0], at[1], scale_part : scale_part + 1, :]
        d_normed = near_ref[...].astype(F32) + far_ref[...].astype(F32)
        normed, spread = normed_of(x_ref[...])
        product = d_normed * normed
        grad = d_normed * (1.0 + scale)
        d_x = d_ref[...] + spread * (
            grad
            - jnp.mean(grad, axis=-1, keepdims=True)
            - normed * jnp.mean(grad * normed, axis=-1, keepdims=True)
        )
        sums = [jnp.sum(product, axis=0, keepdims=True), jnp.sum(d_normed, axis=0, keepdims=True)]
        if branch is None:
            d_ref_out, sums_ref = rest
            sums += [jnp.zeros_like(sums[0])] * 2
        else:
            b_near, b_far, small_ref, d_ref_out, sums_ref, grad_ref = rest
            value = b_near[...].astype(F32) + b_far[...].astype(F32)
            value = value + small_ref[bias_row : bias_row + 1, :features]
            kept = d_x[:cut]
            gate = mods_ref[gate_at[0], gate_at[1], gate_part : gate_part + 1, :]
            d_branch = (gate * kept).astype(BF16)
            grad_ref[...] = d_branch
            sums += [
                jnp.sum(kept * value, axis=0, keepdims=True),
                jnp.sum(d_branch.astype(F32), axis=0, keepdims=True),
            ]
        if cut < rows:
            sums.append(jnp.sum(d_x[cut:], axis=0, keepdims=True))
        else:
            sums.append(jnp.zeros_like(sums[0]))
        sums.append(jnp.zeros((3, features), F32))
        sums_ref[...] = jnp.concatenate(sums, axis=0)
        d_ref_out[...] = d_x.astype(d_ref_out.dtype)

    return call(body, operands, outs, "ln_back", flops=60 * rows * features)


def attn_forward(query, merged, proj_weight, block):
    _, rows, width = query.shape
    local = width // 3
    heads = local // HEAD_DIM
    counts = [part.shape[1] for part in merged]
    total = 2 * sum(counts)
    features = proj_weight.shape[2]
    by_keys = rows <= 128

    def body(*refs):
        q_ref, refs = refs[0], refs[1:]
        kv_refs, refs = refs[: len(merged)], refs[len(merged) :]
        proj_ref, att_ref, lse_ref, own_out, other_out, q_s, k_s, v_s, o_s, l_s = refs
        for head in range(heads):
            low = head * HEAD_DIM
            first = 0
            for part, count in zip(kv_refs, counts):
                for side in range(2):
                    at = pl.ds(first, count)
                    k_s[head, at, :] = part[side, :, local + low : local + low + HEAD_DIM]
                    v_s[head, at, :] = part[side, :, 2 * local + low : 2 * local + low + HEAD_DIM]
                    first += count
            for side in range(2):
                q_s[head, side] = q_ref[side, :, low : low + HEAD_DIM]
        for head in range(heads):
            for side in range(2):
                if by_keys:
                    scores = nt(k_s[head], q_s[head, side])
                    highest = jnp.max(scores, axis=0, keepdims=True)
                    raised = jnp.exp2((scores - highest) * EXPONENT)
                    total_row = jnp.sum(raised, axis=0, keepdims=True)
                    out = tn(v_s[head], raised.astype(BF16))
                    o_s[head, side] = (out / total_row).T.astype(BF16)
                    lse_ref[head, side] = highest * EXPONENT + jnp.log2(total_row)
                else:
                    scores = nt(q_s[head, side], k_s[head])
                    highest = jnp.max(scores, axis=1, keepdims=True)
                    raised = jnp.exp2((scores - highest) * EXPONENT)
                    total_row = jnp.sum(raised, axis=1, keepdims=True)
                    out = nn(raised.astype(BF16), v_s[head])
                    o_s[head, side] = (out / total_row).astype(BF16)
                    l_s[head, side] = jnp.broadcast_to(
                        highest * EXPONENT + jnp.log2(total_row), (rows, 128)
                    )
        if not by_keys:
            for head in range(heads):
                for side in range(2):
                    lse_ref[head, side] = l_s[head, side].T[:1]
        for side, out_ref in ((1, other_out), (0, own_out)):
            for head in range(heads):
                low = head * HEAD_DIM
                att_ref[side * rows : (side + 1) * rows, low : low + HEAD_DIM] = o_s[head, side]
            out_ref[...] = nn(
                att_ref[side * rows : (side + 1) * rows, :], proj_ref[block]
            ).astype(BF16)

    return call(
        body,
        [query, *merged, proj_weight],
        [
            shaped((2 * rows, local)),
            shaped((heads, 2, 1, rows), F32),
            shaped((rows, features)),
            shaped((rows, features)),
        ],
        "attn_forward",
        scratch=[
            pltpu.VMEM((heads, 2, rows, HEAD_DIM), BF16),
            pltpu.VMEM((heads, total, HEAD_DIM), BF16),
            pltpu.VMEM((heads, total, HEAD_DIM), BF16),
            pltpu.VMEM((heads, 2, rows, HEAD_DIM), BF16),
            pltpu.VMEM((heads, 2, 8 if by_keys else rows, 128), F32),
        ],
        flops=16 * heads * rows * total * HEAD_DIM + 4 * rows * local * features,
        limit=24,
    )


def attn_backward(merged, normers, grads, proj_weight, block):
    count = len(merged)
    width = merged[0].shape[2]
    local = width // 3
    heads = local // HEAD_DIM
    halves = [part.shape[1] for part in merged]
    total = 2 * sum(halves)
    features = proj_weight.shape[2]
    step = min(halves)
    steps = total // step
    unroll = 4 if step >= 256 else steps * heads

    def body(*refs):
        m_refs, refs = refs[:count], refs[count:]
        l_refs, refs = refs[:count], refs[count:]
        g_refs, refs = refs[: 2 * count], refs[2 * count :]
        proj_ref, refs = refs[0], refs[1:]
        out_refs, refs = refs[:count], refs[count:]
        q_s, k_s, kt_s, v_s, g_s, dq_s, dk_s, dv_s, l_s = refs
        first = 0
        for index in range(count):
            rows = halves[index]
            for side in range(2):
                at = pl.ds(first, rows)
                grad = nt(g_refs[2 * index + side][...], proj_ref[block]).astype(BF16)
                for head in range(heads):
                    low = head * HEAD_DIM
                    part = m_refs[index]
                    q_s[head, at, :] = part[side, :, low : low + HEAD_DIM]
                    keys = part[side, :, local + low : local + low + HEAD_DIM]
                    k_s[head, at, :] = keys
                    kt_s[head, :, at] = keys.T
                    v_s[head, at, :] = part[side, :, 2 * local + low : 2 * local + low + HEAD_DIM]
                    g_s[head, at, :] = grad[:, low : low + HEAD_DIM]
                    for piece in range(rows // step):
                        l_s[head, first // step + piece] = l_refs[index][
                            head, side, :, piece * step : (piece + 1) * step
                        ]
                first += rows
        dk_s[...] = jnp.zeros_like(dk_s)
        dv_s[...] = jnp.zeros_like(dv_s)

        def one(index, carry):
            head, piece = index // steps, lax.rem(index, steps)
            at = pl.ds(pl.multiple_of(piece * step, step), step)
            queries, grad = q_s[head, at, :], g_s[head, at, :]
            probs = jnp.exp2(nt(k_s[head], queries) * EXPONENT - l_s[head, piece])
            product = probs * nt(v_s[head], grad)
            delta = jnp.sum(product, axis=0, keepdims=True)
            d_scores = (product - probs * delta).astype(BF16)
            dv_s[head] += nn(probs.astype(BF16), grad)
            dk_s[head] += nn(d_scores, queries)
            dq_s[head, at, :] = (nn(kt_s[head], d_scores) * SCALING).T.astype(BF16)
            return carry

        lax.fori_loop(0, steps * heads, one, 0, unroll=unroll)
        first = 0
        for index in range(count):
            rows = halves[index]
            for side in range(2):
                at = pl.ds(first, rows)
                out = out_refs[index]
                for head in range(heads):
                    low = head * HEAD_DIM
                    out[side, :, low : low + HEAD_DIM] = dq_s[head, at, :]
                    out[side, :, local + low : local + low + HEAD_DIM] = (
                        dk_s[head, at, :] * SCALING
                    ).astype(BF16)
                    out[side, :, 2 * local + low : 2 * local + low + HEAD_DIM] = dv_s[
                        head, at, :
                    ].astype(BF16)
                first += rows

    def lanes(dtype=BF16):
        return pltpu.VMEM((heads, total, HEAD_DIM), dtype)

    return call(
        body,
        [*merged, *normers, *[half for pair in grads for half in pair], proj_weight],
        [shaped(part.shape) for part in merged],
        "attn_backward",
        scratch=[
            lanes(),
            lanes(),
            pltpu.VMEM((heads, HEAD_DIM, total), BF16),
            lanes(),
            lanes(),
            lanes(),
            lanes(F32),
            lanes(F32),
            pltpu.VMEM((heads, steps, 1, step), F32),
        ],
        flops=20 * heads * total * total * HEAD_DIM + 2 * total * local * features,
        limit=28,
    )


def weight_grads(pairs, bit, blocks):
    features = pairs[0][0][0].shape[1]
    widths = [rights[0].shape[1] for _, rights in pairs]
    each = features // blocks
    operands, spans = [], []
    for lefts, rights in pairs:
        spans.append((len(operands), len(lefts)))
        operands += list(lefts) + list(rights)
    rows = sum(part.shape[0] for part in pairs[0][0])
    out = shaped((blocks // 2, each, sum(widths)))

    def body(bit_ref, *refs):
        kept_ref, away_ref = refs[-2:]
        mine = bit_ref[0]
        low = 0
        for (first, number), width in zip(spans, widths):
            total = None
            for index in range(number):
                term = tn(refs[first + index][...], refs[first + number + index][...])
                total = term if total is None else total + term
            total = total.astype(BF16)
            columns = slice(low, low + width)
            for block in range(blocks):
                piece = total[block * each : (block + 1) * each]

                @pl.when(mine == block % 2)
                def _():
                    kept_ref[block // 2, :, columns] = piece

                @pl.when(mine != block % 2)
                def _():
                    away_ref[block // 2, :, columns] = piece

            low += width

    return call(
        body,
        operands,
        [out, out],
        "weight_grads",
        scalars=[bit],
        flops=2 * rows * features * sum(widths),
        limit=28,
    )


def halve(kept, moved, bit):
    blocks, each, width = kept.shape
    out = shaped((blocks // 2, each, width))

    def body(bit_ref, kept_ref, moved_ref, next_ref, away_ref):
        mine = bit_ref[0]
        for index in range(blocks // 2):
            for place, out_ref in ((1 - mine, away_ref), (mine, next_ref)):
                at = 2 * index + place
                out_ref[index] = (kept_ref[at].astype(F32) + moved_ref[at].astype(F32)).astype(BF16)

    return call(
        body, [kept, moved], [out, out], "halve", scalars=[bit], flops=blocks * each * width
    )


def partners(size, bit):
    return [(index, index ^ bit) for index in range(size)]


def bits_of(size):
    bits = []
    while (1 << len(bits)) < size:
        bits.append(1 << len(bits))
    assert (1 << len(bits)) == size
    return bits


class Links:
    def __init__(self, dp_size, tensor_size):
        self.dp_size = dp_size
        self.tensor_size = tensor_size
        self.dp_bits = bits_of(dp_size)
        self.me = lax.axis_index("dp")
        self.core = lax.rem(lax.axis_index("tensor"), 2)

    def swap(self, value):
        return lax.ppermute(value, "tensor", partners(self.tensor_size, 1))

    def cross(self, value):
        return lax.ppermute(value, "tensor", partners(self.tensor_size, 2))

    def dp_move(self, value, bit):
        return lax.ppermute(value, "dp", partners(self.dp_size, bit))

    def my_bit(self, bit):
        return lax.rem(self.me // bit, 2)

    def joined(self, own, other):
        moved = self.swap(other)
        near = (own.astype(F32) + moved.astype(F32)).astype(BF16)
        return near, self.cross(near)

    def gather_relative(self, value):
        held = value[None]
        for bit in self.dp_bits:
            held = jnp.concatenate([held, self.dp_move(held, bit)], axis=0)
        return held

    def exchange_relative(self, value):
        held = value
        for bit in self.dp_bits:
            split = held.reshape((self.dp_size // (2 * bit), 2, bit) + held.shape[1:])
            moved = self.dp_move(split[:, 1], bit)
            held = jnp.stack([split[:, 0], moved], axis=1).reshape(held.shape)
        return held

    def sum_relative(self, value):
        held = value
        for bit in reversed(self.dp_bits):
            moved = self.dp_move(held[bit:].astype(BF16), bit)
            held = held[:bit].astype(F32) + moved.astype(F32)
        return held[0]

    def reorder(self, value):
        held = value
        for bit in self.dp_bits:
            split = held.reshape((self.dp_size // (2 * bit), 2, bit) + held.shape[1:])
            flipped = jnp.where(self.my_bit(bit) == 1, split[:, ::-1], split)
            held = flipped.reshape(held.shape)
        return held

    def scatter_sum(self, pairs):
        bits = [self.my_bit(bit).reshape(1) for bit in self.dp_bits]
        kept, away = weight_grads(pairs, bits[0], self.dp_size)
        for bit, mine in zip(self.dp_bits[:-1], bits[1:]):
            kept, away = halve(kept, self.dp_move(away, bit), mine)
        moved = self.dp_move(away, self.dp_bits[-1])
        return kept[0].astype(F32) + moved[0].astype(F32)

    def sum_all(self, value):
        held = value
        for bit in self.dp_bits:
            held = held + self.dp_move(held, bit)
        return held


class Weights:
    def __init__(self, qkv, proj, up, down, small, mods):
        self.qkv, self.proj, self.up, self.down = qkv, proj, up, down
        self.small, self.mods = small, mods


class Block:
    def __init__(self, links, weights, index, owners):
        self.links, self.weights, self.index, self.owners = links, weights, index, owners
        self.saved = [dict() for _ in owners]

    def at(self, chunk):
        return (self.index, self.owners[chunk])

    def members(self, latent):
        return [chunk for chunk, owner in enumerate(self.owners) if owner == latent]

    def latents(self):
        return sorted(set(self.owners))

    def enter(self, chunk, stream, normed):
        keep, w = self.saved[chunk], self.weights
        keep["x"] = stream
        keep["normed_attn"] = (normed, self.links.swap(normed))
        keep["qkv"] = qkv_forward(*keep["normed_attn"], w.qkv, w.small, self.index)

    def attention(self, chunk):
        keep, w = self.saved[chunk], self.weights
        merged = [self.saved[c]["qkv"] for c in self.members(self.owners[chunk])]
        keep["attended"], keep["normer"], own, other = attn_forward(
            keep["qkv"], merged, w.proj, self.index
        )
        keep["branch_attn"] = self.links.joined(own, other)

    def mlp(self, chunk):
        keep, w = self.saved[chunk], self.weights
        keep["middle"], normed = merge_attn(
            keep["x"], *keep["branch_attn"], w.small, w.mods, self.at(chunk)
        )
        keep["normed_mlp"] = (normed, self.links.swap(normed))
        own, other, keep["active"], keep["slope"] = mlp_forward(
            *keep["normed_mlp"], w.up, w.down, w.small, self.index
        )
        keep["branch_mlp"] = self.links.joined(own, other)

    def mlp_back(self, chunk, d_out, d_branch):
        keep, w = self.saved[chunk], self.weights
        keep["d_branch_mlp"] = (d_branch, self.links.swap(d_branch))
        own, other, keep["d_hidden"] = mlp_backward(
            *keep["d_branch_mlp"], keep["slope"], w.up, w.down, self.index
        )
        near, far = self.links.joined(own, other)
        branch = (*keep["branch_attn"], w.small, PROJ_BIAS + self.index, self.at(chunk), GATE_ATTN)
        keep["d_middle"], keep["mlp_sums"], grad = ln_back(
            near, far, keep["middle"], d_out, w.mods, self.at(chunk), SCALE_MLP, branch
        )
        keep["d_branch_attn"] = (grad, self.links.swap(grad))

    def attention_back(self, latent):
        w = self.weights
        chunks = [self.saved[c] for c in self.members(latent)]
        grads = attn_backward(
            [keep["qkv"] for keep in chunks],
            [keep["normer"] for keep in chunks],
            [keep["d_branch_attn"] for keep in chunks],
            w.proj,
            self.index,
        )
        for keep, grad in zip(chunks, grads):
            keep["d_qkv"] = grad

    def leave_back(self, chunk, branch=None, cut=None, narrow=False):
        keep, w = self.saved[chunk], self.weights
        near, far = self.links.joined(*qkv_backward(keep["d_qkv"], w.qkv, self.index))
        d_x, keep["attn_sums"], *grad = ln_back(
            near,
            far,
            keep["x"],
            keep["d_middle"],
            w.mods,
            self.at(chunk),
            SCALE_ATTN,
            branch,
            cut,
            narrow,
        )
        return d_x, (grad[0] if grad else None)

    def rows(self, name):
        found = []
        for keep in self.saved:
            value = keep[name]
            if isinstance(value, tuple):
                found += list(value)
            else:
                found.append(value.reshape(-1, value.shape[-1]))
        return found

    def halves(self, name):
        found = []
        for keep in self.saved:
            value = keep[name]
            value = value.reshape(-1, value.shape[-1])
            middle = value.shape[0] // 2
            found += [value[:middle], value[middle:]]
        return found


def pick_matrix(places, length):
    return (places[:, None] == jnp.arange(length, dtype=jnp.int32)[None, :]).astype(BF16)


def table_rows(places, length, features):
    side = math.isqrt(length)
    quarter = features // 4
    frequency = 1.0 / 10000.0 ** (jnp.arange(quarter, dtype=F32) / quarter)
    angle = jnp.arange(side, dtype=jnp.int32).astype(F32)[:, None] * frequency[None, :]
    near = jnp.concatenate([jnp.sin(angle), jnp.cos(angle)], axis=1)
    steps = jnp.arange(side, dtype=jnp.int32)[None, :]
    row_pick = (places[:, None] // side == steps).astype(F32)
    col_pick = (places[:, None] % side == steps).astype(F32)
    return jnp.concatenate(
        [
            jnp.dot(row_pick, near, precision=lax.Precision.HIGHEST),
            jnp.dot(col_pick, near, precision=lax.Precision.HIGHEST),
        ],
        axis=1,
    )


def on_device(dp_size, tensor_size, *arguments):
    (
        tokens_long,
        tokens_short,
        cond_long,
        cond_short,
        perm_long,
        perm_short,
        ada_weight,
        ada_bias,
        qkv_weight,
        qv_bias,
        proj_weight,
        proj_bias,
        up_weight,
        up_bias,
        down_weight,
        down_bias,
        mask_token,
        cot_long,
        cot_short,
    ) = arguments
    assert tokens_long.shape[0] == 1 and tokens_short.shape[0] == 1
    links = Links(dp_size, tensor_size)
    features = tokens_long.shape[2]
    wide = up_weight.shape[2]
    local = qv_bias.shape[2]
    tokens = (tokens_long[0], tokens_short[0])
    cots = (cot_long[0], cot_short[0])
    perms = (perm_long[0], perm_short[0])
    lengths = tuple(rows.shape[0] for rows in tokens)
    kept = tuple(length // 2 for length in lengths)

    cond = jnp.concatenate([cond_long, cond_short]).astype(F32)
    acts = links.gather_relative(jax.nn.silu(cond).astype(BF16))
    flat_acts = acts.reshape(-1, features)
    columns = jnp.einsum("nd,ldm->nlm", flat_acts, ada_weight, preferred_element_type=F32)
    columns = (columns + ada_bias.astype(F32)[None]).astype(BF16)
    columns = columns.reshape((dp_size, 2) + columns.shape[1:])
    mods = links.reorder(links.exchange_relative(columns)).astype(F32)
    mods = jnp.transpose(mods, (2, 1, 0, 3)).reshape(2, 2, 6, features)

    table_width = max(features, wide, 3 * local)

    def padded(rows):
        return jnp.pad(rows.astype(F32), ((0, 0), (0, table_width - rows.shape[1])))

    qkv_bias = jnp.concatenate(
        [qv_bias[:, 0], jnp.zeros_like(qv_bias[:, 0]), qv_bias[:, 1]], axis=1
    )
    small = jnp.concatenate([padded(proj_bias), padded(down_bias), padded(up_bias), padded(qkv_bias)])
    weights = Weights(
        jnp.transpose(qkv_weight, (0, 2, 3, 1)).reshape(2, 3 * local, features),
        proj_weight,
        up_weight,
        down_weight,
        small,
        mods,
    )

    def places_of(latent, first):
        half = kept[latent] // 2
        mine = lax.dynamic_slice_in_dim(perms[latent], first + links.core * half, half)
        other = lax.dynamic_slice_in_dim(perms[latent], first + (1 - links.core) * half, half)
        return mine, other

    kept_places = [places_of(latent, 0) for latent in (0, 1)]
    masked_places = [places_of(latent, kept[latent]) for latent in (0, 1)]
    half_short = kept[1] // 2
    encoder = Block(links, weights, 0, (0, 1))
    decoder = Block(links, weights, 1, (0, 0, 1))
    dec_places = [
        kept_places[0],
        masked_places[0],
        tuple(jnp.concatenate(pair) for pair in zip(kept_places[1], masked_places[1])),
    ]
    dec_lengths = (lengths[0], lengths[0], lengths[1])

    filler = mask_token.astype(F32)[None]
    kept_tables = [
        table_rows(kept_places[latent][0], lengths[latent], features) for latent in (0, 1)
    ]
    masked_rows = [
        filler + table_rows(masked_places[latent][0], lengths[latent], features)
        for latent in (0, 1)
    ]
    for latent in (0, 1):
        stream = nn(pick_matrix(kept_places[latent][0], lengths[latent]), tokens[latent])
        encoder.enter(latent, stream, ln_open(stream, mods, (0, latent)))
    for chunk in (0, 1):
        encoder.attention(chunk)
    decoder.enter(1, masked_rows[0], ln_open(masked_rows[0], mods, (1, 0)))
    for chunk in (0, 1):
        encoder.mlp(chunk)
    for latent, chunk, tail in ((0, 0, None), (1, 2, masked_rows[1])):
        keep = encoder.saved[latent]
        stream, normed = merge_mlp(
            keep["middle"],
            *keep["branch_mlp"],
            small,
            mods,
            (0, latent),
            kept_tables[latent],
            tail,
        )
        decoder.enter(chunk, stream, normed)
    for chunk in (0, 1, 2):
        decoder.attention(chunk)
    for chunk in (0, 1, 2):
        decoder.mlp(chunk)

    decoded, d_decoded, gate_sums, bias_sums, grads_in = [], [], [], [], []
    for chunk in (0, 1, 2):
        keep = decoder.saved[chunk]
        latent = decoder.owners[chunk]
        gate = mods[1, latent, GATE_MLP][None]
        near, far = keep["branch_mlp"]
        branch = near.astype(F32) + far.astype(F32) + down_bias[1].astype(F32)[None]
        own = (keep["middle"] + gate * branch).astype(BF16)
        decoded.append((own, links.swap(own)))
        pick = pick_matrix(dec_places[chunk][0], dec_lengths[chunk])
        d_out = nn(pick, cots[latent])
        grad = (gate * d_out).astype(BF16)
        d_decoded.append(d_out)
        grads_in.append(grad)
        gate_sums.append(jnp.sum(d_out * branch, axis=0))
        bias_sums.append(jnp.sum(grad.astype(F32), axis=0))

    def placed(pairs, places, length):
        pick = pick_matrix(jnp.concatenate([part for pair in places for part in pair]), length)
        return tn(pick, jnp.concatenate([part for pair in pairs for part in pair])).astype(BF16)

    results = (
        placed(decoded[:2], dec_places[:2], lengths[0]),
        placed(decoded[2:], dec_places[2:], lengths[1]),
    )

    for chunk in (0, 1, 2):
        decoder.mlp_back(chunk, d_decoded[chunk], grads_in[chunk])
    dec_wide = links.scatter_sum(
        [
            (decoder.rows("normed_mlp"), decoder.halves("d_hidden")),
            (decoder.rows("d_branch_mlp"), decoder.halves("active")),
            (decoder.rows("d_branch_attn"), decoder.halves("attended")),
        ]
    )
    for latent in (0, 1):
        decoder.attention_back(latent)
    enc_branch = [
        (*encoder.saved[latent]["branch_mlp"], small, DOWN_BIAS, (0, latent), GATE_MLP)
        for latent in (0, 1)
    ]
    d_long, grad_long = decoder.leave_back(0, enc_branch[0])
    d_masked, _ = decoder.leave_back(1, None, 0)
    d_short, grad_short = decoder.leave_back(2, enc_branch[1], half_short)
    dec_qkv = links.scatter_sum([(decoder.rows("normed_attn"), decoder.halves("d_qkv"))])
    encoder.mlp_back(0, d_long, grad_long)
    encoder.mlp_back(1, d_short[:half_short], grad_short)
    enc_wide = links.scatter_sum(
        [
            (encoder.rows("normed_mlp"), encoder.halves("d_hidden")),
            (encoder.rows("d_branch_mlp"), encoder.halves("active")),
            (encoder.rows("d_branch_attn"), encoder.halves("attended")),
        ]
    )
    d_tokens = []
    for latent in (0, 1):
        encoder.attention_back(latent)
    for latent in (0, 1):
        own, _ = encoder.leave_back(latent, narrow=True)
        d_tokens.append(
            placed([(own, links.swap(own))], [kept_places[latent]], lengths[latent])
        )
    enc_qkv = links.scatter_sum([(encoder.rows("normed_attn"), encoder.halves("d_qkv"))])

    def gathered(block, gates):
        sums = []
        for latent in block.latents():
            chunks = block.members(latent)
            attn = sum(block.saved[c]["attn_sums"] for c in chunks)
            mlp = sum(block.saved[c]["mlp_sums"] for c in chunks)
            sums.append(jnp.stack([attn[1], attn[0], mlp[2], mlp[1], mlp[0], gates[latent]]))
        return jnp.stack(sums)

    dec_attn = [keep["attn_sums"] for keep in decoder.saved]
    d_mods = jnp.stack(
        [
            gathered(encoder, [dec_attn[0][2], dec_attn[2][2]]),
            gathered(decoder, [gate_sums[0] + gate_sums[1], gate_sums[2]]),
        ]
    )
    own_sums = jnp.concatenate(
        [
            d_mods.reshape(24, features),
            jnp.stack(
                [
                    sum(keep["mlp_sums"][3] for keep in encoder.saved),
                    sum(keep["mlp_sums"][3] for keep in decoder.saved),
                    dec_attn[0][3] + dec_attn[2][3],
                    sum(bias_sums),
                    dec_attn[1][4] + dec_attn[2][4],
                ]
            ),
        ]
    )
    own_sums = own_sums + links.swap(own_sums)
    d_mods = own_sums[:24].reshape(2, 2, dp_size, -1).astype(BF16)
    mine = links.exchange_relative(links.reorder(jnp.transpose(d_mods, (2, 1, 0, 3))))
    flat_mine = mine.reshape((-1,) + mine.shape[2:])
    grad_ada = jnp.einsum("nd,nlm->ldm", flat_acts, flat_mine, preferred_element_type=F32)
    grad_ada_bias = jnp.sum(flat_mine.astype(F32), axis=0)
    d_acts = jnp.einsum("nlm,ldm->nd", flat_mine, ada_weight, preferred_element_type=F32)
    d_act = links.sum_relative(d_acts.reshape(dp_size, 2, features))
    gate = jax.nn.sigmoid(cond)
    d_cond = (d_act * gate * (1.0 + cond * (1.0 - gate))).astype(BF16)

    def column_sums(block, name):
        return sum(jnp.sum(part.astype(F32), axis=0) for part in block.rows(name))

    qkv_sums = [column_sums(block, "d_qkv") for block in (encoder, decoder)]
    totals = jnp.concatenate(
        [own_sums[24:].reshape(-1)]
        + [column_sums(block, "d_hidden") for block in (encoder, decoder)]
        + [part for sums in qkv_sums for part in (sums[:local], sums[2 * local :])]
    )
    totals = links.sum_all(totals)
    proj_out = totals[: 2 * features].reshape(2, features)
    down_out = totals[2 * features : 4 * features].reshape(2, features)
    mask_out = totals[4 * features : 5 * features]
    first = 5 * features
    up_out = totals[first : first + 2 * wide].reshape(2, wide)
    first += 2 * wide
    qv_out = totals[first : first + 4 * local].reshape(2, 2, local)

    up_grad = jnp.stack([enc_wide[:, :wide], dec_wide[:, :wide]])
    down_grad = jnp.stack([enc_wide[:, wide : 2 * wide], dec_wide[:, wide : 2 * wide]])
    proj_grad = jnp.stack([enc_wide[:, 2 * wide :], dec_wide[:, 2 * wide :]])
    qkv_grad = jnp.stack([enc_qkv, dec_qkv]).reshape(2, -1, 3, local)

    return (
        results[0][None],
        results[1][None],
        d_tokens[0][None],
        d_tokens[1][None],
        d_cond[:1],
        d_cond[1:],
        grad_ada,
        grad_ada_bias,
        qkv_grad,
        qv_out,
        jnp.transpose(proj_grad, (0, 2, 1)),
        proj_out,
        up_grad,
        up_out,
        jnp.transpose(down_grad, (0, 2, 1)),
        down_out,
        mask_out,
    )


def solution(mesh):
    in_specs = (
        P("dp", None, None),
        P("dp", None, None),
        P("dp", None),
        P("dp", None),
        P("dp", None),
        P("dp", None),
        P(None, None, "dp"),
        P(None, "dp"),
        P(None, None, None, "tensor"),
        P(None, None, "tensor"),
        P(None, "tensor", None),
        P(),
        P(None, None, "tensor"),
        P(None, "tensor"),
        P(None, "tensor", None),
        P(),
        P(),
        P("dp", None, None),
        P("dp", None, None),
    )
    out_specs = (
        P("dp", None, None),
        P("dp", None, None),
        P("dp", None, None),
        P("dp", None, None),
        P("dp", None),
        P("dp", None),
        P(None, None, "dp"),
        P(None, "dp"),
        P(None, "dp", None, "tensor"),
        P(None, None, "tensor"),
        P(None, "tensor", "dp"),
        P(),
        P(None, "dp", "tensor"),
        P(None, "tensor"),
        P(None, "tensor", "dp"),
        P(),
        P(),
    )

    def step(*arguments):
        return on_device(mesh.shape["dp"], mesh.shape["tensor"], *arguments)

    return jax.shard_map(
        step, mesh=mesh, in_specs=in_specs, out_specs=out_specs, check_vma=False
    )
```

```python
import math

import jax
import jax.numpy as jnp
from jax import lax
from jax.experimental import pallas as pl
from jax.experimental.pallas import tpu as pltpu
from jax.sharding import PartitionSpec as P

HEAD_DIM = 72
EPSILON = 1e-06
BF16 = jnp.bfloat16
F32 = jnp.float32
MIB = 1 << 20
SCALING = HEAD_DIM**-0.5
EXPONENT = SCALING * math.log2(math.e)
GELU_A = math.sqrt(2.0 / math.pi)
GELU_B = 0.044715

SHIFT_ATTN, SCALE_ATTN, GATE_ATTN, SHIFT_MLP, SCALE_MLP, GATE_MLP = range(6)
PROJ_BIAS, DOWN_BIAS, UP_BIAS, QKV_BIAS = 0, 2, 4, 6


def nn(left, right):
    return lax.dot_general(left, right, (((1,), (0,)), ((), ())), preferred_element_type=F32)


def nt(left, right):
    return lax.dot_general(left, right, (((1,), (1,)), ((), ())), preferred_element_type=F32)


def tn(left, right):
    return lax.dot_general(left, right, (((0,), (0,)), ((), ())), preferred_element_type=F32)


def shaped(shape, dtype=BF16):
    return jax.ShapeDtypeStruct(shape, dtype)


class Queue:
    def __init__(self):
        self.token = jnp.zeros((8, 128), F32)

    def tie(self, *values):
        *values, self.token = lax.optimization_barrier((*values, self.token))
        return values[0] if len(values) == 1 else tuple(values)

    def call(self, body, operands, outs, name, scalars=(), far=(), scratch=(), limit=16):
        fast = pl.BlockSpec(memory_space=pltpu.VMEM)
        small = pl.BlockSpec(memory_space=pltpu.SMEM)
        anywhere = pl.BlockSpec(memory_space=pl.ANY)
        inputs = len(scalars) + len(far) + len(operands)

        def whole(token_ref, *refs):
            body(*refs[: inputs + len(outs)], *refs[inputs + len(outs) + 1 :])
            refs[inputs + len(outs)][...] = token_ref[...]

        *results, self.token = pl.pallas_call(
            whole,
            in_specs=[fast] + [small] * len(scalars) + [anywhere] * len(far) + [fast] * len(operands),
            out_specs=[fast] * (len(outs) + 1),
            out_shape=[*outs, shaped((8, 128), F32)],
            scratch_shapes=list(scratch),
            cost_estimate=pl.CostEstimate(flops=1000, transcendentals=0, bytes_accessed=1000),
            compiler_params=pltpu.CompilerParams(vmem_limit_bytes=limit * MIB),
            name=name,
        )(
            pltpu.with_memory_space_constraint(self.token, pltpu.VMEM),
            *scalars,
            *far,
            *[pltpu.with_memory_space_constraint(value, pltpu.VMEM) for value in operands],
        )
        return results


def normed_of(values):
    center = values - jnp.mean(values, axis=-1, keepdims=True)
    spread = jnp.mean(center * center, axis=-1, keepdims=True)
    scale = lax.rsqrt(spread + EPSILON)
    return center * scale, scale


def modulate(values, mods_ref, at, scale_part, shift_part):
    block, latent = at
    scale = mods_ref[block, latent, scale_part : scale_part + 1, :]
    shift = mods_ref[block, latent, shift_part : shift_part + 1, :]
    return (normed_of(values)[0] * (1.0 + scale) + shift).astype(BF16)


def branch_of(near_ref, far_ref, small_ref, row, features):
    return (
        near_ref[...].astype(F32)
        + far_ref[...].astype(F32)
        + small_ref[row : row + 1, :features]
    )


class Rows:
    def __init__(self, *spans):
        self.spans = spans
        self.count = sum(span[2] for span in spans)

    def places(self, perm_ref, core, other=False):
        found = []
        for first, stride, count in self.spans:
            low = perm_ref[:, first : first + count]
            high = perm_ref[:, first + stride : first + stride + count]
            found.append(jnp.where((core == 1) != other, high, low))
        return found[0] if len(found) == 1 else jnp.concatenate(found, axis=1)


def pick_columns(places, length):
    index = lax.broadcasted_iota(jnp.int32, (length, places.shape[1]), 0)
    return (index == places).astype(F32).astype(BF16)


def gather_rows(queue, core, perm, source, rows):
    length, features = source.shape

    def body(core_ref, perm_ref, source_ref, out_ref):
        pick = pick_columns(rows.places(perm_ref, core_ref[0]), length)
        out_ref[...] = tn(pick, source_ref[...])

    outs = [shaped((rows.count, features), F32)]
    return queue.call(body, [perm, source], outs, "gather_rows", scalars=[core])[0]


def place_rows(queue, core, perm, pairs, rows):
    length = perm.shape[1]
    features = pairs[0][0].shape[1]

    def body(core_ref, perm_ref, *refs):
        out_ref = refs[-1]
        places = [
            chunk.places(perm_ref, core_ref[0], other) for chunk in rows for other in (False, True)
        ]
        values = jnp.concatenate([ref[...] for ref in refs[:-1]], axis=0)
        pick = pick_columns(jnp.concatenate(places, axis=1), length)
        out_ref[...] = nn(pick, values).astype(BF16)

    operands = [perm] + [half for pair in pairs for half in pair]
    outs = [shaped((length, features))]
    return queue.call(body, operands, outs, "place_rows", scalars=[core], limit=24)[0]


def table_rows(queue, core, perm, waves, rows, filler=None):
    side, half = waves.shape

    def body(core_ref, perm_ref, waves_ref, *refs):
        places = rows.places(perm_ref, core_ref[0])
        index = lax.broadcasted_iota(jnp.int32, (side, places.shape[1]), 0)
        row_pick = ((places >= index * side) & (places < (index + 1) * side)).astype(F32)
        row = jnp.sum(row_pick * index.astype(F32), axis=0, keepdims=True)
        col_pick = (index.astype(F32) == places.astype(F32) - row * side).astype(F32)
        for low, pick in ((0, row_pick), (half, col_pick)):
            out = lax.dot_general(
                pick,
                waves_ref[...],
                (((0,), (0,)), ((), ())),
                precision=lax.Precision.HIGHEST,
                preferred_element_type=F32,
            )
            if filler is not None:
                out = out + refs[0][:, low : low + half]
            refs[-1][:, low : low + half] = out

    operands = [perm, waves] + ([] if filler is None else [filler])
    outs = [shaped((rows.count, 2 * half), F32)]
    return queue.call(body, operands, outs, "table_rows", scalars=[core])[0]


def ln_open(queue, stream, mods, at):
    def body(x_ref, mods_ref, out_ref):
        out_ref[...] = modulate(x_ref[...], mods_ref, at, SCALE_ATTN, SHIFT_ATTN)

    return queue.call(body, [stream, mods], [shaped(stream.shape)], "ln_open")[0]


def near_sum(queue, own, moved):
    def body(own_ref, moved_ref, out_ref):
        out_ref[...] = (own_ref[...].astype(F32) + moved_ref[...].astype(F32)).astype(BF16)

    return queue.call(body, [own, moved], [shaped(own.shape)], "near_sum")[0]


def merge_attn(queue, stream, near, far, small, mods, at):
    features = stream.shape[1]
    block, latent = at

    def body(x_ref, near_ref, far_ref, small_ref, mods_ref, mid_ref, out_ref):
        branch = branch_of(near_ref, far_ref, small_ref, PROJ_BIAS + block, features)
        middle = x_ref[...] + mods_ref[block, latent, GATE_ATTN : GATE_ATTN + 1, :] * branch
        mid_ref[...] = middle
        out_ref[...] = modulate(middle, mods_ref, at, SCALE_MLP, SHIFT_MLP)

    outs = [shaped(stream.shape, F32), shaped(stream.shape)]
    return queue.call(body, [stream, near, far, small, mods], outs, "merge_attn")


def merge_mlp(queue, pieces, small, mods, at, table, tail):
    features = table.shape[1]
    counts = [piece[0].shape[0] for piece in pieces]
    block, latent = at
    total = sum(counts) + (0 if tail is None else tail.shape[0])
    following = (block + 1, latent)

    def body(table_ref, small_ref, mods_ref, *refs):
        x_ref, out_ref = refs[-2:]
        gate = mods_ref[block, latent, GATE_MLP : GATE_MLP + 1, :]
        first = 0
        for index, count in enumerate(counts):
            mid_ref, near_ref, far_ref = refs[3 * index : 3 * index + 3]
            branch = branch_of(near_ref, far_ref, small_ref, DOWN_BIAS + block, features)
            stream = mid_ref[...] + gate * branch + table_ref[first : first + count, :]
            x_ref[first : first + count, :] = stream
            out_ref[first : first + count, :] = modulate(
                stream, mods_ref, following, SCALE_ATTN, SHIFT_ATTN
            )
            first += count
        if tail is not None:
            stream = refs[3 * len(counts)][...]
            x_ref[first:, :] = stream
            out_ref[first:, :] = modulate(stream, mods_ref, following, SCALE_ATTN, SHIFT_ATTN)

    operands = [table, small, mods] + [part for piece in pieces for part in piece]
    operands += [] if tail is None else [tail]
    outs = [shaped((total, features), F32), shaped((total, features))]
    return queue.call(body, operands, outs, "merge_mlp")


def finish(queue, middle, near, far, d_out, small, mods, at):
    features = middle.shape[1]
    block, latent = at

    def body(mid_ref, near_ref, far_ref, d_ref, small_ref, mods_ref, out_ref, sums_ref):
        branch = branch_of(near_ref, far_ref, small_ref, DOWN_BIAS + block, features)
        gate = mods_ref[block, latent, GATE_MLP : GATE_MLP + 1, :]
        out_ref[...] = (mid_ref[...] + gate * branch).astype(BF16)
        total = jnp.sum(d_ref[...] * branch, axis=0, keepdims=True)
        sums_ref[...] = jnp.broadcast_to(total, (8, features))

    outs = [shaped(middle.shape), shaped((8, features), F32)]
    return queue.call(body, [middle, near, far, d_out, small, mods], outs, "finish")


def first_grad(queue, d_out, mods, at):
    features = d_out.shape[1]
    block, latent = at

    def body(d_ref, mods_ref, out_ref, sums_ref):
        gate = mods_ref[block, latent, GATE_MLP : GATE_MLP + 1, :]
        grad = (gate * d_ref[...]).astype(BF16)
        out_ref[...] = grad
        total = jnp.sum(grad.astype(F32), axis=0, keepdims=True)
        sums_ref[...] = jnp.broadcast_to(total, (8, features))

    outs = [shaped(d_out.shape), shaped((8, features), F32)]
    return queue.call(body, [d_out, mods], outs, "first_grad")


def qkv_forward(queue, own, other, weight, small, block):
    rows = own.shape[0]
    width = weight.shape[1]

    def body(own_ref, other_ref, w_ref, small_ref, out_ref):
        bias = small_ref[QKV_BIAS + block : QKV_BIAS + block + 1, :width]
        both = jnp.concatenate([own_ref[...], other_ref[...]], axis=0)
        out = (nt(both, w_ref[block]) + bias).astype(BF16)
        out_ref[0] = out[:rows]
        out_ref[1] = out[rows:]

    outs = [shaped((2, rows, width))]
    return queue.call(body, [own, other, weight, small], outs, "qkv_forward")[0]


def qkv_backward(queue, grads, weight, block):
    _, rows, _ = grads.shape
    features = weight.shape[2]

    def body(g_ref, w_ref, own_ref, other_ref):
        both = jnp.concatenate([g_ref[0], g_ref[1]], axis=0)
        out = nn(both, w_ref[block]).astype(BF16)
        own_ref[...] = out[:rows]
        other_ref[...] = out[rows:]

    outs = [shaped((rows, features)), shaped((rows, features))]
    return queue.call(body, [grads, weight], outs, "qkv_backward")


def mlp_forward(queue, own, other, up_weight, down_weight, small, block):
    rows, features = own.shape
    wide = up_weight.shape[2]

    def body(own_ref, other_ref, up_ref, down_ref, small_ref, own_out, other_out, act_ref, slope_ref):
        bias = small_ref[UP_BIAS + block : UP_BIAS + block + 1, :wide]
        both = jnp.concatenate([own_ref[...], other_ref[...]], axis=0)
        hidden = nn(both, up_ref[block]) + bias
        squared = hidden * hidden
        bent = jnp.tanh(GELU_A * hidden * (1.0 + GELU_B * squared))
        half = 0.5 + 0.5 * bent
        active = (hidden * half).astype(BF16)
        slope = half + 0.5 * hidden * (1.0 - bent * bent) * (
            GELU_A + 3.0 * GELU_A * GELU_B * squared
        )
        act_ref[...] = active
        slope_ref[...] = slope.astype(BF16)
        out = nn(active, down_ref[block]).astype(BF16)
        own_out[...] = out[:rows]
        other_out[...] = out[rows:]

    part, full = shaped((rows, features)), shaped((2 * rows, wide))
    operands = [own, other, up_weight, down_weight, small]
    return queue.call(body, operands, [part, part, full, full], "mlp_forward")


def mlp_backward(queue, own, other, slope, up_weight, down_weight, block):
    rows, features = own.shape
    wide = up_weight.shape[2]

    def body(own_ref, other_ref, slope_ref, up_ref, down_ref, own_out, other_out, hid_ref):
        both = jnp.concatenate([own_ref[...], other_ref[...]], axis=0)
        d_active = nt(both, down_ref[block])
        d_hidden = (d_active * slope_ref[...].astype(F32)).astype(BF16)
        hid_ref[...] = d_hidden
        out = nt(d_hidden, up_ref[block]).astype(BF16)
        own_out[...] = out[:rows]
        other_out[...] = out[rows:]

    part = shaped((rows, features))
    operands = [own, other, slope, up_weight, down_weight]
    return queue.call(body, operands, [part, part, shaped((2 * rows, wide))], "mlp_backward")


def ln_back(queue, near, far, stream, d_out, mods, at, scale_part, branch=None, narrow=False):
    rows, features = stream.shape
    pieces = [] if branch is None else branch[0]
    counts = [piece[0].shape[0] for piece in pieces]
    inner = sum(counts)
    operands = [near, far, stream, d_out, mods]
    outs = [shaped((8, features), F32)]
    if narrow:
        outs.append(shaped((rows, features)))
    if pieces:
        _, small, bias_row, gate_at, gate_part = branch
        operands += [small] + [half for piece in pieces for half in piece]
        outs += [shaped((count, features), F32) for count in counts]
        outs += [shaped((count, features)) for count in counts]
    inputs = len(operands)

    def body(*refs):
        near_ref, far_ref, x_ref, d_ref, mods_ref = refs[:5]
        sums_ref, *out_refs = refs[inputs:]
        scale = mods_ref[at[0], at[1], scale_part : scale_part + 1, :]
        d_normed = near_ref[...].astype(F32) + far_ref[...].astype(F32)
        normed, spread = normed_of(x_ref[...])
        product = d_normed * normed
        grad = d_normed * (1.0 + scale)
        d_x = d_ref[...] + spread * (
            grad
            - jnp.mean(grad, axis=-1, keepdims=True)
            - normed * jnp.mean(grad * normed, axis=-1, keepdims=True)
        )
        zero = jnp.zeros((1, features), F32)
        gate_sum, bias_sum, rest_sum = zero, zero, zero
        if narrow:
            out_refs[0][...] = d_x.astype(BF16)
        elif inner < rows:
            rest_sum = jnp.sum(d_x[inner:], axis=0, keepdims=True)
        first = 0
        for index, count in enumerate(counts):
            piece_near, piece_far = refs[6 + 2 * index : 8 + 2 * index]
            value = branch_of(piece_near, piece_far, refs[5], bias_row, features)
            part = d_x[first : first + count]
            gate = mods_ref[gate_at[0], gate_at[1], gate_part : gate_part + 1, :]
            d_branch = (gate * part).astype(BF16)
            out_refs[index][...] = part
            out_refs[len(counts) + index][...] = d_branch
            gate_sum = gate_sum + jnp.sum(part * value, axis=0, keepdims=True)
            bias_sum = bias_sum + jnp.sum(d_branch.astype(F32), axis=0, keepdims=True)
            first += count
        sums_ref[...] = jnp.concatenate(
            [
                jnp.sum(product, axis=0, keepdims=True),
                jnp.sum(d_normed, axis=0, keepdims=True),
                gate_sum,
                bias_sum,
                rest_sum,
                jnp.zeros((3, features), F32),
            ],
            axis=0,
        )

    return queue.call(body, operands, outs, "ln_back")


def attn_forward(queue, query, merged, proj_weight, block):
    _, rows, width = query.shape
    local = width // 3
    heads = local // HEAD_DIM
    counts = [part.shape[1] for part in merged]
    total = 2 * sum(counts)
    features = proj_weight.shape[2]
    by_keys = rows < 128

    def body(*refs):
        q_ref, refs = refs[0], refs[1:]
        kv_refs, refs = refs[: len(merged)], refs[len(merged) :]
        proj_ref, att_ref, lse_ref, own_out, other_out, q_s, k_s, v_s, o_s, l_s = refs
        for head in range(heads):
            low = head * HEAD_DIM
            first = 0
            for part, count in zip(kv_refs, counts):
                for side in range(2):
                    at = pl.ds(first, count)
                    k_s[head, at, :] = part[side, :, local + low : local + low + HEAD_DIM]
                    v_s[head, at, :] = part[side, :, 2 * local + low : 2 * local + low + HEAD_DIM]
                    first += count
            for side in range(2):
                q_s[head, side] = q_ref[side, :, low : low + HEAD_DIM]
        for head in range(heads):
            for side in range(2):
                if by_keys:
                    scores = nt(k_s[head], q_s[head, side])
                    highest = jnp.max(scores, axis=0, keepdims=True)
                    raised = jnp.exp2((scores - highest) * EXPONENT)
                    total_row = jnp.sum(raised, axis=0, keepdims=True)
                    out = tn(v_s[head], raised.astype(BF16))
                    o_s[head, side] = (out / total_row).T.astype(BF16)
                    lse_ref[head, side] = highest * EXPONENT + jnp.log2(total_row)
                else:
                    scores = nt(q_s[head, side], k_s[head])
                    highest = jnp.max(scores, axis=1, keepdims=True)
                    raised = jnp.exp2((scores - highest) * EXPONENT)
                    total_row = jnp.sum(raised, axis=1, keepdims=True)
                    out = nn(raised.astype(BF16), v_s[head])
                    o_s[head, side] = (out / total_row).astype(BF16)
                    l_s[head, side] = jnp.broadcast_to(
                        highest * EXPONENT + jnp.log2(total_row), (rows, 128)
                    )
        if not by_keys:
            for head in range(heads):
                for side in range(2):
                    lse_ref[head, side] = l_s[head, side].T[:1]
        for side, out_ref in ((1, other_out), (0, own_out)):
            for head in range(heads):
                low = head * HEAD_DIM
                att_ref[side * rows : (side + 1) * rows, low : low + HEAD_DIM] = o_s[head, side]
            out_ref[...] = nn(
                att_ref[side * rows : (side + 1) * rows, :], proj_ref[block]
            ).astype(BF16)

    return queue.call(
        body,
        [query, *merged, proj_weight],
        [
            shaped((2 * rows, local)),
            shaped((heads, 2, 1, rows), F32),
            shaped((rows, features)),
            shaped((rows, features)),
        ],
        "attn_forward",
        scratch=[
            pltpu.VMEM((heads, 2, rows, HEAD_DIM), BF16),
            pltpu.VMEM((heads, total, HEAD_DIM), BF16),
            pltpu.VMEM((heads, total, HEAD_DIM), BF16),
            pltpu.VMEM((heads, 2, rows, HEAD_DIM), BF16),
            pltpu.VMEM((heads, 2, 8 if by_keys else rows, 128), F32),
        ],
        limit=24,
    )


def attn_backward(queue, merged, normers, grads, proj_weight, block):
    count = len(merged)
    width = merged[0].shape[2]
    local = width // 3
    heads = local // HEAD_DIM
    halves = [part.shape[1] for part in merged]
    total = 2 * sum(halves)
    step = min(halves)
    steps = total // step
    unroll = 4 if step * steps > 512 else steps * heads

    def body(*refs):
        m_refs, refs = refs[:count], refs[count:]
        l_refs, refs = refs[:count], refs[count:]
        g_refs, refs = refs[: 2 * count], refs[2 * count :]
        proj_ref, refs = refs[0], refs[1:]
        out_refs, refs = refs[:count], refs[count:]
        q_s, k_s, kt_s, v_s, g_s, dq_s, dk_s, dv_s, l_s = refs
        first = 0
        for index in range(count):
            rows = halves[index]
            for side in range(2):
                at = pl.ds(first, rows)
                grad = nt(g_refs[2 * index + side][...], proj_ref[block]).astype(BF16)
                for head in range(heads):
                    low = head * HEAD_DIM
                    part = m_refs[index]
                    q_s[head, at, :] = part[side, :, low : low + HEAD_DIM]
                    keys = part[side, :, local + low : local + low + HEAD_DIM]
                    k_s[head, at, :] = keys
                    kt_s[head, :, at] = keys.T
                    v_s[head, at, :] = part[side, :, 2 * local + low : 2 * local + low + HEAD_DIM]
                    g_s[head, at, :] = grad[:, low : low + HEAD_DIM]
                    for piece in range(rows // step):
                        l_s[head, first // step + piece] = l_refs[index][
                            head, side, :, piece * step : (piece + 1) * step
                        ]
                first += rows
        dk_s[...] = jnp.zeros_like(dk_s)
        dv_s[...] = jnp.zeros_like(dv_s)

        def one(index, carry):
            head, piece = index // steps, lax.rem(index, steps)
            at = pl.ds(pl.multiple_of(piece * step, step), step)
            queries, grad = q_s[head, at, :], g_s[head, at, :]
            probs = jnp.exp2(nt(k_s[head], queries) * EXPONENT - l_s[head, piece])
            product = probs * nt(v_s[head], grad)
            delta = jnp.sum(product, axis=0, keepdims=True)
            d_scores = (product - probs * delta).astype(BF16)
            dv_s[head] += nn(probs.astype(BF16), grad)
            dk_s[head] += nn(d_scores, queries)
            dq_s[head, at, :] = (nn(kt_s[head], d_scores) * SCALING).T.astype(BF16)
            return carry

        lax.fori_loop(0, steps * heads, one, 0, unroll=unroll)
        first = 0
        for index in range(count):
            rows = halves[index]
            for side in range(2):
                at = pl.ds(first, rows)
                out = out_refs[index]
                for head in range(heads):
                    low = head * HEAD_DIM
                    out[side, :, low : low + HEAD_DIM] = dq_s[head, at, :]
                    out[side, :, local + low : local + low + HEAD_DIM] = (
                        dk_s[head, at, :] * SCALING
                    ).astype(BF16)
                    out[side, :, 2 * local + low : 2 * local + low + HEAD_DIM] = dv_s[
                        head, at, :
                    ].astype(BF16)
                first += rows

    def lanes(dtype=BF16):
        return pltpu.VMEM((heads, total, HEAD_DIM), dtype)

    return queue.call(
        body,
        [*merged, *normers, *[half for pair in grads for half in pair], proj_weight],
        [shaped(part.shape) for part in merged],
        "attn_backward",
        scratch=[
            lanes(),
            lanes(),
            pltpu.VMEM((heads, HEAD_DIM, total), BF16),
            lanes(),
            lanes(),
            lanes(),
            lanes(F32),
            lanes(F32),
            pltpu.VMEM((heads, steps, 1, step), F32),
        ],
        limit=28,
    )


def split_at(bits, bit):
    place = len(bits) - 1 - bits.index(bit)
    stride = 1 << place
    return [index for index in range(1 << len(bits)) if not index & stride], stride


def weight_grads(queue, pairs, mine, bits, bit):
    blocks = 1 << len(bits)
    features = pairs[0][0][0].shape[1]
    widths = [rights[0].shape[1] for _, rights in pairs]
    each = features // blocks
    rows = sum(part.shape[0] for part in pairs[0][0])
    far, plan, scratch = [], [], []
    for number, (lefts, rights) in enumerate(pairs):
        for place, parts in enumerate((lefts, rights)):
            first = 0
            for part in parts:
                plan.append((len(far), 2 * number + place, first, part.shape[0]))
                far.append(part)
                first += part.shape[0]
            scratch.append(pltpu.VMEM((rows, parts[0].shape[1]), BF16))
    buffers = len(scratch)
    scratch.append(pltpu.VMEM((blocks, each, sum(widths)), BF16))
    scratch.append(pltpu.SemaphoreType.DMA((len(plan),)))
    out = shaped((blocks // 2, each, sum(widths)))
    starts, stride = split_at(bits, bit)

    def body(mine_ref, *refs):
        sources, refs = refs[: len(far)], refs[len(far) :]
        kept_ref, away_ref, sums_ref, *held = refs
        full, done = held[buffers], held[buffers + 1]
        copies = [
            pltpu.make_async_copy(
                sources[source], held[buffer].at[pl.ds(first, count)], done.at[index]
            )
            for index, (source, buffer, first, count) in enumerate(plan)
        ]
        for copy in copies:
            copy.start()
        low = 0
        ones = jnp.ones((8, rows), BF16)
        for number, width in enumerate(widths):
            for copy, (_, buffer, _, _) in zip(copies, plan):
                if buffer // 2 == number:
                    copy.wait()
            left, right = held[2 * number][...], held[2 * number + 1][...]
            total = tn(left, right).astype(BF16)
            columns = slice(low, low + width)
            for block in range(blocks):
                full[block, :, columns] = total[block * each : (block + 1) * each]
            sums_ref[:, columns] = nn(ones, right)
            low += width
        at = mine_ref[0] * stride
        for index, start in enumerate(starts):
            kept_ref[index] = full[start + at]
            away_ref[index] = full[start + stride - at]

    return queue.call(
        body,
        [],
        [out, out, shaped((8, sum(widths)), F32)],
        "weight_grads",
        scalars=[mine],
        far=far,
        scratch=scratch,
        limit=32,
    )


def halve(queue, kept, moved, mine, bits, bit):
    blocks, each, width = kept.shape
    out = shaped((blocks // 2, each, width))
    starts, stride = split_at(bits, bit)

    def body(mine_ref, kept_ref, moved_ref, next_ref, away_ref):
        at = mine_ref[0] * stride
        for place, out_ref in ((stride - at, away_ref), (at, next_ref)):
            for index, start in enumerate(starts):
                total = kept_ref[start + place].astype(F32) + moved_ref[start + place].astype(F32)
                out_ref[index] = total.astype(BF16)

    return queue.call(body, [kept, moved], [out, out], "halve", scalars=[mine])


def spread_mods(queue, me, columns, features):
    size, latents, blocks, each = columns.shape

    def body(me_ref, in_ref, out_ref, flat):
        for device in range(size):
            block = in_ref[jnp.bitwise_xor(device, me_ref[0])].astype(F32)
            for latent in range(latents):
                flat[latent, :, device * each : (device + 1) * each] = block[latent]
        for latent in range(latents):
            for part in range(6):
                rows = flat[latent, :, part * features : (part + 1) * features]
                for index in range(blocks):
                    out_ref[index, latent, part : part + 1, :] = rows[index : index + 1]

    return queue.call(
        body,
        [columns],
        [shaped((blocks, latents, 6, features), F32)],
        "spread_mods",
        scalars=[me],
        scratch=[pltpu.VMEM((latents, blocks, size * each), F32)],
    )[0]


def collect_sums(queue, sources, recipe):
    features = sources[0].shape[1]
    count = -(-len(recipe) // 8) * 8

    def body(*refs):
        out_ref = refs[-1]
        for index, terms in enumerate(recipe):
            total = None
            for source, row in terms:
                term = refs[source][row : row + 1, :]
                total = term if total is None else total + term
            out_ref[index : index + 1, :] = total
        if count > len(recipe):
            out_ref[len(recipe) :, :] = jnp.zeros((count - len(recipe), features), F32)

    return queue.call(body, sources, [shaped((count, features), F32)], "collect_sums")[0]


def pack_mods(queue, me, own, moved, latents, blocks, size, features):
    each = 6 * features // size
    rows = own.shape[0]

    def body(me_ref, own_ref, moved_ref, out_ref, total_ref, flat):
        total = own_ref[...] + moved_ref[...]
        total_ref[...] = total
        for latent in range(latents):
            for index in range(blocks):
                for part in range(6):
                    row = (index * latents + latent) * 6 + part
                    flat[latent, index : index + 1, part * features : (part + 1) * features] = total[
                        row : row + 1
                    ]
        for device in range(size):
            for latent in range(latents):
                out_ref[jnp.bitwise_xor(device, me_ref[0]), latent] = flat[
                    latent, :, device * each : (device + 1) * each
                ].astype(BF16)

    return queue.call(
        body,
        [own, moved],
        [shaped((size, latents, blocks, each)), shaped((rows, features), F32)],
        "pack_mods",
        scalars=[me],
        scratch=[pltpu.VMEM((latents, blocks, 6 * features), F32)],
    )


def partners(size, bit):
    return [(index, index ^ bit) for index in range(size)]


def bits_of(size):
    bits = []
    while (1 << len(bits)) < size:
        bits.append(1 << len(bits))
    assert (1 << len(bits)) == size
    return bits


class Links:
    def __init__(self, dp_size, tensor_size):
        self.dp_size = dp_size
        self.tensor_size = tensor_size
        self.dp_bits = bits_of(dp_size)
        me = lax.axis_index("dp")
        self.me = me.reshape(1)
        self.core = lax.rem(lax.axis_index("tensor"), 2).reshape(1)
        self.mine = {bit: lax.rem(me // bit, 2).reshape(1) for bit in self.dp_bits}

    def swap(self, value):
        return lax.ppermute(value, "tensor", partners(self.tensor_size, 1))

    def cross(self, value):
        return lax.ppermute(value, "tensor", partners(self.tensor_size, 2))

    def dp_move(self, value, bit):
        return lax.ppermute(value, "dp", partners(self.dp_size, bit))

    def gather_relative(self, value):
        held = value[None]
        for bit in self.dp_bits:
            held = jnp.concatenate([held, self.dp_move(held, bit)], axis=0)
        return held

    def exchange_relative(self, value):
        held = value
        for bit in self.dp_bits:
            split = held.reshape((self.dp_size // (2 * bit), 2, bit) + held.shape[1:])
            moved = self.dp_move(split[:, 1], bit)
            held = jnp.stack([split[:, 0], moved], axis=1).reshape(held.shape)
        return held

    def sum_relative(self, value):
        held = value
        for bit in reversed(self.dp_bits):
            moved = self.dp_move(held[bit:].astype(BF16), bit)
            held = held[:bit].astype(F32) + moved.astype(F32)
        return held[0]

    def sum_all(self, value):
        held = value
        for bit in self.dp_bits:
            held = held + self.dp_move(held, bit)
        return held


class ScatterSum:
    def __init__(self, queue, links, pairs, order):
        self.queue, self.links = queue, links
        self.order = list(order)
        self.open = sorted(self.order, reverse=True)
        bit = self.order[0]
        self.kept, away, self.sums = weight_grads(
            queue, pairs, links.mine[bit], self.open, bit
        )
        self.send(away)

    def send(self, away):
        bit = self.order.pop(0)
        self.open.remove(bit)
        self.moved = self.links.dp_move(away, bit)

    def step(self):
        if self.order:
            bit = self.order[0]
            self.kept, away = halve(
                self.queue, self.kept, self.moved, self.links.mine[bit], self.open, bit
            )
            self.send(away)

    def result(self):
        while self.order:
            self.step()
        return self.kept[0].astype(F32) + self.moved[0].astype(F32)


class Weights:
    def __init__(self, qkv, proj, up, down, small, mods):
        self.qkv, self.proj, self.up, self.down = qkv, proj, up, down
        self.small, self.mods = small, mods


class Chunk:
    def __init__(self, queue, links, weights, block, latent, family):
        self.queue, self.links, self.weights = queue, links, weights
        self.block, self.latent, self.at = block, latent, (block, latent)
        self.family = family
        family.append(self)

    def enter(self, stream, normed):
        self.x = stream
        self.normed_attn = (normed, self.links.swap(normed))

    def qkv(self):
        w = self.weights
        self.merged = qkv_forward(self.queue, *self.normed_attn, w.qkv, w.small, self.block)

    def attention(self):
        merged = [chunk.merged for chunk in self.family]
        self.attended, self.normer, own, other = attn_forward(
            self.queue, self.merged, merged, self.weights.proj, self.block
        )
        self.part = (own, self.links.swap(other))

    def near(self):
        near = near_sum(self.queue, *self.part)
        self.sum = (near, self.links.cross(near))

    def merge(self):
        w = self.weights
        self.branch_attn = self.sum
        self.middle, normed = merge_attn(
            self.queue, self.x, *self.branch_attn, w.small, w.mods, self.at
        )
        self.normed_mlp = (normed, self.links.swap(normed))

    def mlp(self):
        w = self.weights
        own, other, self.active, self.slope = mlp_forward(
            self.queue, *self.normed_mlp, w.up, w.down, w.small, self.block
        )
        self.part = (own, self.links.swap(other))

    def start_back(self, d_out, d_branch):
        self.d_out = d_out
        self.d_branch_mlp = (d_branch, self.links.swap(d_branch))

    def mlp_back(self):
        w = self.weights
        own, other, self.d_hidden = mlp_backward(
            self.queue, *self.d_branch_mlp, self.slope, w.up, w.down, self.block
        )
        self.part = (own, self.links.swap(other))

    def merge_back(self):
        w = self.weights
        branch = ([self.branch_attn], w.small, PROJ_BIAS + self.block, self.at, GATE_ATTN)
        self.mlp_sums, self.d_middle, grad = ln_back(
            self.queue, *self.sum, self.middle, self.d_out, w.mods, self.at, SCALE_MLP, branch
        )
        self.d_branch_attn = (grad, self.links.swap(grad))

    def attention_back(self):
        family = self.family
        grads = attn_backward(
            self.queue,
            [chunk.merged for chunk in family],
            [chunk.normer for chunk in family],
            [chunk.d_branch_attn for chunk in family],
            self.weights.proj,
            self.block,
        )
        for chunk, grad in zip(family, grads):
            chunk.d_qkv = grad

    def qkv_back(self):
        own, other = qkv_backward(self.queue, self.d_qkv, self.weights.qkv, self.block)
        self.part = (own, self.links.swap(other))

    def leave_back(self, branch=None, narrow=False):
        w = self.weights
        self.attn_sums, *rest = ln_back(
            self.queue,
            *self.sum,
            self.x,
            self.d_middle,
            w.mods,
            self.at,
            SCALE_ATTN,
            branch,
            narrow,
        )
        return rest


def pair_rows(chunks, name):
    return [half for chunk in chunks for half in getattr(chunk, name)]


def flat_rows(chunks, name):
    return [
        getattr(chunk, name).reshape(-1, getattr(chunk, name).shape[-1]) for chunk in chunks
    ]


def on_device(dp_size, tensor_size, *arguments):
    (
        tokens_long,
        tokens_short,
        cond_long,
        cond_short,
        perm_long,
        perm_short,
        ada_weight,
        ada_bias,
        qkv_weight,
        qv_bias,
        proj_weight,
        proj_bias,
        up_weight,
        up_bias,
        down_weight,
        down_bias,
        mask_token,
        cot_long,
        cot_short,
    ) = arguments
    assert tokens_long.shape[0] == 1 and tokens_short.shape[0] == 1
    queue = Queue()
    links = Links(dp_size, tensor_size)
    core = links.core
    features = tokens_long.shape[2]
    wide = up_weight.shape[2]
    local = qv_bias.shape[2]
    tokens = (tokens_long[0], tokens_short[0])
    cots = (cot_long[0], cot_short[0])
    perms = (perm_long, perm_short)
    lengths = tuple(rows.shape[0] for rows in tokens)
    kept = tuple(length // 2 for length in lengths)

    cond = jnp.concatenate([cond_long, cond_short]).astype(F32)
    acts = links.gather_relative(jax.nn.silu(cond).astype(BF16))
    flat_acts = acts.reshape(-1, features)
    columns = jnp.einsum("nd,ldm->nlm", flat_acts, ada_weight, preferred_element_type=F32)
    columns = (columns + ada_bias.astype(F32)[None]).astype(BF16)
    columns = links.exchange_relative(columns.reshape((dp_size, 2) + columns.shape[1:]))

    table_width = max(features, wide, 3 * local)

    def padded(rows):
        return jnp.pad(rows.astype(F32), ((0, 0), (0, table_width - rows.shape[1])))

    qkv_bias = jnp.concatenate(
        [qv_bias[:, 0], jnp.zeros_like(qv_bias[:, 0]), qv_bias[:, 1]], axis=1
    )
    small = jnp.concatenate([padded(proj_bias), padded(down_bias), padded(up_bias), padded(qkv_bias)])

    long_half, short_half = kept[0] // 2, kept[1] // 2
    quarter = long_half // 2
    enc_rows = [
        Rows((0, long_half, quarter)),
        Rows((quarter, long_half, quarter)),
        Rows((0, short_half, short_half)),
    ]
    table_places = [Rows((0, long_half, long_half)), Rows((0, short_half, short_half))]
    masked_places = [
        Rows((kept[0], long_half, long_half)),
        Rows((kept[1], short_half, short_half)),
    ]
    dec_rows = [
        table_places[0],
        masked_places[0],
        Rows((0, short_half, short_half), (kept[1], short_half, short_half)),
    ]
    enc_latents, dec_latents = (0, 0, 1), (0, 0, 1)

    streams = [
        gather_rows(queue, core, perms[latent], tokens[latent], rows)
        for latent, rows in zip(enc_latents, enc_rows)
    ]
    mods = spread_mods(queue, links.me, columns, features)
    weights = Weights(
        jnp.transpose(qkv_weight, (0, 2, 3, 1)).reshape(2, 3 * local, features),
        proj_weight,
        up_weight,
        down_weight,
        small,
        mods,
    )
    families = {(block, latent): [] for block in (0, 1) for latent in (0, 1)}

    def chunks_of(block, latents):
        return [
            Chunk(queue, links, weights, block, latent, families[block, latent])
            for latent in latents
        ]

    encoder = chunks_of(0, enc_latents)
    decoder = chunks_of(1, dec_latents)
    ea, eb, es = encoder
    dk, dm, dt = decoder

    for chunk, stream in zip(encoder, streams):
        chunk.enter(stream, ln_open(queue, stream, mods, chunk.at))
    for chunk in encoder:
        chunk.qkv()
    ea.attention()
    eb.attention()
    ea.near()
    es.attention()
    eb.near()
    es.near()
    perms_later, filler, cots_later = queue.tie(perms, mask_token, cots)
    filler = filler.astype(F32)[None]
    waves = []
    for length in lengths:
        side = math.isqrt(length)
        quarter_wave = features // 4
        frequency = 1.0 / 10000.0 ** (jnp.arange(quarter_wave, dtype=F32) / quarter_wave)
        angle = jnp.arange(side, dtype=jnp.int32).astype(F32)[:, None] * frequency[None, :]
        waves.append(jnp.concatenate([jnp.sin(angle), jnp.cos(angle)], axis=1))
    masked = table_rows(queue, core, perms_later[0], waves[0], masked_places[0], filler)
    dm.enter(masked, ln_open(queue, masked, mods, dm.at))
    ea.merge()
    dm.qkv()
    ea.mlp()
    eb.merge()
    ea.near()
    es.merge()
    eb.mlp()
    es.mlp()
    eb.near()
    es.near()
    table_long = table_rows(queue, core, perms_later[0], waves[0], table_places[0])
    table_short = table_rows(queue, core, perms_later[1], waves[1], table_places[1])
    masked_short = table_rows(queue, core, perms_later[1], waves[1], masked_places[1], filler)
    d_out = [
        gather_rows(queue, core, perms_later[latent], cots_later[latent], rows)
        for latent, rows in zip(dec_latents, dec_rows)
    ]
    first_sums = []
    for chunk, grad in zip(decoder, d_out):
        d_branch, sums = first_grad(queue, grad, mods, chunk.at)
        first_sums.append(sums)
        chunk.start_back(grad, d_branch)

    pieces = [(chunk.middle, *chunk.sum) for chunk in encoder]
    for chunk in encoder:
        chunk.branch_mlp = chunk.sum
    dk.enter(*merge_mlp(queue, pieces[:2], small, mods, (0, 0), table_long, None))
    dt.enter(*merge_mlp(queue, pieces[2:], small, mods, (0, 1), table_short, masked_short))
    dk.qkv()
    dk.attention()
    dt.qkv()
    dk.near()
    dm.attention()
    dt.attention()
    dm.near()
    dt.near()
    dk.merge()
    dk.mlp()
    dm.merge()
    dk.near()
    dt.merge()
    forward_sums = [dk.sum]
    dm.mlp()
    dk.mlp_back()
    dm.near()
    forward_sums.append(dm.sum)
    dt.mlp()
    dm.mlp_back()
    dt.near()
    forward_sums.append(dt.sum)
    dt.mlp_back()

    dt.near()
    dk.near()
    dm.near()
    y_first, z_first = list(links.dp_bits), list(links.dp_bits)
    if len(z_first) > 1:
        z_first[0], z_first[1] = z_first[1], z_first[0]

    def wide_sum(chunks, left, right, order):
        return ScatterSum(queue, links, [(pair_rows(chunks, left), flat_rows(chunks, right))], order)

    dec_up = wide_sum(decoder, "normed_mlp", "d_hidden", y_first)
    decoded, gate_sums = [], []
    for chunk, grad, summed in zip(decoder, d_out, forward_sums):
        own, sums = finish(queue, chunk.middle, *summed, grad, small, mods, chunk.at)
        gate_sums.append(sums)
        decoded.append((own, links.swap(own)))
    dt.merge_back()
    dec_down = wide_sum(decoder, "d_branch_mlp", "active", z_first)
    dt.attention_back()
    dk.merge_back()
    dt.qkv_back()
    dt.near()
    dm.merge_back()
    dm.attention_back()
    dk.qkv_back()
    dm.qkv_back()
    dk.near()
    dm.near()

    enc_branch = (small, DOWN_BIAS, (0, 0), GATE_MLP)
    short_branch = (small, DOWN_BIAS, (0, 1), GATE_MLP)
    d_short, grad_short = dt.leave_back(([es.branch_mlp], *short_branch))
    es.start_back(d_short, grad_short)
    dec_proj = ScatterSum(
        queue,
        links,
        [
            (pair_rows(decoder, "d_branch_attn"), flat_rows(decoder, "attended")),
            (pair_rows(decoder, "normed_attn"), flat_rows(decoder, "d_qkv")),
        ],
        y_first,
    )
    dec_up.step()
    d_a, d_b, grad_a, grad_b = dk.leave_back(([ea.branch_mlp, eb.branch_mlp], *enc_branch))
    ea.start_back(d_a, grad_a)
    eb.start_back(d_b, grad_b)

    es.mlp_back()
    ea.mlp_back()
    eb.mlp_back()
    es.near()
    ea.near()
    eb.near()
    dm.leave_back()
    dec_down.step()
    enc_up = wide_sum(encoder, "normed_mlp", "d_hidden", y_first)
    es.merge_back()
    enc_down = wide_sum(encoder, "d_branch_mlp", "active", z_first)
    es.attention_back()
    es.qkv_back()
    ea.merge_back()
    es.near()
    eb.merge_back()
    ea.attention_back()
    ea.qkv_back()
    eb.qkv_back()
    ea.near()
    eb.near()
    enc_proj = ScatterSum(
        queue,
        links,
        [
            (pair_rows(encoder, "d_branch_attn"), flat_rows(encoder, "attended")),
            (pair_rows(encoder, "normed_attn"), flat_rows(encoder, "d_qkv")),
        ],
        y_first,
    )
    own_tokens = []
    for chunk in (es, ea, eb):
        (own,) = chunk.leave_back(narrow=True)
        own_tokens.append((own, links.swap(own)))

    sources, recipe = [], []

    def row(array, index):
        for place, source in enumerate(sources):
            if source is array:
                return place, index
        sources.append(array)
        return len(sources) - 1, index

    for block, chunks in ((0, encoder), (1, decoder)):
        for latent in (0, 1):
            members = [chunk for chunk in chunks if chunk.latent == latent]
            if block == 0:
                gates = [row((dk, dt)[latent].attn_sums, 2)]
            else:
                gates = [
                    row(gate_sums[index], 0)
                    for index, chunk in enumerate(decoder)
                    if chunk.latent == latent
                ]
            recipe += [
                [row(chunk.attn_sums, 1) for chunk in members],
                [row(chunk.attn_sums, 0) for chunk in members],
                [row(chunk.mlp_sums, 2) for chunk in members],
                [row(chunk.mlp_sums, 1) for chunk in members],
                [row(chunk.mlp_sums, 0) for chunk in members],
                gates,
            ]
    recipe += [
        [row(chunk.mlp_sums, 3) for chunk in encoder],
        [row(chunk.mlp_sums, 3) for chunk in decoder],
        [row(chunk.attn_sums, 3) for chunk in (dk, dt)],
        [row(sums, 0) for sums in first_sums],
        [row(chunk.attn_sums, 4) for chunk in (dm, dt)],
    ]
    own_sums = collect_sums(queue, sources, recipe)
    packed, all_sums = pack_mods(
        queue, links.me, own_sums, links.swap(own_sums), 2, 2, dp_size, features
    )
    mine = links.exchange_relative(packed)
    flat_mine = mine.reshape((-1,) + mine.shape[2:])
    grad_ada = jnp.einsum("nd,nlm->ldm", flat_acts, flat_mine, preferred_element_type=F32)
    grad_ada_bias = jnp.sum(flat_mine.astype(F32), axis=0)
    d_acts = jnp.einsum("nlm,ldm->nd", flat_mine, ada_weight, preferred_element_type=F32)
    d_act = links.sum_relative(d_acts.reshape(dp_size, 2, features))
    gate = jax.nn.sigmoid(cond)
    d_cond = (d_act * gate * (1.0 + cond * (1.0 - gate))).astype(BF16)

    qkv_sums = [part.sums[0, local:] for part in (enc_proj, dec_proj)]
    totals = jnp.concatenate(
        [all_sums[24:29].reshape(-1), enc_up.sums[0], dec_up.sums[0]]
        + [part for sums in qkv_sums for part in (sums[:local], sums[2 * local :])]
    )
    totals = links.sum_all(totals)
    proj_out = totals[: 2 * features].reshape(2, features)
    down_out = totals[2 * features : 4 * features].reshape(2, features)
    mask_out = totals[4 * features : 5 * features]
    first = 5 * features
    up_out = totals[first : first + 2 * wide].reshape(2, wide)
    first += 2 * wide
    qv_out = totals[first : first + 4 * local].reshape(2, 2, local)

    for part in (enc_up, dec_proj, enc_down, dec_up, dec_down):
        part.step()
    results = (
        place_rows(queue, core, perms_later[0], decoded[:2], dec_rows[:2]),
        place_rows(queue, core, perms_later[1], decoded[2:], dec_rows[2:]),
    )
    for part in (enc_up, dec_proj, enc_down, enc_proj):
        part.step()
    d_tokens = (
        place_rows(queue, core, perms_later[0], own_tokens[1:], enc_rows[:2]),
        place_rows(queue, core, perms_later[1], own_tokens[:1], enc_rows[2:]),
    )
    enc_att, dec_att = enc_proj.result(), dec_proj.result()
    up_grad = jnp.stack([enc_up.result(), dec_up.result()])
    down_grad = jnp.stack([enc_down.result(), dec_down.result()])
    proj_grad = jnp.stack([enc_att[:, :local], dec_att[:, :local]])
    qkv_grad = jnp.stack([enc_att[:, local:], dec_att[:, local:]]).reshape(2, -1, 3, local)

    return (
        results[0][None],
        results[1][None],
        d_tokens[0][None],
        d_tokens[1][None],
        d_cond[:1],
        d_cond[1:],
        grad_ada,
        grad_ada_bias,
        qkv_grad,
        qv_out,
        jnp.transpose(proj_grad, (0, 2, 1)),
        proj_out,
        up_grad,
        up_out,
        jnp.transpose(down_grad, (0, 2, 1)),
        down_out,
        mask_out,
    )


def solution(mesh):
    in_specs = (
        P("dp", None, None),
        P("dp", None, None),
        P("dp", None),
        P("dp", None),
        P("dp", None),
        P("dp", None),
        P(None, None, "dp"),
        P(None, "dp"),
        P(None, None, None, "tensor"),
        P(None, None, "tensor"),
        P(None, "tensor", None),
        P(),
        P(None, None, "tensor"),
        P(None, "tensor"),
        P(None, "tensor", None),
        P(),
        P(),
        P("dp", None, None),
        P("dp", None, None),
    )
    out_specs = (
        P("dp", None, None),
        P("dp", None, None),
        P("dp", None, None),
        P("dp", None, None),
        P("dp", None),
        P("dp", None),
        P(None, None, "dp"),
        P(None, "dp"),
        P(None, "dp", None, "tensor"),
        P(None, None, "tensor"),
        P(None, "tensor", "dp"),
        P(),
        P(None, "dp", "tensor"),
        P(None, "tensor"),
        P(None, "tensor", "dp"),
        P(),
        P(),
    )

    def step(*arguments):
        return on_device(mesh.shape["dp"], mesh.shape["tensor"], *arguments)

    return jax.shard_map(
        step, mesh=mesh, in_specs=in_specs, out_specs=out_specs, check_vma=False
    )
```

```python
import math

import jax
import jax.numpy as jnp
from jax import lax
from jax.experimental import pallas as pl
from jax.experimental.pallas import tpu as pltpu
from jax.sharding import PartitionSpec as P

HEAD_DIM = 72
EPSILON = 1e-06
BF16 = jnp.bfloat16
F32 = jnp.float32
MIB = 1 << 20
SCALING = HEAD_DIM**-0.5
EXPONENT = SCALING * math.log2(math.e)
GELU_A = math.sqrt(2.0 / math.pi)
GELU_B = 0.044715

SHIFT_ATTN, SCALE_ATTN, GATE_ATTN, SHIFT_MLP, SCALE_MLP, GATE_MLP = range(6)
PROJ_BIAS, DOWN_BIAS, UP_BIAS, QKV_BIAS = 0, 2, 4, 6


def nn(left, right):
    return lax.dot_general(left, right, (((1,), (0,)), ((), ())), preferred_element_type=F32)


def nt(left, right):
    return lax.dot_general(left, right, (((1,), (1,)), ((), ())), preferred_element_type=F32)


def tn(left, right):
    return lax.dot_general(left, right, (((0,), (0,)), ((), ())), preferred_element_type=F32)


def shaped(shape, dtype=BF16):
    return jax.ShapeDtypeStruct(shape, dtype)


COSTS = {
    "gather_rows": 0.8, "ln_open": 0.4, "near_sum": 0.4, "merge_attn": 0.6, "merge_mlp": 0.6,
    "finish": 1.0, "first_grad": 0.5, "qkv_forward": 1.2, "qkv_backward": 1.2, "mlp_forward": 3.5,
    "mlp_backward": 3.0, "ln_back": 1.2, "attn_forward": 4.0, "attn_backward": 9.0,
    "weight_grads": 6.5, "halve": 1.5, "place_rows": 3.0, "table_rows": 1.0,
}


class Queue:
    def __init__(self):
        self.token = jnp.zeros((8, 128), F32)

    def tie(self, *values):
        *values, self.token = lax.optimization_barrier((*values, self.token))
        return values[0] if len(values) == 1 else tuple(values)

    def call(
        self, body, operands, outs, name, scalars=(), far=(), far_outs=(), scratch=(), copies=0, limit=10
    ):
        fast = pl.BlockSpec(memory_space=pltpu.VMEM)
        small = pl.BlockSpec(memory_space=pltpu.SMEM)
        slow = pl.BlockSpec(memory_space=pltpu.HBM)
        last = len(scalars) + len(far) + len(operands) + len(outs) + len(far_outs)

        def whole(token_ref, *refs):
            body(*refs[:last], *refs[last + 1 :])
            refs[last][...] = token_ref[...]

        *results, self.token = pl.pallas_call(
            whole,
            in_specs=[fast] + [small] * len(scalars) + [slow] * len(far) + [fast] * len(operands),
            out_specs=[fast] * len(outs) + [slow] * len(far_outs) + [fast],
            out_shape=[
                *outs,
                *[pltpu.HBM(out.shape, out.dtype) for out in far_outs],
                shaped((8, 128), F32),
            ],
            scratch_shapes=list(scratch)
            + ([pltpu.SemaphoreType.DMA((copies,))] if copies else []),
            cost_estimate=pl.CostEstimate(
                flops=int(COSTS.get(name, 1.0) * 1e9), transcendentals=0, bytes_accessed=1000
            ),
            compiler_params=pltpu.CompilerParams(vmem_limit_bytes=limit * MIB),
            name=name,
        )(
            pltpu.with_memory_space_constraint(self.token, pltpu.VMEM),
            *scalars,
            *[pltpu.with_memory_space_constraint(value, pltpu.HBM) for value in far],
            *[pltpu.with_memory_space_constraint(value, pltpu.VMEM) for value in operands],
        )
        return results


def copy_rows(sources, target, semaphores, first=0):
    found, row = [], 0
    for index, source in enumerate(sources):
        count = source.shape[0]
        copy = pltpu.make_async_copy(
            source, target.at[pl.ds(row, count)], semaphores.at[first + index]
        )
        copy.start()
        found.append(copy)
        row += count
    return found


def normed_of(values):
    center = values - jnp.mean(values, axis=-1, keepdims=True)
    spread = jnp.mean(center * center, axis=-1, keepdims=True)
    scale = lax.rsqrt(spread + EPSILON)
    return center * scale, scale


def modulate(values, mods_ref, at, scale_part, shift_part):
    block, latent = at
    scale = mods_ref[block, latent, scale_part : scale_part + 1, :]
    shift = mods_ref[block, latent, shift_part : shift_part + 1, :]
    return (normed_of(values)[0] * (1.0 + scale) + shift).astype(BF16)


def branch_of(near_ref, far_ref, small_ref, row, features):
    return (
        near_ref[...].astype(F32)
        + far_ref[...].astype(F32)
        + small_ref[row : row + 1, :features]
    )


class Rows:
    def __init__(self, *spans):
        self.spans = spans
        self.count = sum(span[2] for span in spans)

    def places(self, perm_ref, core, other=False):
        found = []
        for first, stride, count in self.spans:
            low = perm_ref[:, first : first + count]
            high = perm_ref[:, first + stride : first + stride + count]
            found.append(jnp.where((core == 1) != other, high, low))
        return found[0] if len(found) == 1 else jnp.concatenate(found, axis=1)


def pick_columns(places, length):
    index = lax.broadcasted_iota(jnp.int32, (length, places.shape[1]), 0)
    return (index == places).astype(F32).astype(BF16)


def gather_rows(queue, core, perm, source, rows, dtype):
    length, features = source.shape

    def body(core_ref, perm_ref, source_ref, out_ref):
        pick = pick_columns(rows.places(perm_ref, core_ref[0]), length)
        out_ref[...] = tn(pick, source_ref[...]).astype(dtype)

    outs = [shaped((rows.count, features), dtype)]
    return queue.call(body, [perm, source], outs, "gather_rows", scalars=[core])[0]


def place_rows(queue, core, perm, own, other, rows, first):
    length = perm.shape[1]
    features = own.shape[1]
    last = first + sum(chunk.count for chunk in rows)

    def body(core_ref, perm_ref, own_ref, other_ref, out_ref):
        places = [
            chunk.places(perm_ref, core_ref[0], other) for other in (False, True) for chunk in rows
        ]
        values = jnp.concatenate([own_ref[first:last, :], other_ref[first:last, :]], axis=0)
        pick = pick_columns(jnp.concatenate(places, axis=1), length)
        out_ref[...] = nn(pick, values).astype(BF16)

    outs = [shaped((length, features))]
    return queue.call(
        body, [perm, own, other], outs, "place_rows", scalars=[core], limit=12
    )[0]


def table_rows(queue, core, perm, waves, rows, filler=None):
    side, half = waves.shape

    def body(core_ref, perm_ref, waves_ref, *refs):
        places = rows.places(perm_ref, core_ref[0])
        index = lax.broadcasted_iota(jnp.int32, (side, places.shape[1]), 0)
        row_pick = ((places >= index * side) & (places < (index + 1) * side)).astype(F32)
        row = jnp.sum(row_pick * index.astype(F32), axis=0, keepdims=True)
        col_pick = (index.astype(F32) == places.astype(F32) - row * side).astype(F32)
        for low, pick in ((0, row_pick), (half, col_pick)):
            out = lax.dot_general(
                pick,
                waves_ref[...],
                (((0,), (0,)), ((), ())),
                precision=lax.Precision.HIGHEST,
                preferred_element_type=F32,
            )
            if filler is not None:
                out = out + refs[0][:, low : low + half]
            refs[-1][:, low : low + half] = out

    operands = [perm, waves] + ([] if filler is None else [filler])
    outs = [shaped((rows.count, 2 * half), F32)]
    return queue.call(body, operands, outs, "table_rows", scalars=[core])[0]


def ln_open(queue, stream, mods, at):
    def body(x_ref, mods_ref, out_ref):
        out_ref[...] = modulate(x_ref[...], mods_ref, at, SCALE_ATTN, SHIFT_ATTN)

    return queue.call(body, [stream, mods], [shaped(stream.shape)], "ln_open")[0]


def near_sum(queue, own, moved):
    def body(own_ref, moved_ref, out_ref):
        out_ref[...] = (own_ref[...].astype(F32) + moved_ref[...].astype(F32)).astype(BF16)

    return queue.call(body, [own, moved], [shaped(own.shape)], "near_sum")[0]


def merge_attn(queue, stream, near, far, small, mods, at):
    features = stream.shape[1]
    block, latent = at

    def body(x_ref, near_ref, far_ref, small_ref, mods_ref, mid_ref, out_ref):
        branch = branch_of(near_ref, far_ref, small_ref, PROJ_BIAS + block, features)
        middle = x_ref[...] + mods_ref[block, latent, GATE_ATTN : GATE_ATTN + 1, :] * branch
        mid_ref[...] = middle
        out_ref[...] = modulate(middle, mods_ref, at, SCALE_MLP, SHIFT_MLP)

    outs = [shaped(stream.shape, F32), shaped(stream.shape)]
    return queue.call(body, [stream, near, far, small, mods], outs, "merge_attn")


def merge_mlp(queue, pieces, small, mods, at, table, tail):
    features = table.shape[1]
    counts = [piece[0].shape[0] for piece in pieces]
    block, latent = at
    total = sum(counts) + (0 if tail is None else tail.shape[0])
    following = (block + 1, latent)

    def body(table_ref, small_ref, mods_ref, *refs):
        x_ref, out_ref = refs[-2:]
        gate = mods_ref[block, latent, GATE_MLP : GATE_MLP + 1, :]
        first = 0
        for index, count in enumerate(counts):
            mid_ref, near_ref, far_ref = refs[3 * index : 3 * index + 3]
            branch = branch_of(near_ref, far_ref, small_ref, DOWN_BIAS + block, features)
            stream = mid_ref[...] + gate * branch + table_ref[first : first + count, :]
            x_ref[first : first + count, :] = stream
            out_ref[first : first + count, :] = modulate(
                stream, mods_ref, following, SCALE_ATTN, SHIFT_ATTN
            )
            first += count
        if tail is not None:
            stream = refs[3 * len(counts)][...]
            x_ref[first:, :] = stream
            out_ref[first:, :] = modulate(stream, mods_ref, following, SCALE_ATTN, SHIFT_ATTN)

    operands = [table, small, mods] + [part for piece in pieces for part in piece]
    operands += [] if tail is None else [tail]
    outs = [shaped((total, features), F32), shaped((total, features))]
    return queue.call(body, operands, outs, "merge_mlp")


def finish(queue, parts, small, mods):
    counts = [part[0].shape[0] for part in parts]
    features = parts[0][0].shape[1]

    def body(small_ref, mods_ref, *refs):
        out_ref, sums_ref = refs[-2:]
        sums_ref[...] = jnp.zeros_like(sums_ref)
        first = 0
        for index, count in enumerate(counts):
            mid_ref, near_ref, far_ref, d_ref = refs[4 * index : 4 * index + 4]
            block, latent = parts[index][4]
            branch = branch_of(near_ref, far_ref, small_ref, DOWN_BIAS + block, features)
            gate = mods_ref[block, latent, GATE_MLP : GATE_MLP + 1, :]
            out_ref[first : first + count, :] = (mid_ref[...] + gate * branch).astype(BF16)
            total = jnp.sum(d_ref[...].astype(F32) * branch, axis=0, keepdims=True)
            sums_ref[latent : latent + 1, :] += total
            first += count

    outs = [shaped((sum(counts), features)), shaped((8, features), F32)]
    operands = [small, mods] + [value for part in parts for value in part[:4]]
    return queue.call(body, operands, outs, "finish")


def first_grad(queue, d_out, mods, at):
    features = d_out.shape[1]
    block, latent = at

    def body(d_ref, mods_ref, out_ref, sums_ref):
        gate = mods_ref[block, latent, GATE_MLP : GATE_MLP + 1, :]
        grad = (gate * d_ref[...].astype(F32)).astype(BF16)
        out_ref[...] = grad
        total = jnp.sum(grad.astype(F32), axis=0, keepdims=True)
        sums_ref[...] = jnp.broadcast_to(total, (8, features))

    outs = [shaped(d_out.shape), shaped((8, features), F32)]
    return queue.call(body, [d_out, mods], outs, "first_grad")


def qkv_forward(queue, own, other, weight, small, block):
    rows, features = own.shape
    width = weight.shape[1]

    def body(own_ref, other_ref, w_ref, small_ref, out_ref, rows_ref, done):
        copies = copy_rows([own_ref, other_ref], rows_ref, done)
        bias = small_ref[QKV_BIAS + block : QKV_BIAS + block + 1, :width]
        both = jnp.concatenate([own_ref[...], other_ref[...]], axis=0)
        out = (nt(both, w_ref[block]) + bias).astype(BF16)
        out_ref[0] = out[:rows]
        out_ref[1] = out[rows:]
        for copy in copies:
            copy.wait()

    return queue.call(
        body,
        [own, other, weight, small],
        [shaped((2, rows, width))],
        "qkv_forward",
        far_outs=[shaped((2 * rows, features))],
        copies=2,
    )


def qkv_backward(queue, grads, weight, block):
    _, rows, _ = grads.shape
    features = weight.shape[2]

    def body(g_ref, w_ref, own_ref, other_ref):
        both = jnp.concatenate([g_ref[0], g_ref[1]], axis=0)
        out = nn(both, w_ref[block]).astype(BF16)
        own_ref[...] = out[:rows]
        other_ref[...] = out[rows:]

    outs = [shaped((rows, features)), shaped((rows, features))]
    return queue.call(body, [grads, weight], outs, "qkv_backward")


def mlp_forward(queue, own, other, up_weight, down_weight, small, block):
    rows, features = own.shape
    wide = up_weight.shape[2]

    def body(
        own_ref, other_ref, up_ref, down_ref, small_ref,
        own_out, other_out, slope_ref, rows_ref, act_ref, act_s, done,
    ):
        copies = copy_rows([own_ref, other_ref], rows_ref, done)
        bias = small_ref[UP_BIAS + block : UP_BIAS + block + 1, :wide]
        both = jnp.concatenate([own_ref[...], other_ref[...]], axis=0)
        hidden = nn(both, up_ref[block]) + bias
        squared = hidden * hidden
        bent = jnp.tanh(GELU_A * hidden * (1.0 + GELU_B * squared))
        half = 0.5 + 0.5 * bent
        act_s[...] = (hidden * half).astype(BF16)
        slope = half + 0.5 * hidden * (1.0 - bent * bent) * (
            GELU_A + 3.0 * GELU_A * GELU_B * squared
        )
        slope_ref[...] = slope.astype(BF16)
        copies += copy_rows([act_s], act_ref, done, 2)
        out = nn(act_s[...], down_ref[block]).astype(BF16)
        own_out[...] = out[:rows]
        other_out[...] = out[rows:]
        for copy in copies:
            copy.wait()

    full = shaped((2 * rows, wide))
    return queue.call(
        body,
        [own, other, up_weight, down_weight, small],
        [shaped((rows, features)), shaped((rows, features)), full],
        "mlp_forward",
        far_outs=[shaped((2 * rows, features)), full],
        scratch=[pltpu.VMEM((2 * rows, wide), BF16)],
        copies=3,
        limit=12,
    )


def mlp_backward(queue, own, other, slope, up_weight, down_weight, block):
    rows, features = own.shape
    wide = up_weight.shape[2]

    def body(
        own_ref, other_ref, slope_ref, up_ref, down_ref,
        own_out, other_out, rows_ref, hid_ref, hid_s, done,
    ):
        copies = copy_rows([own_ref, other_ref], rows_ref, done)
        both = jnp.concatenate([own_ref[...], other_ref[...]], axis=0)
        d_active = nt(both, down_ref[block])
        hid_s[...] = (d_active * slope_ref[...].astype(F32)).astype(BF16)
        copies += copy_rows([hid_s], hid_ref, done, 2)
        out = nt(hid_s[...], up_ref[block]).astype(BF16)
        own_out[...] = out[:rows]
        other_out[...] = out[rows:]
        for copy in copies:
            copy.wait()

    return queue.call(
        body,
        [own, other, slope, up_weight, down_weight],
        [shaped((rows, features)), shaped((rows, features))],
        "mlp_backward",
        far_outs=[shaped((2 * rows, features)), shaped((2 * rows, wide))],
        scratch=[pltpu.VMEM((2 * rows, wide), BF16)],
        copies=3,
        limit=12,
    )


def ln_back(queue, near, far, stream, d_out, mods, at, scale_part, branch=None, narrow=False):
    rows, features = stream.shape
    pieces = [] if branch is None else branch[0]
    counts = [piece[0].shape[0] for piece in pieces]
    inner = sum(counts)
    operands = [near, far, stream, d_out, mods]
    outs = [shaped((8, features), F32)]
    if narrow:
        outs.append(shaped((rows, features)))
    if pieces:
        _, small, bias_row, gate_at, gate_part = branch
        operands += [small] + [half for piece in pieces for half in piece]
        outs += [shaped((count, features), F32) for count in counts]
        outs += [shaped((count, features)) for count in counts]
    inputs = len(operands)

    def body(*refs):
        near_ref, far_ref, x_ref, d_ref, mods_ref = refs[:5]
        sums_ref, *out_refs = refs[inputs:]
        scale = mods_ref[at[0], at[1], scale_part : scale_part + 1, :]
        d_normed = near_ref[...].astype(F32) + far_ref[...].astype(F32)
        normed, spread = normed_of(x_ref[...])
        product = d_normed * normed
        grad = d_normed * (1.0 + scale)
        d_x = d_ref[...].astype(F32) + spread * (
            grad
            - jnp.mean(grad, axis=-1, keepdims=True)
            - normed * jnp.mean(grad * normed, axis=-1, keepdims=True)
        )
        zero = jnp.zeros((1, features), F32)
        gate_sum, bias_sum, rest_sum = zero, zero, zero
        if narrow:
            out_refs[0][...] = d_x.astype(BF16)
        elif inner < rows:
            rest_sum = jnp.sum(d_x[inner:], axis=0, keepdims=True)
        first = 0
        for index, count in enumerate(counts):
            piece_near, piece_far = refs[6 + 2 * index : 8 + 2 * index]
            value = branch_of(piece_near, piece_far, refs[5], bias_row, features)
            part = d_x[first : first + count]
            gate = mods_ref[gate_at[0], gate_at[1], gate_part : gate_part + 1, :]
            d_branch = (gate * part).astype(BF16)
            out_refs[index][...] = part
            out_refs[len(counts) + index][...] = d_branch
            gate_sum = gate_sum + jnp.sum(part * value, axis=0, keepdims=True)
            bias_sum = bias_sum + jnp.sum(d_branch.astype(F32), axis=0, keepdims=True)
            first += count
        sums_ref[...] = jnp.concatenate(
            [
                jnp.sum(product, axis=0, keepdims=True),
                jnp.sum(d_normed, axis=0, keepdims=True),
                gate_sum,
                bias_sum,
                rest_sum,
                jnp.zeros((3, features), F32),
            ],
            axis=0,
        )

    return queue.call(body, operands, outs, "ln_back")


def attn_forward(queue, query, merged, proj_weight, block):
    _, rows, width = query.shape
    local = width // 3
    heads = local // HEAD_DIM
    counts = [part.shape[1] for part in merged]
    total = 2 * sum(counts)
    features = proj_weight.shape[2]
    by_keys = rows < 128

    def body(*refs):
        q_ref, refs = refs[0], refs[1:]
        kv_refs, refs = refs[: len(merged)], refs[len(merged) :]
        proj_ref, lse_ref, own_out, other_out, att_far, q_s, k_s, v_s, o_s, l_s, att_ref, done = refs
        for head in range(heads):
            low = head * HEAD_DIM
            first = 0
            for part, count in zip(kv_refs, counts):
                for side in range(2):
                    at = pl.ds(first, count)
                    k_s[head, at, :] = part[side, :, local + low : local + low + HEAD_DIM]
                    v_s[head, at, :] = part[side, :, 2 * local + low : 2 * local + low + HEAD_DIM]
                    first += count
            for side in range(2):
                q_s[head, side] = q_ref[side, :, low : low + HEAD_DIM]
        for head in range(heads):
            for side in range(2):
                if by_keys:
                    scores = nt(k_s[head], q_s[head, side])
                    highest = jnp.max(scores, axis=0, keepdims=True)
                    raised = jnp.exp2((scores - highest) * EXPONENT)
                    total_row = jnp.sum(raised, axis=0, keepdims=True)
                    out = tn(v_s[head], raised.astype(BF16))
                    o_s[head, side] = (out / total_row).T.astype(BF16)
                    lse_ref[head, side] = highest * EXPONENT + jnp.log2(total_row)
                else:
                    scores = nt(q_s[head, side], k_s[head])
                    highest = jnp.max(scores, axis=1, keepdims=True)
                    raised = jnp.exp2((scores - highest) * EXPONENT)
                    total_row = jnp.sum(raised, axis=1, keepdims=True)
                    out = nn(raised.astype(BF16), v_s[head])
                    o_s[head, side] = (out / total_row).astype(BF16)
                    l_s[head, side] = jnp.broadcast_to(
                        highest * EXPONENT + jnp.log2(total_row), (rows, 128)
                    )
        if not by_keys:
            for head in range(heads):
                for side in range(2):
                    lse_ref[head, side] = l_s[head, side].T[:1]
        for side, out_ref in ((1, other_out), (0, own_out)):
            for head in range(heads):
                low = head * HEAD_DIM
                att_ref[side * rows : (side + 1) * rows, low : low + HEAD_DIM] = o_s[head, side]
            out_ref[...] = nn(
                att_ref[side * rows : (side + 1) * rows, :], proj_ref[block]
            ).astype(BF16)
        for copy in copy_rows([att_ref], att_far, done):
            copy.wait()

    return queue.call(
        body,
        [query, *merged, proj_weight],
        [
            shaped((heads, 2, 1, rows), F32),
            shaped((rows, features)),
            shaped((rows, features)),
        ],
        "attn_forward",
        far_outs=[shaped((2 * rows, local))],
        scratch=[
            pltpu.VMEM((heads, 2, rows, HEAD_DIM), BF16),
            pltpu.VMEM((heads, total, HEAD_DIM), BF16),
            pltpu.VMEM((heads, total, HEAD_DIM), BF16),
            pltpu.VMEM((heads, 2, rows, HEAD_DIM), BF16),
            pltpu.VMEM((heads, 2, 8 if by_keys else rows, 128), F32),
            pltpu.VMEM((2 * rows, local), BF16),
        ],
        copies=1,
        limit=13,
    )


def attn_backward(queue, merged, normers, grads, proj_weight, block):
    count = len(merged)
    width = merged[0].shape[2]
    local = width // 3
    heads = local // HEAD_DIM
    halves = [part.shape[1] for part in merged]
    total = 2 * sum(halves)
    features = proj_weight.shape[2]
    step = min(halves)
    steps = total // step
    unroll = 4 if step * steps > 512 else steps * heads

    def body(*refs):
        m_refs, refs = refs[:count], refs[count:]
        l_refs, refs = refs[:count], refs[count:]
        g_refs, refs = refs[: 2 * count], refs[2 * count :]
        proj_ref, refs = refs[0], refs[1:]
        out_refs, refs = refs[:count], refs[count:]
        row_refs, refs = refs[:count], refs[count:]
        qkv_refs, refs = refs[:count], refs[count:]
        q_s, k_s, kt_s, v_s, g_s, dq_s, dk_s, dv_s, l_s, done = refs
        copies = []
        for index in range(count):
            copies += copy_rows(
                g_refs[2 * index : 2 * index + 2], row_refs[index], done, 2 * index
            )
        first = 0
        for index in range(count):
            rows = halves[index]
            for side in range(2):
                at = pl.ds(first, rows)
                grad = nt(g_refs[2 * index + side][...], proj_ref[block]).astype(BF16)
                for head in range(heads):
                    low = head * HEAD_DIM
                    part = m_refs[index]
                    q_s[head, at, :] = part[side, :, low : low + HEAD_DIM]
                    keys = part[side, :, local + low : local + low + HEAD_DIM]
                    k_s[head, at, :] = keys
                    kt_s[head, :, at] = keys.T
                    v_s[head, at, :] = part[side, :, 2 * local + low : 2 * local + low + HEAD_DIM]
                    g_s[head, at, :] = grad[:, low : low + HEAD_DIM]
                    for piece in range(rows // step):
                        l_s[head, first // step + piece] = l_refs[index][
                            head, side, :, piece * step : (piece + 1) * step
                        ]
                first += rows
        dk_s[...] = jnp.zeros_like(dk_s)
        dv_s[...] = jnp.zeros_like(dv_s)

        def one(index, carry):
            head, piece = index // steps, lax.rem(index, steps)
            at = pl.ds(pl.multiple_of(piece * step, step), step)
            queries, grad = q_s[head, at, :], g_s[head, at, :]
            probs = jnp.exp2(nt(k_s[head], queries) * EXPONENT - l_s[head, piece])
            product = probs * nt(v_s[head], grad)
            delta = jnp.sum(product, axis=0, keepdims=True)
            d_scores = (product - probs * delta).astype(BF16)
            dv_s[head] += nn(probs.astype(BF16), grad)
            dk_s[head] += nn(d_scores, queries)
            dq_s[head, at, :] = (nn(kt_s[head], d_scores) * SCALING).T.astype(BF16)
            return carry

        lax.fori_loop(0, steps * heads, one, 0, unroll=unroll)
        first = 0
        for index in range(count):
            rows = halves[index]
            for side in range(2):
                at = pl.ds(first, rows)
                out = out_refs[index]
                for head in range(heads):
                    low = head * HEAD_DIM
                    out[side, :, low : low + HEAD_DIM] = dq_s[head, at, :]
                    out[side, :, local + low : local + low + HEAD_DIM] = (
                        dk_s[head, at, :] * SCALING
                    ).astype(BF16)
                    out[side, :, 2 * local + low : 2 * local + low + HEAD_DIM] = dv_s[
                        head, at, :
                    ].astype(BF16)
                first += rows
            copies += copy_rows(
                [out_refs[index].at[0], out_refs[index].at[1]],
                qkv_refs[index],
                done,
                2 * count + 2 * index,
            )
        for copy in copies:
            copy.wait()

    def lanes(dtype=BF16):
        return pltpu.VMEM((heads, total, HEAD_DIM), dtype)

    return queue.call(
        body,
        [*merged, *normers, *[half for pair in grads for half in pair], proj_weight],
        [shaped(part.shape) for part in merged],
        "attn_backward",
        far_outs=[shaped((2 * rows, features)) for rows in halves]
        + [shaped((2 * rows, width)) for rows in halves],
        copies=4 * count,
        scratch=[
            lanes(),
            lanes(),
            pltpu.VMEM((heads, HEAD_DIM, total), BF16),
            lanes(),
            lanes(),
            lanes(),
            lanes(F32),
            lanes(F32),
            pltpu.VMEM((heads, steps, 1, step), F32),
        ],
        limit=16,
    )


def split_at(bits, bit):
    place = len(bits) - 1 - bits.index(bit)
    stride = 1 << place
    return [index for index in range(1 << len(bits)) if not index & stride], stride


def weight_grads(queue, pairs, bits, cuts):
    blocks = 1 << len(bits)
    features = pairs[0][0][0].shape[1]
    widths = [rights[0].shape[1] for _, rights in pairs]
    each = features // blocks
    rows = sum(part.shape[0] for part in pairs[0][0])
    far, plan, scratch = [], [], []
    for number, (lefts, rights) in enumerate(pairs):
        for place, parts in enumerate((lefts, rights)):
            first = 0
            for part in parts:
                plan.append((len(far), 2 * number + place, first, part.shape[0]))
                far.append(part)
                first += part.shape[0]
            scratch.append(pltpu.VMEM((rows, parts[0].shape[1]), BF16))
    buffers = len(scratch)
    scratch.append(pltpu.VMEM((blocks, each, sum(widths)), BF16))
    outs, far_outs = [], []
    for columns, _, _ in cuts:
        outs += [shaped((blocks // 2, each, columns))] * 2
    if not cuts:
        far_outs.append(shaped((blocks, each, sum(widths))))

    def body(*refs):
        mine_refs, refs = refs[: len(cuts)], refs[len(cuts) :]
        sources, refs = refs[: len(far)], refs[len(far) :]
        out_refs, refs = refs[: len(outs)], refs[len(outs) :]
        sums_ref, *held = refs
        whole_ref = None if cuts else held.pop(0)
        full, done = held[buffers], held[buffers + 1]
        copies = [
            pltpu.make_async_copy(
                sources[source], held[buffer].at[pl.ds(first, count)], done.at[index]
            )
            for index, (source, buffer, first, count) in enumerate(plan)
        ]
        for copy in copies:
            copy.start()
        low = 0
        ones = jnp.ones((8, rows), BF16)
        for number, width in enumerate(widths):
            for copy, (_, buffer, _, _) in zip(copies, plan):
                if buffer // 2 == number:
                    copy.wait()
            left, right = held[2 * number][...], held[2 * number + 1][...]
            total = tn(left, right).astype(BF16)
            columns = slice(low, low + width)
            for block in range(blocks):
                full[block, :, columns] = total[block * each : (block + 1) * each]
            sums_ref[:, columns] = nn(ones, right)
            low += width
        low = 0
        for index, (width, bit, _) in enumerate(cuts):
            starts, stride = split_at(bits, bit)
            at = mine_refs[index][0] * stride
            for place, start in enumerate(starts):
                out_refs[2 * index][place] = full[start + at, :, low : low + width]
                out_refs[2 * index + 1][place] = full[start + stride - at, :, low : low + width]
            low += width
        if not cuts:
            whole = pltpu.make_async_copy(full, whole_ref, done.at[len(plan)])
            whole.start()
            whole.wait()

    found = queue.call(
        body,
        [],
        [*outs, shaped((8, sum(widths)), F32)],
        "weight_grads",
        scalars=[mine for _, _, mine in cuts],
        far=far,
        far_outs=far_outs,
        scratch=scratch,
        copies=len(plan) + 1,
        limit=20 if len(pairs) == 1 else 28,
    )
    if not cuts:
        return found[1], found[0]
    return list(zip(found[:-1:2], found[1:-1:2])), found[-1]


def halve(queue, kept, moved, mine, bits, bit):
    blocks, each, width = kept.shape
    out = shaped((blocks // 2, each, width))
    starts, stride = split_at(bits, bit)

    def body(mine_ref, kept_ref, moved_ref, next_ref, away_ref):
        at = mine_ref[0] * stride
        for place, out_ref in ((stride - at, away_ref), (at, next_ref)):
            for index, start in enumerate(starts):
                total = kept_ref[start + place].astype(F32) + moved_ref[start + place].astype(F32)
                out_ref[index] = total.astype(BF16)

    return queue.call(body, [kept, moved], [out, out], "halve", scalars=[mine])


def spread_mods(queue, me, columns, features):
    size, latents, blocks, each = columns.shape

    def body(me_ref, in_ref, out_ref, flat):
        for device in range(size):
            block = in_ref[jnp.bitwise_xor(device, me_ref[0])].astype(F32)
            for latent in range(latents):
                flat[latent, :, device * each : (device + 1) * each] = block[latent]
        for latent in range(latents):
            for part in range(6):
                rows = flat[latent, :, part * features : (part + 1) * features]
                for index in range(blocks):
                    out_ref[index, latent, part : part + 1, :] = rows[index : index + 1]

    return queue.call(
        body,
        [columns],
        [shaped((blocks, latents, 6, features), F32)],
        "spread_mods",
        scalars=[me],
        scratch=[pltpu.VMEM((latents, blocks, size * each), F32)],
    )[0]


def collect_sums(queue, sources, recipe, parts):
    features = sources[0].shape[1]
    count = -(-len(recipe) // 8) * 8
    counts = [part.shape[0] for part in parts]

    def body(*refs):
        part_refs, refs = refs[: len(parts)], refs[len(parts) :]
        out_ref, joined_ref = refs[-2:]
        for index, terms in enumerate(recipe):
            total = None
            for source, row in terms:
                term = refs[source][row : row + 1, :]
                total = term if total is None else total + term
            out_ref[index : index + 1, :] = total
        if count > len(recipe):
            out_ref[len(recipe) :, :] = jnp.zeros((count - len(recipe), features), F32)
        first = 0
        for part_ref, rows in zip(part_refs, counts):
            joined_ref[first : first + rows, :] = part_ref[...]
            first += rows

    outs = [shaped((count, features), F32), shaped((sum(counts), features))]
    return queue.call(body, [*parts, *sources], outs, "collect_sums")


def pack_mods(queue, me, own, moved, latents, blocks, size, features):
    each = 6 * features // size
    rows = own.shape[0]

    def body(me_ref, own_ref, moved_ref, out_ref, total_ref, flat):
        total = own_ref[...] + moved_ref[...]
        total_ref[...] = total
        for latent in range(latents):
            for index in range(blocks):
                for part in range(6):
                    row = (index * latents + latent) * 6 + part
                    flat[latent, index : index + 1, part * features : (part + 1) * features] = total[
                        row : row + 1
                    ]
        for device in range(size):
            for latent in range(latents):
                out_ref[jnp.bitwise_xor(device, me_ref[0]), latent] = flat[
                    latent, :, device * each : (device + 1) * each
                ].astype(BF16)

    return queue.call(
        body,
        [own, moved],
        [shaped((size, latents, blocks, each)), shaped((rows, features), F32)],
        "pack_mods",
        scalars=[me],
        scratch=[pltpu.VMEM((latents, blocks, 6 * features), F32)],
    )


def partners(size, bit):
    return [(index, index ^ bit) for index in range(size)]


def bits_of(size):
    bits = []
    while (1 << len(bits)) < size:
        bits.append(1 << len(bits))
    assert (1 << len(bits)) == size
    return bits


class Links:
    def __init__(self, dp_size, tensor_size):
        self.dp_size = dp_size
        self.tensor_size = tensor_size
        self.dp_bits = bits_of(dp_size)
        me = lax.axis_index("dp")
        self.me = me.reshape(1)
        self.core = lax.rem(lax.axis_index("tensor"), 2).reshape(1)
        self.mine = {bit: lax.rem(me // bit, 2).reshape(1) for bit in self.dp_bits}

    def swap(self, value):
        return lax.ppermute(value, "tensor", partners(self.tensor_size, 1))

    def cross(self, value):
        return lax.ppermute(value, "tensor", partners(self.tensor_size, 2))

    def dp_move(self, value, bit):
        return lax.ppermute(value, "dp", partners(self.dp_size, bit))

    def gather_relative(self, value):
        held = value[None]
        for bit in self.dp_bits:
            held = jnp.concatenate([held, self.dp_move(held, bit)], axis=0)
        return held

    def exchange_relative(self, value, total=None):
        held = value
        for bit in reversed(self.dp_bits):
            split = held.reshape((self.dp_size // (2 * bit), 2, bit) + held.shape[1:])
            away = split[:, 1]
            if total is None:
                moved = self.dp_move(away, bit)
            else:
                sent = jnp.concatenate([away.astype(F32).reshape(-1), total])
                came = self.dp_move(sent, bit)
                moved = came[: away.size].reshape(away.shape).astype(held.dtype)
                total = total + came[away.size :]
            held = jnp.stack([split[:, 0], moved], axis=1).reshape(held.shape)
        return held if total is None else (held, total)

    def sum_relative(self, value):
        held = value
        for bit in reversed(self.dp_bits):
            moved = self.dp_move(held[bit:].astype(BF16), bit)
            held = held[:bit].astype(F32) + moved.astype(F32)
        return held[0]


class ScatterSum:
    def __init__(self, queue, links, kept, away, order):
        self.queue, self.links, self.kept = queue, links, kept
        self.order = list(order)
        self.open = sorted(self.order, reverse=True)
        self.send(away)

    def send(self, away):
        bit = self.order.pop(0)
        self.open.remove(bit)
        self.moved = self.links.dp_move(away, bit)

    def step(self):
        if self.order:
            bit = self.order[0]
            self.kept, away = halve(
                self.queue, self.kept, self.moved, self.links.mine[bit], self.open, bit
            )
            self.send(away)

    def result(self):
        while self.order:
            self.step()
        return self.kept[0].astype(F32) + self.moved[0].astype(F32)


def reduced(queue, links, pairs, after=None):
    whole, sums = weight_grads(queue, pairs, sorted(links.dp_bits, reverse=True), [])
    flat = whole.reshape(-1, whole.shape[-1])
    if after is not None:
        flat, after = lax.optimization_barrier((flat, after))
    return lax.psum_scatter(flat, "dp", scatter_dimension=0, tiled=True), sums, after


def scatter_sums(queue, links, pairs, cuts):
    bits = sorted(links.dp_bits, reverse=True)
    found, sums = weight_grads(
        queue, pairs, bits, [(columns, order[0], links.mine[order[0]]) for columns, order in cuts]
    )
    pieces = [
        ScatterSum(queue, links, kept, away, order)
        for (kept, away), (_, order) in zip(found, cuts)
    ]
    return pieces, sums


class Weights:
    def __init__(self, qkv, proj, up, down, small, mods):
        self.qkv, self.proj, self.up, self.down = qkv, proj, up, down
        self.small, self.mods = small, mods


class Chunk:
    def __init__(self, queue, links, weights, block, latent, family):
        self.queue, self.links, self.weights = queue, links, weights
        self.block, self.latent, self.at = block, latent, (block, latent)
        self.family = family
        family.append(self)

    def enter(self, stream, normed):
        self.x = stream
        self.normed_attn = (normed, self.links.swap(normed))

    def qkv(self):
        w = self.weights
        self.merged, self.normed_attn_rows = qkv_forward(
            self.queue, *self.normed_attn, w.qkv, w.small, self.block
        )

    def attention(self):
        merged = [chunk.merged for chunk in self.family]
        self.normer, own, other, self.attended_rows = attn_forward(
            self.queue, self.merged, merged, self.weights.proj, self.block
        )
        self.part = (own, self.links.swap(other))

    def near(self):
        near = near_sum(self.queue, *self.part)
        self.sum = (near, self.links.cross(near))

    def merge(self):
        w = self.weights
        self.branch_attn = self.sum
        self.middle, normed = merge_attn(
            self.queue, self.x, *self.branch_attn, w.small, w.mods, self.at
        )
        self.normed_mlp = (normed, self.links.swap(normed))

    def mlp(self):
        w = self.weights
        own, other, self.slope, self.normed_mlp_rows, self.active_rows = mlp_forward(
            self.queue, *self.normed_mlp, w.up, w.down, w.small, self.block
        )
        self.part = (own, self.links.swap(other))

    def start_back(self, d_out, d_branch):
        self.d_out = d_out
        self.d_branch_mlp = (d_branch, self.links.swap(d_branch))

    def mlp_back(self):
        w = self.weights
        own, other, self.d_branch_mlp_rows, self.d_hidden_rows = mlp_backward(
            self.queue, *self.d_branch_mlp, self.slope, w.up, w.down, self.block
        )
        self.part = (own, self.links.swap(other))

    def merge_back(self):
        w = self.weights
        branch = ([self.branch_attn], w.small, PROJ_BIAS + self.block, self.at, GATE_ATTN)
        self.mlp_sums, self.d_middle, grad = ln_back(
            self.queue, *self.sum, self.middle, self.d_out, w.mods, self.at, SCALE_MLP, branch
        )
        self.d_branch_attn = (grad, self.links.swap(grad))

    def attention_back(self):
        family = self.family
        grads = attn_backward(
            self.queue,
            [chunk.merged for chunk in family],
            [chunk.normer for chunk in family],
            [chunk.d_branch_attn for chunk in family],
            self.weights.proj,
            self.block,
        )
        count = len(family)
        for index, chunk in enumerate(family):
            chunk.d_qkv, chunk.d_branch_attn_rows, chunk.d_qkv_rows = grads[index::count]

    def qkv_back(self):
        own, other = qkv_backward(self.queue, self.d_qkv, self.weights.qkv, self.block)
        self.part = (own, self.links.swap(other))

    def leave_back(self, branch=None, narrow=False):
        w = self.weights
        self.attn_sums, *rest = ln_back(
            self.queue,
            *self.sum,
            self.x,
            self.d_middle,
            w.mods,
            self.at,
            SCALE_ATTN,
            branch,
            narrow,
        )
        return rest


def rows_of(chunks, name):
    return [getattr(chunk, name + "_rows") for chunk in chunks]


def on_device(dp_size, tensor_size, *arguments):
    (
        tokens_long,
        tokens_short,
        cond_long,
        cond_short,
        perm_long,
        perm_short,
        ada_weight,
        ada_bias,
        qkv_weight,
        qv_bias,
        proj_weight,
        proj_bias,
        up_weight,
        up_bias,
        down_weight,
        down_bias,
        mask_token,
        cot_long,
        cot_short,
    ) = arguments
    assert tokens_long.shape[0] == 1 and tokens_short.shape[0] == 1
    queue = Queue()
    links = Links(dp_size, tensor_size)
    core = links.core
    features = tokens_long.shape[2]
    wide = up_weight.shape[2]
    local = qv_bias.shape[2]
    tokens = (tokens_long[0], tokens_short[0])
    cots = (cot_long[0], cot_short[0])
    perms = (perm_long, perm_short)
    lengths = tuple(rows.shape[0] for rows in tokens)
    kept = tuple(length // 2 for length in lengths)

    cond = jnp.concatenate([cond_long, cond_short]).astype(F32)
    acts = links.gather_relative(jax.nn.silu(cond).astype(BF16))
    flat_acts = acts.reshape(-1, features)
    columns = jnp.einsum("nd,ldm->nlm", flat_acts, ada_weight, preferred_element_type=F32)
    columns = (columns + ada_bias.astype(F32)[None]).astype(BF16)
    columns = links.exchange_relative(columns.reshape((dp_size, 2) + columns.shape[1:]))

    table_width = max(features, wide, 3 * local)

    def padded(rows):
        return jnp.pad(rows.astype(F32), ((0, 0), (0, table_width - rows.shape[1])))

    qkv_bias = jnp.concatenate(
        [qv_bias[:, 0], jnp.zeros_like(qv_bias[:, 0]), qv_bias[:, 1]], axis=1
    )
    small = jnp.concatenate([padded(proj_bias), padded(down_bias), padded(up_bias), padded(qkv_bias)])

    long_half, short_half = kept[0] // 2, kept[1] // 2
    quarter = long_half // 2
    enc_rows = [
        Rows((0, long_half, quarter)),
        Rows((quarter, long_half, quarter)),
        Rows((0, short_half, short_half)),
    ]
    table_places = [Rows((0, long_half, long_half)), Rows((0, short_half, short_half))]
    masked_places = [
        Rows((kept[0], long_half, long_half)),
        Rows((kept[1], short_half, short_half)),
    ]
    dec_rows = [
        table_places[0],
        masked_places[0],
        Rows((0, short_half, short_half), (kept[1], short_half, short_half)),
    ]
    enc_latents, dec_latents = (0, 0, 1), (0, 0, 1)

    streams = [
        gather_rows(queue, core, perms[latent], tokens[latent], rows, F32)
        for latent, rows in zip(enc_latents, enc_rows)
    ]
    mods = spread_mods(queue, links.me, columns, features)
    weights = Weights(
        jnp.transpose(qkv_weight, (0, 2, 3, 1)).reshape(2, 3 * local, features),
        proj_weight,
        up_weight,
        down_weight,
        small,
        mods,
    )
    families = {(block, latent): [] for block in (0, 1) for latent in (0, 1)}

    def chunks_of(block, latents):
        return [
            Chunk(queue, links, weights, block, latent, families[block, latent])
            for latent in latents
        ]

    encoder = chunks_of(0, enc_latents)
    decoder = chunks_of(1, dec_latents)
    ea, eb, es = encoder
    dk, dm, dt = decoder

    for chunk, stream in zip(encoder, streams):
        chunk.enter(stream, ln_open(queue, stream, mods, chunk.at))
    for chunk in encoder:
        chunk.qkv()
    ea.attention()
    eb.attention()
    ea.near()
    es.attention()
    eb.near()
    es.near()
    perms_later, filler, cots_later = queue.tie(perms, mask_token, cots)
    filler = filler.astype(F32)[None]
    waves = []
    for length in lengths:
        side = math.isqrt(length)
        quarter_wave = features // 4
        frequency = 1.0 / 10000.0 ** (jnp.arange(quarter_wave, dtype=F32) / quarter_wave)
        angle = jnp.arange(side, dtype=jnp.int32).astype(F32)[:, None] * frequency[None, :]
        waves.append(jnp.concatenate([jnp.sin(angle), jnp.cos(angle)], axis=1))
    masked = table_rows(queue, core, perms_later[0], waves[0], masked_places[0], filler)
    dm.enter(masked, ln_open(queue, masked, mods, dm.at))
    ea.merge()
    dm.qkv()
    ea.mlp()
    eb.merge()
    ea.near()
    es.merge()
    eb.mlp()
    es.mlp()
    eb.near()
    es.near()
    table_long = table_rows(queue, core, perms_later[0], waves[0], table_places[0])
    table_short = table_rows(queue, core, perms_later[1], waves[1], table_places[1])
    masked_short = table_rows(queue, core, perms_later[1], waves[1], masked_places[1], filler)
    d_out = [
        gather_rows(queue, core, perms_later[latent], cots_later[latent], rows, BF16)
        for latent, rows in zip(dec_latents, dec_rows)
    ]
    first_sums = []
    for chunk, grad in zip(decoder, d_out):
        d_branch, sums = first_grad(queue, grad, mods, chunk.at)
        first_sums.append(sums)
        chunk.start_back(grad, d_branch)

    pieces = [(chunk.middle, *chunk.sum) for chunk in encoder]
    for chunk in encoder:
        chunk.branch_mlp = chunk.sum
    dk.enter(*merge_mlp(queue, pieces[:2], small, mods, (0, 0), table_long, None))
    dt.enter(*merge_mlp(queue, pieces[2:], small, mods, (0, 1), table_short, masked_short))
    dk.qkv()
    dk.attention()
    dt.qkv()
    dk.near()
    dm.attention()
    dt.attention()
    dm.near()
    dt.near()
    dk.merge()
    dk.mlp()
    dm.merge()
    forward = {dk: dk.part}
    dk.mlp_back()
    dm.mlp()
    dk.near()
    forward[dm] = dm.part
    dm.mlp_back()
    dt.merge()
    dm.near()
    dt.mlp()
    forward[dt] = dt.part
    dt.mlp_back()
    dt.near()

    y_first, z_first = list(links.dp_bits), list(links.dp_bits)
    if len(z_first) > 1:
        z_first[0], z_first[1] = z_first[1], z_first[0]

    def wide_pairs(chunks):
        return [
            (rows_of(chunks, "normed_mlp"), rows_of(chunks, "d_hidden")),
            (rows_of(chunks, "d_branch_mlp"), rows_of(chunks, "active")),
        ]

    def attention_pairs(chunks):
        return [
            (rows_of(chunks, "d_branch_attn"), rows_of(chunks, "attended")),
            (rows_of(chunks, "normed_attn"), rows_of(chunks, "d_qkv")),
        ]

    sums_there = {}

    def forward_sum(chunk):
        near = near_sum(queue, *forward[chunk])
        sums_there[chunk] = (near, links.cross(near))

    dk.merge_back()
    dec_wide, dec_wide_sums, _ = reduced(queue, links, wide_pairs(decoder))
    dm.merge_back()
    forward_sum(dk)
    forward_sum(dm)
    dm.attention_back()
    dk.qkv_back()
    dk.near()
    dm.qkv_back()
    dt.merge_back()
    dm.near()
    dt.attention_back()
    dt.qkv_back()
    dt.near()
    enc_branch = (small, DOWN_BIAS, (0, 0), GATE_MLP)
    short_branch = (small, DOWN_BIAS, (0, 1), GATE_MLP)
    d_a, d_b, grad_a, grad_b = dk.leave_back(([ea.branch_mlp, eb.branch_mlp], *enc_branch))
    ea.start_back(d_a, grad_a)
    eb.start_back(d_b, grad_b)

    ea.mlp_back()
    eb.mlp_back()
    ea.near()
    eb.near()
    (dec_attn,), dec_attn_sums = scatter_sums(
        queue, links, attention_pairs(decoder), [(4 * local, y_first)]
    )
    dm.leave_back()
    d_short, grad_short = dt.leave_back(([es.branch_mlp], *short_branch))
    es.start_back(d_short, grad_short)
    es.mlp_back()
    es.near()
    ea.merge_back()
    enc_wide, enc_wide_sums, dec_wide = reduced(queue, links, wide_pairs(encoder), dec_wide)
    eb.merge_back()
    forward_sum(dt)
    dec_attn.step()
    ea.attention_back()
    ea.qkv_back()
    ea.near()
    eb.qkv_back()
    es.merge_back()
    eb.near()
    es.attention_back()
    es.qkv_back()
    es.near()
    (enc_attn,), enc_attn_sums = scatter_sums(
        queue, links, attention_pairs(encoder), [(4 * local, y_first)]
    )
    dec_attn.step()
    own_tokens = []
    for chunk in (ea, eb, es):
        own_tokens += chunk.leave_back(narrow=True)
    decoded, gate_sums = finish(
        queue,
        [
            (chunk.middle, *sums_there[chunk], d_out[index], chunk.at)
            for index, chunk in enumerate(decoder)
        ],
        small,
        mods,
    )

    sources, recipe = [], []

    def row(array, index):
        for place, source in enumerate(sources):
            if source is array:
                return place, index
        sources.append(array)
        return len(sources) - 1, index

    for block, chunks in ((0, encoder), (1, decoder)):
        for latent in (0, 1):
            members = [chunk for chunk in chunks if chunk.latent == latent]
            if block == 0:
                gates = [row((dk, dt)[latent].attn_sums, 2)]
            else:
                gates = [row(gate_sums, latent)]
            recipe += [
                [row(chunk.attn_sums, 1) for chunk in members],
                [row(chunk.attn_sums, 0) for chunk in members],
                [row(chunk.mlp_sums, 2) for chunk in members],
                [row(chunk.mlp_sums, 1) for chunk in members],
                [row(chunk.mlp_sums, 0) for chunk in members],
                gates,
            ]
    recipe += [
        [row(chunk.mlp_sums, 3) for chunk in encoder],
        [row(chunk.mlp_sums, 3) for chunk in decoder],
        [row(chunk.attn_sums, 3) for chunk in (dk, dt)],
        [row(sums, 0) for sums in first_sums],
        [row(chunk.attn_sums, 4) for chunk in (dm, dt)],
    ]
    own_sums, joined = collect_sums(queue, sources, recipe, own_tokens)
    packed, all_sums = pack_mods(
        queue, links.me, own_sums, links.swap(own_sums), 2, 2, dp_size, features
    )
    totals = jnp.concatenate(
        [all_sums[24:29].reshape(-1), enc_wide_sums[0, :wide], dec_wide_sums[0, :wide]]
        + [
            sums[0, first : first + local]
            for sums in (enc_attn_sums, dec_attn_sums)
            for first in (local, 3 * local)
        ]
    )
    mine, totals = links.exchange_relative(packed, totals)
    flat_mine = mine.reshape((-1,) + mine.shape[2:])
    grad_ada = jnp.einsum("nd,nlm->ldm", flat_acts, flat_mine, preferred_element_type=F32)
    grad_ada_bias = jnp.sum(flat_mine.astype(F32), axis=0)
    d_acts = jnp.einsum("nlm,ldm->nd", flat_mine, ada_weight, preferred_element_type=F32)
    d_act = links.sum_relative(d_acts.reshape(dp_size, 2, features))
    gate = jax.nn.sigmoid(cond)
    d_cond = (d_act * gate * (1.0 + cond * (1.0 - gate))).astype(BF16)

    proj_out = totals[: 2 * features].reshape(2, features)
    down_out = totals[2 * features : 4 * features].reshape(2, features)
    mask_out = totals[4 * features : 5 * features]
    first = 5 * features
    up_out = totals[first : first + 2 * wide].reshape(2, wide)
    first += 2 * wide
    qv_out = totals[first : first + 4 * local].reshape(2, 2, local)

    enc_attn.step()
    decoded_other = links.swap(decoded)
    results = (
        place_rows(queue, core, perms_later[0], decoded, decoded_other, dec_rows[:2], 0),
        place_rows(
            queue, core, perms_later[1], decoded, decoded_other, dec_rows[2:], 2 * long_half
        ),
    )
    enc_attn.step()
    joined_other = links.swap(joined)
    d_tokens = (
        place_rows(queue, core, perms_later[0], joined, joined_other, enc_rows[:2], 0),
        place_rows(queue, core, perms_later[1], joined, joined_other, enc_rows[2:], long_half),
    )
    up_grad = jnp.stack([enc_wide[:, :wide], dec_wide[:, :wide]]).astype(F32)
    down_grad = jnp.stack([enc_wide[:, wide:], dec_wide[:, wide:]]).astype(F32)
    dec_att, enc_att = dec_attn.result(), enc_attn.result()
    proj_grad = jnp.stack([enc_att[:, :local], dec_att[:, :local]])
    qkv_grad = jnp.stack([enc_att[:, local:], dec_att[:, local:]]).reshape(2, -1, 3, local)

    return (
        results[0][None],
        results[1][None],
        d_tokens[0][None],
        d_tokens[1][None],
        d_cond[:1],
        d_cond[1:],
        grad_ada,
        grad_ada_bias,
        qkv_grad,
        qv_out,
        jnp.transpose(proj_grad, (0, 2, 1)),
        proj_out,
        up_grad,
        up_out,
        jnp.transpose(down_grad, (0, 2, 1)),
        down_out,
        mask_out,
    )


def solution(mesh):
    in_specs = (
        P("dp", None, None),
        P("dp", None, None),
        P("dp", None),
        P("dp", None),
        P("dp", None),
        P("dp", None),
        P(None, None, "dp"),
        P(None, "dp"),
        P(None, None, None, "tensor"),
        P(None, None, "tensor"),
        P(None, "tensor", None),
        P(),
        P(None, None, "tensor"),
        P(None, "tensor"),
        P(None, "tensor", None),
        P(),
        P(),
        P("dp", None, None),
        P("dp", None, None),
    )
    out_specs = (
        P("dp", None, None),
        P("dp", None, None),
        P("dp", None, None),
        P("dp", None, None),
        P("dp", None),
        P("dp", None),
        P(None, None, "dp"),
        P(None, "dp"),
        P(None, "dp", None, "tensor"),
        P(None, None, "tensor"),
        P(None, "tensor", "dp"),
        P(),
        P(None, "dp", "tensor"),
        P(None, "tensor"),
        P(None, "tensor", "dp"),
        P(),
        P(),
    )

    def step(*arguments):
        return on_device(mesh.shape["dp"], mesh.shape["tensor"], *arguments)

    return jax.shard_map(
        step, mesh=mesh, in_specs=in_specs, out_specs=out_specs, check_vma=False
    )
```

```python
import math

import jax
import jax.numpy as jnp
from jax import lax
from jax.experimental import pallas as pl
from jax.experimental.pallas import tpu as pltpu
from jax.sharding import PartitionSpec as P

HEAD_DIM = 72
EPSILON = 1e-06
BF16 = jnp.bfloat16
F32 = jnp.float32
MIB = 1 << 20
SCALING = HEAD_DIM**-0.5
EXPONENT = SCALING * math.log2(math.e)
GELU_A = math.sqrt(2.0 / math.pi)
GELU_B = 0.044715

SHIFT_ATTN, SCALE_ATTN, GATE_ATTN, SHIFT_MLP, SCALE_MLP, GATE_MLP = range(6)
PROJ_BIAS, DOWN_BIAS, UP_BIAS, QKV_BIAS = 0, 2, 4, 6


def nn(left, right):
    return lax.dot_general(left, right, (((1,), (0,)), ((), ())), preferred_element_type=F32)


def nt(left, right):
    return lax.dot_general(left, right, (((1,), (1,)), ((), ())), preferred_element_type=F32)


def tn(left, right):
    return lax.dot_general(left, right, (((0,), (0,)), ((), ())), preferred_element_type=F32)


def shaped(shape, dtype=BF16):
    return jax.ShapeDtypeStruct(shape, dtype)


COSTS = {
    "gather_rows": 0.8, "ln_open": 0.4, "near_sum": 0.4, "merge_attn": 0.6, "merge_mlp": 0.6,
    "finish": 1.0, "first_grad": 0.5, "qkv_forward": 1.2, "qkv_backward": 1.2, "mlp_forward": 3.5,
    "mlp_backward": 3.0, "ln_back": 1.2, "attn_forward": 0.0, "attn_backward": 0.0,
    "weight_grads": 6.5, "halve": 1.5, "place_rows": 3.0, "table_rows": 1.0,
}


class Queue:
    def __init__(self):
        self.token = jnp.zeros((8, 128), F32)

    def tie(self, *values):
        *values, self.token = lax.optimization_barrier((*values, self.token))
        return values[0] if len(values) == 1 else tuple(values)

    def call(
        self, body, operands, outs, name, scalars=(), far=(), far_outs=(), scratch=(), copies=0, limit=10
    ):
        fast = pl.BlockSpec(memory_space=pltpu.VMEM)
        small = pl.BlockSpec(memory_space=pltpu.SMEM)
        slow = pl.BlockSpec(memory_space=pltpu.HBM)
        last = len(scalars) + len(far) + len(operands) + len(outs) + len(far_outs)

        def whole(token_ref, *refs):
            body(*refs[:last], *refs[last + 1 :])
            refs[last][...] = token_ref[...]

        *results, self.token = pl.pallas_call(
            whole,
            in_specs=[fast] + [small] * len(scalars) + [slow] * len(far) + [fast] * len(operands),
            out_specs=[fast] * len(outs) + [slow] * len(far_outs) + [fast],
            out_shape=[
                *outs,
                *[pltpu.HBM(out.shape, out.dtype) for out in far_outs],
                shaped((8, 128), F32),
            ],
            scratch_shapes=list(scratch)
            + ([pltpu.SemaphoreType.DMA((copies,))] if copies else []),
            cost_estimate=pl.CostEstimate(
                flops=int(COSTS.get(name, 1.0) * 1.15e9), transcendentals=0, bytes_accessed=1000
            ),
            compiler_params=pltpu.CompilerParams(vmem_limit_bytes=limit * MIB),
            name=name,
        )(
            pltpu.with_memory_space_constraint(self.token, pltpu.VMEM),
            *scalars,
            *[pltpu.with_memory_space_constraint(value, pltpu.HBM) for value in far],
            *[pltpu.with_memory_space_constraint(value, pltpu.VMEM) for value in operands],
        )
        return results


def copy_rows(sources, target, semaphores, first=0):
    found, row = [], 0
    for index, source in enumerate(sources):
        count = source.shape[0]
        copy = pltpu.make_async_copy(
            source, target.at[pl.ds(row, count)], semaphores.at[first + index]
        )
        copy.start()
        found.append(copy)
        row += count
    return found


def normed_of(values):
    center = values - jnp.mean(values, axis=-1, keepdims=True)
    spread = jnp.mean(center * center, axis=-1, keepdims=True)
    scale = lax.rsqrt(spread + EPSILON)
    return center * scale, scale


def modulate(values, mods_ref, at, scale_part, shift_part):
    block, latent = at
    scale = mods_ref[block, latent, scale_part : scale_part + 1, :]
    shift = mods_ref[block, latent, shift_part : shift_part + 1, :]
    return (normed_of(values)[0] * (1.0 + scale) + shift).astype(BF16)


def branch_of(near_ref, far_ref, small_ref, row, features):
    return (
        near_ref[...].astype(F32)
        + far_ref[...].astype(F32)
        + small_ref[row : row + 1, :features]
    )


class Rows:
    def __init__(self, *spans):
        self.spans = spans
        self.count = sum(span[2] for span in spans)

    def places(self, perm_ref, core, other=False):
        found = []
        for first, stride, count in self.spans:
            low = perm_ref[:, first : first + count]
            high = perm_ref[:, first + stride : first + stride + count]
            found.append(jnp.where((core == 1) != other, high, low))
        return found[0] if len(found) == 1 else jnp.concatenate(found, axis=1)


def pick_columns(places, length):
    index = lax.broadcasted_iota(jnp.int32, (length, places.shape[1]), 0)
    return (index == places).astype(F32).astype(BF16)


def gather_rows(queue, core, perm, source, rows, dtype):
    length, features = source.shape

    def body(core_ref, perm_ref, source_ref, out_ref):
        pick = pick_columns(rows.places(perm_ref, core_ref[0]), length)
        out_ref[...] = tn(pick, source_ref[...]).astype(dtype)

    outs = [shaped((rows.count, features), dtype)]
    return queue.call(body, [perm, source], outs, "gather_rows", scalars=[core])[0]


def place_rows(queue, core, perm, own, other, rows, first):
    length = perm.shape[1]
    features = own.shape[1]
    last = first + sum(chunk.count for chunk in rows)

    def body(core_ref, perm_ref, own_ref, other_ref, out_ref):
        places = [
            chunk.places(perm_ref, core_ref[0], other) for other in (False, True) for chunk in rows
        ]
        values = jnp.concatenate([own_ref[first:last, :], other_ref[first:last, :]], axis=0)
        pick = pick_columns(jnp.concatenate(places, axis=1), length)
        out_ref[...] = nn(pick, values).astype(BF16)

    outs = [shaped((length, features))]
    return queue.call(
        body, [perm, own, other], outs, "place_rows", scalars=[core], limit=12
    )[0]


def table_rows(queue, core, perm, waves, rows, filler=None):
    side, half = waves.shape

    def body(core_ref, perm_ref, waves_ref, *refs):
        places = rows.places(perm_ref, core_ref[0])
        index = lax.broadcasted_iota(jnp.int32, (side, places.shape[1]), 0)
        row_pick = ((places >= index * side) & (places < (index + 1) * side)).astype(F32)
        row = jnp.sum(row_pick * index.astype(F32), axis=0, keepdims=True)
        col_pick = (index.astype(F32) == places.astype(F32) - row * side).astype(F32)
        for low, pick in ((0, row_pick), (half, col_pick)):
            out = lax.dot_general(
                pick,
                waves_ref[...],
                (((0,), (0,)), ((), ())),
                precision=lax.Precision.HIGHEST,
                preferred_element_type=F32,
            )
            if filler is not None:
                out = out + refs[0][:, low : low + half]
            refs[-1][:, low : low + half] = out

    operands = [perm, waves] + ([] if filler is None else [filler])
    outs = [shaped((rows.count, 2 * half), F32)]
    return queue.call(body, operands, outs, "table_rows", scalars=[core])[0]


def ln_open(queue, stream, mods, at):
    def body(x_ref, mods_ref, out_ref):
        out_ref[...] = modulate(x_ref[...], mods_ref, at, SCALE_ATTN, SHIFT_ATTN)

    return queue.call(body, [stream, mods], [shaped(stream.shape)], "ln_open")[0]


def near_sum(queue, own, moved):
    def body(own_ref, moved_ref, out_ref):
        out_ref[...] = (own_ref[...].astype(F32) + moved_ref[...].astype(F32)).astype(BF16)

    return queue.call(body, [own, moved], [shaped(own.shape)], "near_sum")[0]


def merge_attn(queue, stream, near, far, small, mods, at):
    features = stream.shape[1]
    block, latent = at

    def body(x_ref, near_ref, far_ref, small_ref, mods_ref, mid_ref, out_ref):
        branch = branch_of(near_ref, far_ref, small_ref, PROJ_BIAS + block, features)
        middle = x_ref[...] + mods_ref[block, latent, GATE_ATTN : GATE_ATTN + 1, :] * branch
        mid_ref[...] = middle
        out_ref[...] = modulate(middle, mods_ref, at, SCALE_MLP, SHIFT_MLP)

    outs = [shaped(stream.shape, F32), shaped(stream.shape)]
    return queue.call(body, [stream, near, far, small, mods], outs, "merge_attn")


def merge_mlp(queue, pieces, small, mods, at, table, tail):
    features = table.shape[1]
    counts = [piece[0].shape[0] for piece in pieces]
    block, latent = at
    total = sum(counts) + (0 if tail is None else tail.shape[0])
    following = (block + 1, latent)

    def body(table_ref, small_ref, mods_ref, *refs):
        x_ref, out_ref = refs[-2:]
        gate = mods_ref[block, latent, GATE_MLP : GATE_MLP + 1, :]
        first = 0
        for index, count in enumerate(counts):
            mid_ref, near_ref, far_ref = refs[3 * index : 3 * index + 3]
            branch = branch_of(near_ref, far_ref, small_ref, DOWN_BIAS + block, features)
            stream = mid_ref[...] + gate * branch + table_ref[first : first + count, :]
            x_ref[first : first + count, :] = stream
            out_ref[first : first + count, :] = modulate(
                stream, mods_ref, following, SCALE_ATTN, SHIFT_ATTN
            )
            first += count
        if tail is not None:
            stream = refs[3 * len(counts)][...]
            x_ref[first:, :] = stream
            out_ref[first:, :] = modulate(stream, mods_ref, following, SCALE_ATTN, SHIFT_ATTN)

    operands = [table, small, mods] + [part for piece in pieces for part in piece]
    operands += [] if tail is None else [tail]
    outs = [shaped((total, features), F32), shaped((total, features))]
    return queue.call(body, operands, outs, "merge_mlp")


def finish(queue, parts, small, mods):
    counts = [part[0].shape[0] for part in parts]
    features = parts[0][0].shape[1]

    def body(small_ref, mods_ref, *refs):
        out_ref, sums_ref = refs[-2:]
        sums_ref[...] = jnp.zeros_like(sums_ref)
        first = 0
        for index, count in enumerate(counts):
            mid_ref, near_ref, far_ref, d_ref = refs[4 * index : 4 * index + 4]
            block, latent = parts[index][4]
            branch = branch_of(near_ref, far_ref, small_ref, DOWN_BIAS + block, features)
            gate = mods_ref[block, latent, GATE_MLP : GATE_MLP + 1, :]
            out_ref[first : first + count, :] = (mid_ref[...] + gate * branch).astype(BF16)
            total = jnp.sum(d_ref[...].astype(F32) * branch, axis=0, keepdims=True)
            sums_ref[latent : latent + 1, :] += total
            first += count

    outs = [shaped((sum(counts), features)), shaped((8, features), F32)]
    operands = [small, mods] + [value for part in parts for value in part[:4]]
    return queue.call(body, operands, outs, "finish")


def first_grad(queue, d_out, mods, at):
    features = d_out.shape[1]
    block, latent = at

    def body(d_ref, mods_ref, out_ref, sums_ref):
        gate = mods_ref[block, latent, GATE_MLP : GATE_MLP + 1, :]
        grad = (gate * d_ref[...].astype(F32)).astype(BF16)
        out_ref[...] = grad
        total = jnp.sum(grad.astype(F32), axis=0, keepdims=True)
        sums_ref[...] = jnp.broadcast_to(total, (8, features))

    outs = [shaped(d_out.shape), shaped((8, features), F32)]
    return queue.call(body, [d_out, mods], outs, "first_grad")


def qkv_forward(queue, own, other, weight, small, block):
    rows, features = own.shape
    width = weight.shape[1]

    def body(own_ref, other_ref, w_ref, small_ref, out_ref, rows_ref, done):
        copies = copy_rows([own_ref, other_ref], rows_ref, done)
        bias = small_ref[QKV_BIAS + block : QKV_BIAS + block + 1, :width]
        both = jnp.concatenate([own_ref[...], other_ref[...]], axis=0)
        out = (nt(both, w_ref[block]) + bias).astype(BF16)
        out_ref[0] = out[:rows]
        out_ref[1] = out[rows:]
        for copy in copies:
            copy.wait()

    return queue.call(
        body,
        [own, other, weight, small],
        [shaped((2, rows, width))],
        "qkv_forward",
        far_outs=[shaped((2 * rows, features))],
        copies=2,
    )


def qkv_backward(queue, grads, weight, block):
    _, rows, _ = grads.shape
    features = weight.shape[2]

    def body(g_ref, w_ref, own_ref, other_ref):
        both = jnp.concatenate([g_ref[0], g_ref[1]], axis=0)
        out = nn(both, w_ref[block]).astype(BF16)
        own_ref[...] = out[:rows]
        other_ref[...] = out[rows:]

    outs = [shaped((rows, features)), shaped((rows, features))]
    return queue.call(body, [grads, weight], outs, "qkv_backward")


def mlp_forward(queue, own, other, up_weight, down_weight, small, block):
    rows, features = own.shape
    wide = up_weight.shape[2]

    def body(
        own_ref, other_ref, up_ref, down_ref, small_ref,
        own_out, other_out, slope_ref, rows_ref, act_ref, act_s, done,
    ):
        copies = copy_rows([own_ref, other_ref], rows_ref, done)
        bias = small_ref[UP_BIAS + block : UP_BIAS + block + 1, :wide]
        both = jnp.concatenate([own_ref[...], other_ref[...]], axis=0)
        hidden = nn(both, up_ref[block]) + bias
        squared = hidden * hidden
        bent = jnp.tanh(GELU_A * hidden * (1.0 + GELU_B * squared))
        half = 0.5 + 0.5 * bent
        act_s[...] = (hidden * half).astype(BF16)
        slope = half + 0.5 * hidden * (1.0 - bent * bent) * (
            GELU_A + 3.0 * GELU_A * GELU_B * squared
        )
        slope_ref[...] = slope.astype(BF16)
        copies += copy_rows([act_s], act_ref, done, 2)
        out = nn(act_s[...], down_ref[block]).astype(BF16)
        own_out[...] = out[:rows]
        other_out[...] = out[rows:]
        for copy in copies:
            copy.wait()

    full = shaped((2 * rows, wide))
    return queue.call(
        body,
        [own, other, up_weight, down_weight, small],
        [shaped((rows, features)), shaped((rows, features)), full],
        "mlp_forward",
        far_outs=[shaped((2 * rows, features)), full],
        scratch=[pltpu.VMEM((2 * rows, wide), BF16)],
        copies=3,
        limit=12,
    )


def mlp_backward(queue, own, other, slope, up_weight, down_weight, block):
    rows, features = own.shape
    wide = up_weight.shape[2]

    def body(
        own_ref, other_ref, slope_ref, up_ref, down_ref,
        own_out, other_out, rows_ref, hid_ref, hid_s, done,
    ):
        copies = copy_rows([own_ref, other_ref], rows_ref, done)
        both = jnp.concatenate([own_ref[...], other_ref[...]], axis=0)
        d_active = nt(both, down_ref[block])
        hid_s[...] = (d_active * slope_ref[...].astype(F32)).astype(BF16)
        copies += copy_rows([hid_s], hid_ref, done, 2)
        out = nt(hid_s[...], up_ref[block]).astype(BF16)
        own_out[...] = out[:rows]
        other_out[...] = out[rows:]
        for copy in copies:
            copy.wait()

    return queue.call(
        body,
        [own, other, slope, up_weight, down_weight],
        [shaped((rows, features)), shaped((rows, features))],
        "mlp_backward",
        far_outs=[shaped((2 * rows, features)), shaped((2 * rows, wide))],
        scratch=[pltpu.VMEM((2 * rows, wide), BF16)],
        copies=3,
        limit=12,
    )


def ln_back(queue, near, far, stream, d_out, mods, at, scale_part, branch=None, narrow=False):
    rows, features = stream.shape
    pieces = [] if branch is None else branch[0]
    counts = [piece[0].shape[0] for piece in pieces]
    inner = sum(counts)
    operands = [near, far, stream, d_out, mods]
    outs = [shaped((8, features), F32)]
    if narrow:
        outs.append(shaped((rows, features)))
    if pieces:
        _, small, bias_row, gate_at, gate_part = branch
        operands += [small] + [half for piece in pieces for half in piece]
        outs += [shaped((count, features), F32) for count in counts]
        outs += [shaped((count, features)) for count in counts]
    inputs = len(operands)

    def body(*refs):
        near_ref, far_ref, x_ref, d_ref, mods_ref = refs[:5]
        sums_ref, *out_refs = refs[inputs:]
        scale = mods_ref[at[0], at[1], scale_part : scale_part + 1, :]
        d_normed = near_ref[...].astype(F32) + far_ref[...].astype(F32)
        normed, spread = normed_of(x_ref[...])
        product = d_normed * normed
        grad = d_normed * (1.0 + scale)
        d_x = d_ref[...].astype(F32) + spread * (
            grad
            - jnp.mean(grad, axis=-1, keepdims=True)
            - normed * jnp.mean(grad * normed, axis=-1, keepdims=True)
        )
        zero = jnp.zeros((1, features), F32)
        gate_sum, bias_sum, rest_sum = zero, zero, zero
        if narrow:
            out_refs[0][...] = d_x.astype(BF16)
        elif inner < rows:
            rest_sum = jnp.sum(d_x[inner:], axis=0, keepdims=True)
        first = 0
        for index, count in enumerate(counts):
            piece_near, piece_far = refs[6 + 2 * index : 8 + 2 * index]
            value = branch_of(piece_near, piece_far, refs[5], bias_row, features)
            part = d_x[first : first + count]
            gate = mods_ref[gate_at[0], gate_at[1], gate_part : gate_part + 1, :]
            d_branch = (gate * part).astype(BF16)
            out_refs[index][...] = part
            out_refs[len(counts) + index][...] = d_branch
            gate_sum = gate_sum + jnp.sum(part * value, axis=0, keepdims=True)
            bias_sum = bias_sum + jnp.sum(d_branch.astype(F32), axis=0, keepdims=True)
            first += count
        sums_ref[...] = jnp.concatenate(
            [
                jnp.sum(product, axis=0, keepdims=True),
                jnp.sum(d_normed, axis=0, keepdims=True),
                gate_sum,
                bias_sum,
                rest_sum,
                jnp.zeros((3, features), F32),
            ],
            axis=0,
        )

    return queue.call(body, operands, outs, "ln_back")


def attn_forward(queue, query, merged, proj_weight, block):
    _, rows, width = query.shape
    local = width // 3
    heads = local // HEAD_DIM
    counts = [part.shape[1] for part in merged]
    total = 2 * sum(counts)
    features = proj_weight.shape[2]
    by_keys = rows < 128

    def body(*refs):
        q_ref, refs = refs[0], refs[1:]
        kv_refs, refs = refs[: len(merged)], refs[len(merged) :]
        proj_ref, lse_ref, own_out, other_out, att_far, q_s, k_s, v_s, o_s, l_s, att_ref, done = refs
        for head in range(heads):
            low = head * HEAD_DIM
            first = 0
            for part, count in zip(kv_refs, counts):
                for side in range(2):
                    at = pl.ds(first, count)
                    k_s[head, at, :] = part[side, :, local + low : local + low + HEAD_DIM]
                    v_s[head, at, :] = part[side, :, 2 * local + low : 2 * local + low + HEAD_DIM]
                    first += count
            for side in range(2):
                q_s[head, side] = q_ref[side, :, low : low + HEAD_DIM]
        for head in range(heads):
            for side in range(2):
                if by_keys:
                    scores = nt(k_s[head], q_s[head, side])
                    highest = jnp.max(scores, axis=0, keepdims=True)
                    raised = jnp.exp2((scores - highest) * EXPONENT)
                    total_row = jnp.sum(raised, axis=0, keepdims=True)
                    out = tn(v_s[head], raised.astype(BF16))
                    o_s[head, side] = (out / total_row).T.astype(BF16)
                    lse_ref[head, side] = highest * EXPONENT + jnp.log2(total_row)
                else:
                    scores = nt(q_s[head, side], k_s[head])
                    highest = jnp.max(scores, axis=1, keepdims=True)
                    raised = jnp.exp2((scores - highest) * EXPONENT)
                    total_row = jnp.sum(raised, axis=1, keepdims=True)
                    out = nn(raised.astype(BF16), v_s[head])
                    o_s[head, side] = (out / total_row).astype(BF16)
                    l_s[head, side] = jnp.broadcast_to(
                        highest * EXPONENT + jnp.log2(total_row), (rows, 128)
                    )
        if not by_keys:
            for head in range(heads):
                for side in range(2):
                    lse_ref[head, side] = l_s[head, side].T[:1]
        for side, out_ref in ((1, other_out), (0, own_out)):
            for head in range(heads):
                low = head * HEAD_DIM
                att_ref[side * rows : (side + 1) * rows, low : low + HEAD_DIM] = o_s[head, side]
            out_ref[...] = nn(
                att_ref[side * rows : (side + 1) * rows, :], proj_ref[block]
            ).astype(BF16)
        for copy in copy_rows([att_ref], att_far, done):
            copy.wait()

    return queue.call(
        body,
        [query, *merged, proj_weight],
        [
            shaped((heads, 2, 1, rows), F32),
            shaped((rows, features)),
            shaped((rows, features)),
        ],
        "attn_forward",
        far_outs=[shaped((2 * rows, local))],
        scratch=[
            pltpu.VMEM((heads, 2, rows, HEAD_DIM), BF16),
            pltpu.VMEM((heads, total, HEAD_DIM), BF16),
            pltpu.VMEM((heads, total, HEAD_DIM), BF16),
            pltpu.VMEM((heads, 2, rows, HEAD_DIM), BF16),
            pltpu.VMEM((heads, 2, 8 if by_keys else rows, 128), F32),
            pltpu.VMEM((2 * rows, local), BF16),
        ],
        copies=1,
        limit=13,
    )


def attn_backward(queue, merged, normers, grads, proj_weight, block):
    count = len(merged)
    width = merged[0].shape[2]
    local = width // 3
    heads = local // HEAD_DIM
    halves = [part.shape[1] for part in merged]
    total = 2 * sum(halves)
    features = proj_weight.shape[2]
    step = min(halves)
    steps = total // step
    unroll = 4 if step * steps > 512 else steps * heads

    def body(*refs):
        m_refs, refs = refs[:count], refs[count:]
        l_refs, refs = refs[:count], refs[count:]
        g_refs, refs = refs[: 2 * count], refs[2 * count :]
        proj_ref, refs = refs[0], refs[1:]
        out_refs, refs = refs[:count], refs[count:]
        row_refs, refs = refs[:count], refs[count:]
        qkv_refs, refs = refs[:count], refs[count:]
        q_s, k_s, kt_s, v_s, g_s, dq_s, dk_s, dv_s, l_s, done = refs
        copies = []
        for index in range(count):
            copies += copy_rows(
                g_refs[2 * index : 2 * index + 2], row_refs[index], done, 2 * index
            )
        first = 0
        for index in range(count):
            rows = halves[index]
            for side in range(2):
                at = pl.ds(first, rows)
                grad = nt(g_refs[2 * index + side][...], proj_ref[block]).astype(BF16)
                for head in range(heads):
                    low = head * HEAD_DIM
                    part = m_refs[index]
                    q_s[head, at, :] = part[side, :, low : low + HEAD_DIM]
                    keys = part[side, :, local + low : local + low + HEAD_DIM]
                    k_s[head, at, :] = keys
                    kt_s[head, :, at] = keys.T
                    v_s[head, at, :] = part[side, :, 2 * local + low : 2 * local + low + HEAD_DIM]
                    g_s[head, at, :] = grad[:, low : low + HEAD_DIM]
                    for piece in range(rows // step):
                        l_s[head, first // step + piece] = l_refs[index][
                            head, side, :, piece * step : (piece + 1) * step
                        ]
                first += rows
        dk_s[...] = jnp.zeros_like(dk_s)
        dv_s[...] = jnp.zeros_like(dv_s)

        def one(index, carry):
            head, piece = index // steps, lax.rem(index, steps)
            at = pl.ds(pl.multiple_of(piece * step, step), step)
            queries, grad = q_s[head, at, :], g_s[head, at, :]
            probs = jnp.exp2(nt(k_s[head], queries) * EXPONENT - l_s[head, piece])
            product = probs * nt(v_s[head], grad)
            delta = jnp.sum(product, axis=0, keepdims=True)
            d_scores = (product - probs * delta).astype(BF16)
            dv_s[head] += nn(probs.astype(BF16), grad)
            dk_s[head] += nn(d_scores, queries)
            dq_s[head, at, :] = (nn(kt_s[head], d_scores) * SCALING).T.astype(BF16)
            return carry

        lax.fori_loop(0, steps * heads, one, 0, unroll=unroll)
        first = 0
        for index in range(count):
            rows = halves[index]
            for side in range(2):
                at = pl.ds(first, rows)
                out = out_refs[index]
                for head in range(heads):
                    low = head * HEAD_DIM
                    out[side, :, low : low + HEAD_DIM] = dq_s[head, at, :]
                    out[side, :, local + low : local + low + HEAD_DIM] = (
                        dk_s[head, at, :] * SCALING
                    ).astype(BF16)
                    out[side, :, 2 * local + low : 2 * local + low + HEAD_DIM] = dv_s[
                        head, at, :
                    ].astype(BF16)
                first += rows
            copies += copy_rows(
                [out_refs[index].at[0], out_refs[index].at[1]],
                qkv_refs[index],
                done,
                2 * count + 2 * index,
            )
        for copy in copies:
            copy.wait()

    def lanes(dtype=BF16):
        return pltpu.VMEM((heads, total, HEAD_DIM), dtype)

    return queue.call(
        body,
        [*merged, *normers, *[half for pair in grads for half in pair], proj_weight],
        [shaped(part.shape) for part in merged],
        "attn_backward",
        far_outs=[shaped((2 * rows, features)) for rows in halves]
        + [shaped((2 * rows, width)) for rows in halves],
        copies=4 * count,
        scratch=[
            lanes(),
            lanes(),
            pltpu.VMEM((heads, HEAD_DIM, total), BF16),
            lanes(),
            lanes(),
            lanes(),
            lanes(F32),
            lanes(F32),
            pltpu.VMEM((heads, steps, 1, step), F32),
        ],
        limit=16,
    )


def split_at(bits, bit):
    place = len(bits) - 1 - bits.index(bit)
    stride = 1 << place
    return [index for index in range(1 << len(bits)) if not index & stride], stride


def weight_grads(queue, pairs, bits, cuts):
    blocks = 1 << len(bits)
    features = pairs[0][0][0].shape[1]
    widths = [rights[0].shape[1] for _, rights in pairs]
    each = features // blocks
    rows = sum(part.shape[0] for part in pairs[0][0])
    far, plan, scratch = [], [], []
    for number, (lefts, rights) in enumerate(pairs):
        for place, parts in enumerate((lefts, rights)):
            first = 0
            for part in parts:
                plan.append((len(far), 2 * number + place, first, part.shape[0]))
                far.append(part)
                first += part.shape[0]
            scratch.append(pltpu.VMEM((rows, parts[0].shape[1]), BF16))
    buffers = len(scratch)
    scratch.append(pltpu.VMEM((blocks, each, sum(widths)), BF16))
    outs, far_outs = [], []
    for columns, _, _ in cuts:
        outs += [shaped((blocks // 2, each, columns))] * 2
    if not cuts:
        far_outs.append(shaped((blocks, each, sum(widths))))

    def body(*refs):
        mine_refs, refs = refs[: len(cuts)], refs[len(cuts) :]
        sources, refs = refs[: len(far)], refs[len(far) :]
        out_refs, refs = refs[: len(outs)], refs[len(outs) :]
        sums_ref, *held = refs
        whole_ref = None if cuts else held.pop(0)
        full, done = held[buffers], held[buffers + 1]
        copies = [
            pltpu.make_async_copy(
                sources[source], held[buffer].at[pl.ds(first, count)], done.at[index]
            )
            for index, (source, buffer, first, count) in enumerate(plan)
        ]
        for copy in copies:
            copy.start()
        low = 0
        ones = jnp.ones((8, rows), BF16)
        for number, width in enumerate(widths):
            for copy, (_, buffer, _, _) in zip(copies, plan):
                if buffer // 2 == number:
                    copy.wait()
            left, right = held[2 * number][...], held[2 * number + 1][...]
            total = tn(left, right).astype(BF16)
            columns = slice(low, low + width)
            for block in range(blocks):
                full[block, :, columns] = total[block * each : (block + 1) * each]
            sums_ref[:, columns] = nn(ones, right)
            low += width
        low = 0
        for index, (width, bit, _) in enumerate(cuts):
            starts, stride = split_at(bits, bit)
            at = mine_refs[index][0] * stride
            for place, start in enumerate(starts):
                out_refs[2 * index][place] = full[start + at, :, low : low + width]
                out_refs[2 * index + 1][place] = full[start + stride - at, :, low : low + width]
            low += width
        if not cuts:
            whole = pltpu.make_async_copy(full, whole_ref, done.at[len(plan)])
            whole.start()
            whole.wait()

    found = queue.call(
        body,
        [],
        [*outs, shaped((8, sum(widths)), F32)],
        "weight_grads",
        scalars=[mine for _, _, mine in cuts],
        far=far,
        far_outs=far_outs,
        scratch=scratch,
        copies=len(plan) + 1,
        limit=20 if len(pairs) == 1 else 28,
    )
    if not cuts:
        return found[1], found[0]
    return list(zip(found[:-1:2], found[1:-1:2])), found[-1]


def halve(queue, kept, moved, mine, bits, bit):
    blocks, each, width = kept.shape
    out = shaped((blocks // 2, each, width))
    starts, stride = split_at(bits, bit)

    def body(mine_ref, kept_ref, moved_ref, next_ref, away_ref):
        at = mine_ref[0] * stride
        for place, out_ref in ((stride - at, away_ref), (at, next_ref)):
            for index, start in enumerate(starts):
                total = kept_ref[start + place].astype(F32) + moved_ref[start + place].astype(F32)
                out_ref[index] = total.astype(BF16)

    return queue.call(body, [kept, moved], [out, out], "halve", scalars=[mine])


def spread_mods(queue, me, columns, features):
    size, latents, blocks, each = columns.shape

    def body(me_ref, in_ref, out_ref, flat):
        for device in range(size):
            block = in_ref[jnp.bitwise_xor(device, me_ref[0])].astype(F32)
            for latent in range(latents):
                flat[latent, :, device * each : (device + 1) * each] = block[latent]
        for latent in range(latents):
            for part in range(6):
                rows = flat[latent, :, part * features : (part + 1) * features]
                for index in range(blocks):
                    out_ref[index, latent, part : part + 1, :] = rows[index : index + 1]

    return queue.call(
        body,
        [columns],
        [shaped((blocks, latents, 6, features), F32)],
        "spread_mods",
        scalars=[me],
        scratch=[pltpu.VMEM((latents, blocks, size * each), F32)],
    )[0]


def collect_sums(queue, sources, recipe, parts):
    features = sources[0].shape[1]
    count = -(-len(recipe) // 8) * 8
    counts = [part.shape[0] for part in parts]

    def body(*refs):
        part_refs, refs = refs[: len(parts)], refs[len(parts) :]
        out_ref, joined_ref = refs[-2:]
        for index, terms in enumerate(recipe):
            total = None
            for source, row in terms:
                term = refs[source][row : row + 1, :]
                total = term if total is None else total + term
            out_ref[index : index + 1, :] = total
        if count > len(recipe):
            out_ref[len(recipe) :, :] = jnp.zeros((count - len(recipe), features), F32)
        first = 0
        for part_ref, rows in zip(part_refs, counts):
            joined_ref[first : first + rows, :] = part_ref[...]
            first += rows

    outs = [shaped((count, features), F32), shaped((sum(counts), features))]
    return queue.call(body, [*parts, *sources], outs, "collect_sums")


def pack_mods(queue, me, own, moved, latents, blocks, size, features):
    each = 6 * features // size
    rows = own.shape[0]

    def body(me_ref, own_ref, moved_ref, out_ref, total_ref, flat):
        total = own_ref[...] + moved_ref[...]
        total_ref[...] = total
        for latent in range(latents):
            for index in range(blocks):
                for part in range(6):
                    row = (index * latents + latent) * 6 + part
                    flat[latent, index : index + 1, part * features : (part + 1) * features] = total[
                        row : row + 1
                    ]
        for device in range(size):
            for latent in range(latents):
                out_ref[jnp.bitwise_xor(device, me_ref[0]), latent] = flat[
                    latent, :, device * each : (device + 1) * each
                ].astype(BF16)

    return queue.call(
        body,
        [own, moved],
        [shaped((size, latents, blocks, each)), shaped((rows, features), F32)],
        "pack_mods",
        scalars=[me],
        scratch=[pltpu.VMEM((latents, blocks, 6 * features), F32)],
    )


def partners(size, bit):
    return [(index, index ^ bit) for index in range(size)]


def bits_of(size):
    bits = []
    while (1 << len(bits)) < size:
        bits.append(1 << len(bits))
    assert (1 << len(bits)) == size
    return bits


class Links:
    def __init__(self, dp_size, tensor_size):
        self.dp_size = dp_size
        self.tensor_size = tensor_size
        self.dp_bits = bits_of(dp_size)
        me = lax.axis_index("dp")
        self.me = me.reshape(1)
        self.core = lax.rem(lax.axis_index("tensor"), 2).reshape(1)
        self.mine = {bit: lax.rem(me // bit, 2).reshape(1) for bit in self.dp_bits}

    def swap(self, value):
        return lax.ppermute(value, "tensor", partners(self.tensor_size, 1))

    def cross(self, value):
        return lax.ppermute(value, "tensor", partners(self.tensor_size, 2))

    def dp_move(self, value, bit):
        return lax.ppermute(value, "dp", partners(self.dp_size, bit))

    def gather_relative(self, value):
        held = value[None]
        for bit in self.dp_bits:
            held = jnp.concatenate([held, self.dp_move(held, bit)], axis=0)
        return held

    def exchange_relative(self, value, total=None):
        held = value
        for bit in reversed(self.dp_bits):
            split = held.reshape((self.dp_size // (2 * bit), 2, bit) + held.shape[1:])
            away = split[:, 1]
            if total is None:
                moved = self.dp_move(away, bit)
            else:
                sent = jnp.concatenate([away.astype(F32).reshape(-1), total])
                came = self.dp_move(sent, bit)
                moved = came[: away.size].reshape(away.shape).astype(held.dtype)
                total = total + came[away.size :]
            held = jnp.stack([split[:, 0], moved], axis=1).reshape(held.shape)
        return held if total is None else (held, total)

    def sum_relative(self, value):
        held = value
        for bit in reversed(self.dp_bits):
            moved = self.dp_move(held[bit:].astype(BF16), bit)
            held = held[:bit].astype(F32) + moved.astype(F32)
        return held[0]


class ScatterSum:
    def __init__(self, queue, links, kept, away, order):
        self.queue, self.links, self.kept = queue, links, kept
        self.order = list(order)
        self.open = sorted(self.order, reverse=True)
        self.send(away)

    def send(self, away):
        bit = self.order.pop(0)
        self.open.remove(bit)
        self.moved = self.links.dp_move(away, bit)

    def step(self):
        if self.order:
            bit = self.order[0]
            self.kept, away = halve(
                self.queue, self.kept, self.moved, self.links.mine[bit], self.open, bit
            )
            self.send(away)


def last_sums(queue, parts):
    shapes = [part.kept.shape[1:] for part in parts]

    def body(*refs):
        for index in range(len(parts)):
            kept_ref, moved_ref = refs[2 * index : 2 * index + 2]
            total = kept_ref[0].astype(F32) + moved_ref[0].astype(F32)
            refs[2 * len(parts) + index][...] = total

    operands = [value for part in parts for value in (part.kept, part.moved)]
    return queue.call(body, operands, [shaped(shape, F32) for shape in shapes], "last_sums")


def emit_wide(queue, parts, wide):
    each = parts[0].shape[0]

    def body(up_ref, down_ref, both_ref, up_out, down_out):
        up_out[0] = up_ref[...]
        down_out[0] = down_ref[...]
        up_out[1] = both_ref[:, :wide].astype(F32)
        down_out[1] = both_ref[:, wide:].astype(F32)

    features = parts[1].shape[1]
    outs = [shaped((2, each, wide), F32), shaped((2, each, features), F32)]
    return queue.call(body, parts, outs, "emit_wide")


def emit_attention(queue, encoder, decoder, local):
    each = decoder.shape[0]

    def body(kept_ref, moved_ref, dec_ref, proj_ref, qkv_ref):
        total = kept_ref[0].astype(F32) + moved_ref[0].astype(F32)
        for index, value in enumerate((total, dec_ref[...])):
            proj_ref[index] = value[:, :local]
            for part in range(3):
                qkv_ref[index, part] = value[:, (part + 1) * local : (part + 2) * local]

    outs = [shaped((2, each, local), F32), shaped((2, 3, each, local), F32)]
    return queue.call(body, [encoder.kept, encoder.moved, decoder], outs, "emit_attention")


def reduced(queue, links, pairs):
    whole, sums = weight_grads(queue, pairs, sorted(links.dp_bits, reverse=True), [])
    flat = whole.reshape(-1, whole.shape[-1])
    return lax.psum_scatter(flat, "dp", scatter_dimension=0, tiled=True), sums


def scatter_sums(queue, links, pairs, cuts):
    bits = sorted(links.dp_bits, reverse=True)
    found, sums = weight_grads(
        queue, pairs, bits, [(columns, order[0], links.mine[order[0]]) for columns, order in cuts]
    )
    pieces = [
        ScatterSum(queue, links, kept, away, order)
        for (kept, away), (_, order) in zip(found, cuts)
    ]
    return pieces, sums


class Weights:
    def __init__(self, qkv, proj, up, down, small, mods):
        self.qkv, self.proj, self.up, self.down = qkv, proj, up, down
        self.small, self.mods = small, mods


class Chunk:
    def __init__(self, queue, links, weights, block, latent, family):
        self.queue, self.links, self.weights = queue, links, weights
        self.block, self.latent, self.at = block, latent, (block, latent)
        self.family = family
        family.append(self)

    def enter(self, stream, normed):
        self.x = stream
        self.normed_attn = (normed, self.links.swap(normed))

    def qkv(self):
        w = self.weights
        self.merged, self.normed_attn_rows = qkv_forward(
            self.queue, *self.normed_attn, w.qkv, w.small, self.block
        )

    def attention(self):
        merged = [chunk.merged for chunk in self.family]
        self.normer, own, other, self.attended_rows = attn_forward(
            self.queue, self.merged, merged, self.weights.proj, self.block
        )
        self.part = (own, self.links.swap(other))

    def near(self):
        near = near_sum(self.queue, *self.part)
        self.sum = (near, self.links.cross(near))

    def merge(self):
        w = self.weights
        self.branch_attn = self.sum
        self.middle, normed = merge_attn(
            self.queue, self.x, *self.branch_attn, w.small, w.mods, self.at
        )
        self.normed_mlp = (normed, self.links.swap(normed))

    def mlp(self):
        w = self.weights
        own, other, self.slope, self.normed_mlp_rows, self.active_rows = mlp_forward(
            self.queue, *self.normed_mlp, w.up, w.down, w.small, self.block
        )
        self.part = (own, self.links.swap(other))

    def start_back(self, d_out, d_branch):
        self.d_out = d_out
        self.d_branch_mlp = (d_branch, self.links.swap(d_branch))

    def mlp_back(self):
        w = self.weights
        own, other, self.d_branch_mlp_rows, self.d_hidden_rows = mlp_backward(
            self.queue, *self.d_branch_mlp, self.slope, w.up, w.down, self.block
        )
        self.part = (own, self.links.swap(other))

    def merge_back(self):
        w = self.weights
        branch = ([self.branch_attn], w.small, PROJ_BIAS + self.block, self.at, GATE_ATTN)
        self.mlp_sums, self.d_middle, grad = ln_back(
            self.queue, *self.sum, self.middle, self.d_out, w.mods, self.at, SCALE_MLP, branch
        )
        self.d_branch_attn = (grad, self.links.swap(grad))

    def attention_back(self):
        family = self.family
        grads = attn_backward(
            self.queue,
            [chunk.merged for chunk in family],
            [chunk.normer for chunk in family],
            [chunk.d_branch_attn for chunk in family],
            self.weights.proj,
            self.block,
        )
        count = len(family)
        for index, chunk in enumerate(family):
            chunk.d_qkv, chunk.d_branch_attn_rows, chunk.d_qkv_rows = grads[index::count]

    def qkv_back(self):
        own, other = qkv_backward(self.queue, self.d_qkv, self.weights.qkv, self.block)
        self.part = (own, self.links.swap(other))

    def leave_back(self, branch=None, narrow=False):
        w = self.weights
        self.attn_sums, *rest = ln_back(
            self.queue,
            *self.sum,
            self.x,
            self.d_middle,
            w.mods,
            self.at,
            SCALE_ATTN,
            branch,
            narrow,
        )
        return rest


def rows_of(chunks, name):
    return [getattr(chunk, name + "_rows") for chunk in chunks]


def on_device(dp_size, tensor_size, *arguments):
    (
        tokens_long,
        tokens_short,
        cond_long,
        cond_short,
        perm_long,
        perm_short,
        ada_weight,
        ada_bias,
        qkv_weight,
        qv_bias,
        proj_weight,
        proj_bias,
        up_weight,
        up_bias,
        down_weight,
        down_bias,
        mask_token,
        cot_long,
        cot_short,
    ) = arguments
    assert tokens_long.shape[0] == 1 and tokens_short.shape[0] == 1
    queue = Queue()
    links = Links(dp_size, tensor_size)
    core = links.core
    features = tokens_long.shape[2]
    wide = up_weight.shape[2]
    local = qv_bias.shape[2]
    tokens = (tokens_long[0], tokens_short[0])
    cots = (cot_long[0], cot_short[0])
    perms = (perm_long, perm_short)
    lengths = tuple(rows.shape[0] for rows in tokens)
    kept = tuple(length // 2 for length in lengths)

    cond = jnp.concatenate([cond_long, cond_short]).astype(F32)
    acts = links.gather_relative(jax.nn.silu(cond).astype(BF16))
    flat_acts = acts.reshape(-1, features)
    columns = jnp.einsum("nd,ldm->nlm", flat_acts, ada_weight, preferred_element_type=F32)
    columns = (columns + ada_bias.astype(F32)[None]).astype(BF16)
    columns = links.exchange_relative(columns.reshape((dp_size, 2) + columns.shape[1:]))

    table_width = max(features, wide, 3 * local)

    def padded(rows):
        return jnp.pad(rows.astype(F32), ((0, 0), (0, table_width - rows.shape[1])))

    qkv_bias = jnp.concatenate(
        [qv_bias[:, 0], jnp.zeros_like(qv_bias[:, 0]), qv_bias[:, 1]], axis=1
    )
    small = jnp.concatenate([padded(proj_bias), padded(down_bias), padded(up_bias), padded(qkv_bias)])

    long_half, short_half = kept[0] // 2, kept[1] // 2
    quarter = long_half // 2
    enc_rows = [
        Rows((0, long_half, quarter)),
        Rows((quarter, long_half, quarter)),
        Rows((0, short_half, short_half)),
    ]
    table_places = [Rows((0, long_half, long_half)), Rows((0, short_half, short_half))]
    masked_places = [
        Rows((kept[0], long_half, long_half)),
        Rows((kept[1], short_half, short_half)),
    ]
    dec_rows = [
        table_places[0],
        masked_places[0],
        Rows((0, short_half, short_half), (kept[1], short_half, short_half)),
    ]
    enc_latents, dec_latents = (0, 0, 1), (0, 0, 1)

    streams = [
        gather_rows(queue, core, perms[latent], tokens[latent], rows, F32)
        for latent, rows in zip(enc_latents, enc_rows)
    ]
    mods = spread_mods(queue, links.me, columns, features)
    weights = Weights(
        jnp.transpose(qkv_weight, (0, 2, 3, 1)).reshape(2, 3 * local, features),
        proj_weight,
        up_weight,
        down_weight,
        small,
        mods,
    )
    families = {(block, latent): [] for block in (0, 1) for latent in (0, 1)}

    def chunks_of(block, latents):
        return [
            Chunk(queue, links, weights, block, latent, families[block, latent])
            for latent in latents
        ]

    encoder = chunks_of(0, enc_latents)
    decoder = chunks_of(1, dec_latents)
    ea, eb, es = encoder
    dk, dm, dt = decoder

    for chunk, stream in zip(encoder, streams):
        chunk.enter(stream, ln_open(queue, stream, mods, chunk.at))
    for chunk in encoder:
        chunk.qkv()
    ea.attention()
    eb.attention()
    ea.near()
    es.attention()
    eb.near()
    es.near()
    perms_later, filler, cots_later = queue.tie(perms, mask_token, cots)
    filler = filler.astype(F32)[None]
    waves = []
    for length in lengths:
        side = math.isqrt(length)
        quarter_wave = features // 4
        frequency = 1.0 / 10000.0 ** (jnp.arange(quarter_wave, dtype=F32) / quarter_wave)
        angle = jnp.arange(side, dtype=jnp.int32).astype(F32)[:, None] * frequency[None, :]
        waves.append(jnp.concatenate([jnp.sin(angle), jnp.cos(angle)], axis=1))
    masked = table_rows(queue, core, perms_later[0], waves[0], masked_places[0], filler)
    dm.enter(masked, ln_open(queue, masked, mods, dm.at))
    ea.merge()
    dm.qkv()
    ea.mlp()
    eb.merge()
    ea.near()
    es.merge()
    eb.mlp()
    es.mlp()
    eb.near()
    es.near()
    table_long = table_rows(queue, core, perms_later[0], waves[0], table_places[0])
    table_short = table_rows(queue, core, perms_later[1], waves[1], table_places[1])
    masked_short = table_rows(queue, core, perms_later[1], waves[1], masked_places[1], filler)
    d_out = [
        gather_rows(queue, core, perms_later[latent], cots_later[latent], rows, BF16)
        for latent, rows in zip(dec_latents, dec_rows)
    ]
    first_sums = []
    for chunk, grad in zip(decoder, d_out):
        d_branch, sums = first_grad(queue, grad, mods, chunk.at)
        first_sums.append(sums)
        chunk.start_back(grad, d_branch)

    pieces = [(chunk.middle, *chunk.sum) for chunk in encoder]
    for chunk in encoder:
        chunk.branch_mlp = chunk.sum
    dk.enter(*merge_mlp(queue, pieces[:2], small, mods, (0, 0), table_long, None))
    dt.enter(*merge_mlp(queue, pieces[2:], small, mods, (0, 1), table_short, masked_short))
    dk.qkv()
    dk.attention()
    dt.qkv()
    dk.near()
    dm.attention()
    dt.attention()
    dm.near()
    dt.near()
    dk.merge()
    dk.mlp()
    dm.merge()
    forward = {dk: dk.part}
    dk.mlp_back()
    dm.mlp()
    dk.near()
    forward[dm] = dm.part
    dm.mlp_back()
    dt.merge()
    dm.near()
    dt.mlp()
    forward[dt] = dt.part
    dt.mlp_back()
    dt.near()

    y_first, z_first = list(links.dp_bits), list(links.dp_bits)
    if len(z_first) > 1:
        z_first[0], z_first[1] = z_first[1], z_first[0]

    def wide_pairs(chunks):
        return [
            (rows_of(chunks, "normed_mlp"), rows_of(chunks, "d_hidden")),
            (rows_of(chunks, "d_branch_mlp"), rows_of(chunks, "active")),
        ]

    def attention_pairs(chunks):
        return [
            (rows_of(chunks, "d_branch_attn"), rows_of(chunks, "attended")),
            (rows_of(chunks, "normed_attn"), rows_of(chunks, "d_qkv")),
        ]

    sums_there = {}

    def forward_sum(chunk):
        near = near_sum(queue, *forward[chunk])
        sums_there[chunk] = (near, links.cross(near))

    def finished(*chunks):
        return finish(
            queue,
            [
                (chunk.middle, *sums_there[chunk], d_out[decoder.index(chunk)], chunk.at)
                for chunk in chunks
            ],
            small,
            mods,
        )

    dk.merge_back()
    dec_wide, dec_wide_sums = reduced(queue, links, wide_pairs(decoder))
    dm.merge_back()
    forward_sum(dk)
    forward_sum(dm)
    dm.attention_back()
    decoded_long, long_sums = finished(dk, dm)
    decoded_other = links.swap(decoded_long)
    dk.qkv_back()
    dm.qkv_back()
    dk.near()
    dm.near()
    dt.merge_back()
    dt.attention_back()
    dt.qkv_back()
    dt.near()
    result_long = place_rows(
        queue, core, perms_later[0], decoded_long, decoded_other, dec_rows[:2], 0
    )
    enc_branch = (small, DOWN_BIAS, (0, 0), GATE_MLP)
    short_branch = (small, DOWN_BIAS, (0, 1), GATE_MLP)
    d_a, d_b, grad_a, grad_b = dk.leave_back(([ea.branch_mlp, eb.branch_mlp], *enc_branch))
    ea.start_back(d_a, grad_a)
    eb.start_back(d_b, grad_b)

    ea.mlp_back()
    eb.mlp_back()
    ea.near()
    eb.near()
    (dec_attn,), dec_attn_sums = scatter_sums(
        queue, links, attention_pairs(decoder), [(4 * local, y_first)]
    )
    dm.leave_back()
    d_short, grad_short = dt.leave_back(([es.branch_mlp], *short_branch))
    es.start_back(d_short, grad_short)
    es.mlp_back()
    es.near()
    ea.merge_back()
    (enc_up, enc_down), enc_wide_sums = scatter_sums(
        queue, links, wide_pairs(encoder), [(wide, y_first), (wide, z_first)]
    )
    dec_attn.step()
    eb.merge_back()
    forward_sum(dt)
    ea.attention_back()
    ea.qkv_back()
    eb.qkv_back()
    ea.near()
    eb.near()
    enc_up.step()
    enc_down.step()
    es.merge_back()
    es.attention_back()
    es.qkv_back()
    es.near()
    (enc_attn,), enc_attn_sums = scatter_sums(
        queue, links, attention_pairs(encoder), [(4 * local, y_first)]
    )
    enc_up.step()
    enc_down.step()
    own_tokens = []
    for chunk in (ea, eb, es):
        own_tokens += chunk.leave_back(narrow=True)
    decoded_short, short_sums = finished(dt)
    decoded_other = links.swap(decoded_short)
    dec_attn.step()

    sources, recipe = [], []

    def row(array, index):
        for place, source in enumerate(sources):
            if source is array:
                return place, index
        sources.append(array)
        return len(sources) - 1, index

    for block, chunks in ((0, encoder), (1, decoder)):
        for latent in (0, 1):
            members = [chunk for chunk in chunks if chunk.latent == latent]
            if block == 0:
                gates = [row((dk, dt)[latent].attn_sums, 2)]
            else:
                gates = [row((long_sums, short_sums)[latent], latent)]
            recipe += [
                [row(chunk.attn_sums, 1) for chunk in members],
                [row(chunk.attn_sums, 0) for chunk in members],
                [row(chunk.mlp_sums, 2) for chunk in members],
                [row(chunk.mlp_sums, 1) for chunk in members],
                [row(chunk.mlp_sums, 0) for chunk in members],
                gates,
            ]
    recipe += [
        [row(chunk.mlp_sums, 3) for chunk in encoder],
        [row(chunk.mlp_sums, 3) for chunk in decoder],
        [row(chunk.attn_sums, 3) for chunk in (dk, dt)],
        [row(sums, 0) for sums in first_sums],
        [row(chunk.attn_sums, 4) for chunk in (dm, dt)],
    ]
    own_sums, joined = collect_sums(queue, sources, recipe, own_tokens)
    enc_attn.step()
    enc_up, enc_down = last_sums(queue, [enc_up, enc_down])
    up_grad, down_grad = emit_wide(queue, [enc_up, enc_down, dec_wide], wide)
    packed, all_sums = pack_mods(
        queue, links.me, own_sums, links.swap(own_sums), 2, 2, dp_size, features
    )
    totals = jnp.concatenate(
        [all_sums[24:29].reshape(-1), enc_wide_sums[0, :wide], dec_wide_sums[0, :wide]]
        + [
            sums[0, first : first + local]
            for sums in (enc_attn_sums, dec_attn_sums)
            for first in (local, 3 * local)
        ]
    )
    mine, totals = links.exchange_relative(packed, totals)
    mine, totals, enc_attn.moved = lax.optimization_barrier((mine, totals, enc_attn.moved))
    enc_attn.step()
    mine = queue.tie(mine)
    result_short = place_rows(
        queue, core, perms_later[1], decoded_short, decoded_other, dec_rows[2:], 0
    )
    flat_mine = mine.reshape((-1,) + mine.shape[2:])
    grad_ada = jnp.einsum("nd,nlm->ldm", flat_acts, flat_mine, preferred_element_type=F32)
    grad_ada_bias = jnp.sum(flat_mine.astype(F32), axis=0)
    d_acts = jnp.einsum("nlm,ldm->nd", flat_mine, ada_weight, preferred_element_type=F32)
    d_act = links.sum_relative(d_acts.reshape(dp_size, 2, features))
    gate = jax.nn.sigmoid(cond)
    d_cond = (d_act * gate * (1.0 + cond * (1.0 - gate))).astype(BF16)

    proj_out = totals[: 2 * features].reshape(2, features)
    down_out = totals[2 * features : 4 * features].reshape(2, features)
    mask_out = totals[4 * features : 5 * features]
    first = 5 * features
    up_out = totals[first : first + 2 * wide].reshape(2, wide)
    first += 2 * wide
    qv_out = totals[first : first + 4 * local].reshape(2, 2, local)

    joined_other = links.swap(joined)
    d_tokens = (
        place_rows(queue, core, perms_later[0], joined, joined_other, enc_rows[:2], 0),
        place_rows(queue, core, perms_later[1], joined, joined_other, enc_rows[2:], long_half),
    )
    (dec_attn,) = last_sums(queue, [dec_attn])
    proj_grad, qkv_grad = emit_attention(queue, enc_attn, dec_attn, local)

    return (
        result_long[None],
        result_short[None],
        d_tokens[0][None],
        d_tokens[1][None],
        d_cond[:1],
        d_cond[1:],
        grad_ada,
        grad_ada_bias,
        jnp.transpose(qkv_grad, (0, 2, 1, 3)),
        qv_out,
        jnp.transpose(proj_grad, (0, 2, 1)),
        proj_out,
        up_grad,
        up_out,
        jnp.transpose(down_grad, (0, 2, 1)),
        down_out,
        mask_out,
    )


def solution(mesh):
    in_specs = (
        P("dp", None, None),
        P("dp", None, None),
        P("dp", None),
        P("dp", None),
        P("dp", None),
        P("dp", None),
        P(None, None, "dp"),
        P(None, "dp"),
        P(None, None, None, "tensor"),
        P(None, None, "tensor"),
        P(None, "tensor", None),
        P(),
        P(None, None, "tensor"),
        P(None, "tensor"),
        P(None, "tensor", None),
        P(),
        P(),
        P("dp", None, None),
        P("dp", None, None),
    )
    out_specs = (
        P("dp", None, None),
        P("dp", None, None),
        P("dp", None, None),
        P("dp", None, None),
        P("dp", None),
        P("dp", None),
        P(None, None, "dp"),
        P(None, "dp"),
        P(None, "dp", None, "tensor"),
        P(None, None, "tensor"),
        P(None, "tensor", "dp"),
        P(),
        P(None, "dp", "tensor"),
        P(None, "tensor"),
        P(None, "tensor", "dp"),
        P(),
        P(),
    )

    def step(*arguments):
        return on_device(mesh.shape["dp"], mesh.shape["tensor"], *arguments)

    return jax.shard_map(
        step, mesh=mesh, in_specs=in_specs, out_specs=out_specs, check_vma=False
    )
```

```python
import math

import jax
import jax.numpy as jnp
from jax import lax
from jax.experimental import pallas as pl
from jax.experimental.pallas import tpu as pltpu
from jax.sharding import PartitionSpec as P

HEAD_DIM = 72
EPSILON = 1e-06
BF16 = jnp.bfloat16
F32 = jnp.float32
MIB = 1 << 20
SCALING = HEAD_DIM**-0.5
EXPONENT = SCALING * math.log2(math.e)
GELU_A = math.sqrt(2.0 / math.pi)
GELU_B = 0.044715

SHIFT_ATTN, SCALE_ATTN, GATE_ATTN, SHIFT_MLP, SCALE_MLP, GATE_MLP = range(6)
PROJ_BIAS, DOWN_BIAS, UP_BIAS, QKV_BIAS = 0, 2, 4, 6


def nn(left, right):
    return lax.dot_general(left, right, (((1,), (0,)), ((), ())), preferred_element_type=F32)


def nt(left, right):
    return lax.dot_general(left, right, (((1,), (1,)), ((), ())), preferred_element_type=F32)


def tn(left, right):
    return lax.dot_general(left, right, (((0,), (0,)), ((), ())), preferred_element_type=F32)


def shaped(shape, dtype=BF16):
    return jax.ShapeDtypeStruct(shape, dtype)


COSTS = {
    "gather_rows": 0.8, "ln_open": 0.4, "near_sum": 0.4, "merge_attn": 0.6, "merge_mlp": 0.6,
    "finish": 1.0, "first_grad": 0.5, "qkv_forward": 1.2, "qkv_backward": 0.0, "mlp_forward": 3.5,
    "mlp_backward": 3.0, "ln_back": 1.2, "attn_forward": 0.0, "attn_backward": 0.0,
    "weight_grads": 6.5, "halve": 1.5, "place_rows": 3.0, "table_rows": 1.0,
}


class Queue:
    def __init__(self):
        self.token = jnp.zeros((8, 128), F32)

    def tie(self, *values):
        *values, self.token = lax.optimization_barrier((*values, self.token))
        return values[0] if len(values) == 1 else tuple(values)

    def call(
        self, body, operands, outs, name, scalars=(), far=(), far_outs=(), scratch=(), copies=0, limit=10
    ):
        fast = pl.BlockSpec(memory_space=pltpu.VMEM)
        small = pl.BlockSpec(memory_space=pltpu.SMEM)
        slow = pl.BlockSpec(memory_space=pltpu.HBM)
        last = len(scalars) + len(far) + len(operands) + len(outs) + len(far_outs)

        def whole(token_ref, *refs):
            body(*refs[:last], *refs[last + 1 :])
            refs[last][...] = token_ref[...]

        *results, self.token = pl.pallas_call(
            whole,
            in_specs=[fast] + [small] * len(scalars) + [slow] * len(far) + [fast] * len(operands),
            out_specs=[fast] * len(outs) + [slow] * len(far_outs) + [fast],
            out_shape=[
                *outs,
                *[pltpu.HBM(out.shape, out.dtype) for out in far_outs],
                shaped((8, 128), F32),
            ],
            scratch_shapes=list(scratch)
            + ([pltpu.SemaphoreType.DMA((copies,))] if copies else []),
            cost_estimate=pl.CostEstimate(
                flops=int(COSTS.get(name, 1.0) * 1.15e9), transcendentals=0, bytes_accessed=1000
            ),
            compiler_params=pltpu.CompilerParams(vmem_limit_bytes=limit * MIB),
            name=name,
        )(
            pltpu.with_memory_space_constraint(self.token, pltpu.VMEM),
            *scalars,
            *[pltpu.with_memory_space_constraint(value, pltpu.HBM) for value in far],
            *[pltpu.with_memory_space_constraint(value, pltpu.VMEM) for value in operands],
        )
        return results


def copy_rows(sources, target, semaphores, first=0):
    found, row = [], 0
    for index, source in enumerate(sources):
        count = source.shape[0]
        copy = pltpu.make_async_copy(
            source, target.at[pl.ds(row, count)], semaphores.at[first + index]
        )
        copy.start()
        found.append(copy)
        row += count
    return found


def normed_of(values):
    center = values - jnp.mean(values, axis=-1, keepdims=True)
    spread = jnp.mean(center * center, axis=-1, keepdims=True)
    scale = lax.rsqrt(spread + EPSILON)
    return center * scale, scale


def modulate(values, mods_ref, at, scale_part, shift_part):
    block, latent = at
    scale = mods_ref[block, latent, scale_part : scale_part + 1, :]
    shift = mods_ref[block, latent, shift_part : shift_part + 1, :]
    return (normed_of(values)[0] * (1.0 + scale) + shift).astype(BF16)


def branch_of(near_ref, far_ref, small_ref, row, features):
    return (
        near_ref[...].astype(F32)
        + far_ref[...].astype(F32)
        + small_ref[row : row + 1, :features]
    )


class Rows:
    def __init__(self, *spans):
        self.spans = spans
        self.count = sum(span[2] for span in spans)

    def places(self, perm_ref, core, other=False):
        found = []
        for first, stride, count in self.spans:
            low = perm_ref[:, first : first + count]
            high = perm_ref[:, first + stride : first + stride + count]
            found.append(jnp.where((core == 1) != other, high, low))
        return found[0] if len(found) == 1 else jnp.concatenate(found, axis=1)


def pick_columns(places, length):
    index = lax.broadcasted_iota(jnp.int32, (length, places.shape[1]), 0)
    return (index == places).astype(F32).astype(BF16)


def gather_rows(queue, core, perm, source, rows, dtype):
    length, features = source.shape

    def body(core_ref, perm_ref, source_ref, out_ref):
        pick = pick_columns(rows.places(perm_ref, core_ref[0]), length)
        out_ref[...] = tn(pick, source_ref[...]).astype(dtype)

    outs = [shaped((rows.count, features), dtype)]
    return queue.call(body, [perm, source], outs, "gather_rows", scalars=[core])[0]


def place_rows(queue, core, perm, own, other, rows, first):
    length = perm.shape[1]
    features = own.shape[1]
    last = first + sum(chunk.count for chunk in rows)

    def body(core_ref, perm_ref, own_ref, other_ref, out_ref):
        places = [
            chunk.places(perm_ref, core_ref[0], other) for other in (False, True) for chunk in rows
        ]
        values = jnp.concatenate([own_ref[first:last, :], other_ref[first:last, :]], axis=0)
        pick = pick_columns(jnp.concatenate(places, axis=1), length)
        out_ref[...] = nn(pick, values).astype(BF16)

    outs = [shaped((length, features))]
    return queue.call(
        body, [perm, own, other], outs, "place_rows", scalars=[core], limit=12
    )[0]


def table_rows(queue, core, perm, waves, rows, filler=None):
    side, half = waves.shape

    def body(core_ref, perm_ref, waves_ref, *refs):
        places = rows.places(perm_ref, core_ref[0])
        index = lax.broadcasted_iota(jnp.int32, (side, places.shape[1]), 0)
        row_pick = ((places >= index * side) & (places < (index + 1) * side)).astype(F32)
        row = jnp.sum(row_pick * index.astype(F32), axis=0, keepdims=True)
        col_pick = (index.astype(F32) == places.astype(F32) - row * side).astype(F32)
        for low, pick in ((0, row_pick), (half, col_pick)):
            out = lax.dot_general(
                pick,
                waves_ref[...],
                (((0,), (0,)), ((), ())),
                precision=lax.Precision.HIGHEST,
                preferred_element_type=F32,
            )
            if filler is not None:
                out = out + refs[0][:, low : low + half]
            refs[-1][:, low : low + half] = out

    operands = [perm, waves] + ([] if filler is None else [filler])
    outs = [shaped((rows.count, 2 * half), F32)]
    return queue.call(body, operands, outs, "table_rows", scalars=[core])[0]


def ln_open(queue, stream, mods, at):
    def body(x_ref, mods_ref, out_ref):
        out_ref[...] = modulate(x_ref[...], mods_ref, at, SCALE_ATTN, SHIFT_ATTN)

    return queue.call(body, [stream, mods], [shaped(stream.shape)], "ln_open")[0]


def near_sum(queue, own, moved):
    def body(own_ref, moved_ref, out_ref):
        out_ref[...] = (own_ref[...].astype(F32) + moved_ref[...].astype(F32)).astype(BF16)

    return queue.call(body, [own, moved], [shaped(own.shape)], "near_sum")[0]


def merge_attn(queue, stream, near, far, small, mods, at):
    features = stream.shape[1]
    block, latent = at

    def body(x_ref, near_ref, far_ref, small_ref, mods_ref, mid_ref, out_ref):
        branch = branch_of(near_ref, far_ref, small_ref, PROJ_BIAS + block, features)
        middle = x_ref[...] + mods_ref[block, latent, GATE_ATTN : GATE_ATTN + 1, :] * branch
        mid_ref[...] = middle
        out_ref[...] = modulate(middle, mods_ref, at, SCALE_MLP, SHIFT_MLP)

    outs = [shaped(stream.shape, F32), shaped(stream.shape)]
    return queue.call(body, [stream, near, far, small, mods], outs, "merge_attn")


def merge_mlp(queue, pieces, small, mods, at, table, tail):
    features = table.shape[1]
    counts = [piece[0].shape[0] for piece in pieces]
    block, latent = at
    total = sum(counts) + (0 if tail is None else tail.shape[0])
    following = (block + 1, latent)

    def body(table_ref, small_ref, mods_ref, *refs):
        x_ref, out_ref = refs[-2:]
        gate = mods_ref[block, latent, GATE_MLP : GATE_MLP + 1, :]
        first = 0
        for index, count in enumerate(counts):
            mid_ref, near_ref, far_ref = refs[3 * index : 3 * index + 3]
            branch = branch_of(near_ref, far_ref, small_ref, DOWN_BIAS + block, features)
            stream = mid_ref[...] + gate * branch + table_ref[first : first + count, :]
            x_ref[first : first + count, :] = stream
            out_ref[first : first + count, :] = modulate(
                stream, mods_ref, following, SCALE_ATTN, SHIFT_ATTN
            )
            first += count
        if tail is not None:
            stream = refs[3 * len(counts)][...]
            x_ref[first:, :] = stream
            out_ref[first:, :] = modulate(stream, mods_ref, following, SCALE_ATTN, SHIFT_ATTN)

    operands = [table, small, mods] + [part for piece in pieces for part in piece]
    operands += [] if tail is None else [tail]
    outs = [shaped((total, features), F32), shaped((total, features))]
    return queue.call(body, operands, outs, "merge_mlp")


def finish(queue, parts, small, mods):
    counts = [part[0].shape[0] for part in parts]
    features = parts[0][0].shape[1]

    def body(small_ref, mods_ref, *refs):
        out_ref, sums_ref = refs[-2:]
        sums_ref[...] = jnp.zeros_like(sums_ref)
        first = 0
        for index, count in enumerate(counts):
            mid_ref, near_ref, far_ref, d_ref = refs[4 * index : 4 * index + 4]
            block, latent = parts[index][4]
            branch = branch_of(near_ref, far_ref, small_ref, DOWN_BIAS + block, features)
            gate = mods_ref[block, latent, GATE_MLP : GATE_MLP + 1, :]
            out_ref[first : first + count, :] = (mid_ref[...] + gate * branch).astype(BF16)
            total = jnp.sum(d_ref[...].astype(F32) * branch, axis=0, keepdims=True)
            sums_ref[latent : latent + 1, :] += total
            first += count

    outs = [shaped((sum(counts), features)), shaped((8, features), F32)]
    operands = [small, mods] + [value for part in parts for value in part[:4]]
    return queue.call(body, operands, outs, "finish")


def first_grad(queue, d_out, mods, at):
    features = d_out.shape[1]
    block, latent = at

    def body(d_ref, mods_ref, out_ref, sums_ref):
        gate = mods_ref[block, latent, GATE_MLP : GATE_MLP + 1, :]
        grad = (gate * d_ref[...].astype(F32)).astype(BF16)
        out_ref[...] = grad
        total = jnp.sum(grad.astype(F32), axis=0, keepdims=True)
        sums_ref[...] = jnp.broadcast_to(total, (8, features))

    outs = [shaped(d_out.shape), shaped((8, features), F32)]
    return queue.call(body, [d_out, mods], outs, "first_grad")


def qkv_forward(queue, own, other, weight, small, block):
    rows, features = own.shape
    width = weight.shape[1]

    def body(own_ref, other_ref, w_ref, small_ref, out_ref, rows_ref, done):
        copies = copy_rows([own_ref, other_ref], rows_ref, done)
        bias = small_ref[QKV_BIAS + block : QKV_BIAS + block + 1, :width]
        both = jnp.concatenate([own_ref[...], other_ref[...]], axis=0)
        out = (nt(both, w_ref[block]) + bias).astype(BF16)
        out_ref[0] = out[:rows]
        out_ref[1] = out[rows:]
        for copy in copies:
            copy.wait()

    return queue.call(
        body,
        [own, other, weight, small],
        [shaped((2, rows, width))],
        "qkv_forward",
        far_outs=[shaped((2 * rows, features))],
        copies=2,
    )


def qkv_backward(queue, grads, weight, block):
    _, rows, _ = grads.shape
    features = weight.shape[2]

    def body(g_ref, w_ref, own_ref, other_ref):
        both = jnp.concatenate([g_ref[0], g_ref[1]], axis=0)
        out = nn(both, w_ref[block]).astype(BF16)
        own_ref[...] = out[:rows]
        other_ref[...] = out[rows:]

    outs = [shaped((rows, features)), shaped((rows, features))]
    return queue.call(body, [grads, weight], outs, "qkv_backward")


def mlp_forward(queue, own, other, up_weight, down_weight, small, block):
    rows, features = own.shape
    wide = up_weight.shape[2]

    def body(
        own_ref, other_ref, up_ref, down_ref, small_ref,
        own_out, other_out, slope_ref, rows_ref, act_ref, act_s, done,
    ):
        copies = copy_rows([own_ref, other_ref], rows_ref, done)
        bias = small_ref[UP_BIAS + block : UP_BIAS + block + 1, :wide]
        both = jnp.concatenate([own_ref[...], other_ref[...]], axis=0)
        hidden = nn(both, up_ref[block]) + bias
        squared = hidden * hidden
        bent = jnp.tanh(GELU_A * hidden * (1.0 + GELU_B * squared))
        half = 0.5 + 0.5 * bent
        act_s[...] = (hidden * half).astype(BF16)
        slope = half + 0.5 * hidden * (1.0 - bent * bent) * (
            GELU_A + 3.0 * GELU_A * GELU_B * squared
        )
        slope_ref[...] = slope.astype(BF16)
        copies += copy_rows([act_s], act_ref, done, 2)
        out = nn(act_s[...], down_ref[block]).astype(BF16)
        own_out[...] = out[:rows]
        other_out[...] = out[rows:]
        for copy in copies:
            copy.wait()

    full = shaped((2 * rows, wide))
    return queue.call(
        body,
        [own, other, up_weight, down_weight, small],
        [shaped((rows, features)), shaped((rows, features)), full],
        "mlp_forward",
        far_outs=[shaped((2 * rows, features)), full],
        scratch=[pltpu.VMEM((2 * rows, wide), BF16)],
        copies=3,
        limit=12,
    )


def mlp_backward(queue, own, other, slope, up_weight, down_weight, block):
    rows, features = own.shape
    wide = up_weight.shape[2]

    def body(
        own_ref, other_ref, slope_ref, up_ref, down_ref,
        own_out, other_out, rows_ref, hid_ref, hid_s, done,
    ):
        copies = copy_rows([own_ref, other_ref], rows_ref, done)
        both = jnp.concatenate([own_ref[...], other_ref[...]], axis=0)
        d_active = nt(both, down_ref[block])
        hid_s[...] = (d_active * slope_ref[...].astype(F32)).astype(BF16)
        copies += copy_rows([hid_s], hid_ref, done, 2)
        out = nt(hid_s[...], up_ref[block]).astype(BF16)
        own_out[...] = out[:rows]
        other_out[...] = out[rows:]
        for copy in copies:
            copy.wait()

    return queue.call(
        body,
        [own, other, slope, up_weight, down_weight],
        [shaped((rows, features)), shaped((rows, features))],
        "mlp_backward",
        far_outs=[shaped((2 * rows, features)), shaped((2 * rows, wide))],
        scratch=[pltpu.VMEM((2 * rows, wide), BF16)],
        copies=3,
        limit=12,
    )


def ln_back(queue, near, far, stream, d_out, mods, at, scale_part, branch=None, narrow=False):
    rows, features = stream.shape
    pieces = [] if branch is None else branch[0]
    counts = [piece[0].shape[0] for piece in pieces]
    inner = sum(counts)
    operands = [near, far, stream, d_out, mods]
    outs = [shaped((8, features), F32)]
    if narrow:
        outs.append(shaped((rows, features)))
    if pieces:
        _, small, bias_row, gate_at, gate_part = branch
        operands += [small] + [half for piece in pieces for half in piece]
        outs += [shaped((count, features), F32) for count in counts]
        outs += [shaped((count, features)) for count in counts]
    inputs = len(operands)

    def body(*refs):
        near_ref, far_ref, x_ref, d_ref, mods_ref = refs[:5]
        sums_ref, *out_refs = refs[inputs:]
        scale = mods_ref[at[0], at[1], scale_part : scale_part + 1, :]
        d_normed = near_ref[...].astype(F32) + far_ref[...].astype(F32)
        normed, spread = normed_of(x_ref[...])
        product = d_normed * normed
        grad = d_normed * (1.0 + scale)
        d_x = d_ref[...].astype(F32) + spread * (
            grad
            - jnp.mean(grad, axis=-1, keepdims=True)
            - normed * jnp.mean(grad * normed, axis=-1, keepdims=True)
        )
        zero = jnp.zeros((1, features), F32)
        gate_sum, bias_sum, rest_sum = zero, zero, zero
        if narrow:
            out_refs[0][...] = d_x.astype(BF16)
        elif inner < rows:
            rest_sum = jnp.sum(d_x[inner:], axis=0, keepdims=True)
        first = 0
        for index, count in enumerate(counts):
            piece_near, piece_far = refs[6 + 2 * index : 8 + 2 * index]
            value = branch_of(piece_near, piece_far, refs[5], bias_row, features)
            part = d_x[first : first + count]
            gate = mods_ref[gate_at[0], gate_at[1], gate_part : gate_part + 1, :]
            d_branch = (gate * part).astype(BF16)
            out_refs[index][...] = part
            out_refs[len(counts) + index][...] = d_branch
            gate_sum = gate_sum + jnp.sum(part * value, axis=0, keepdims=True)
            bias_sum = bias_sum + jnp.sum(d_branch.astype(F32), axis=0, keepdims=True)
            first += count
        sums_ref[...] = jnp.concatenate(
            [
                jnp.sum(product, axis=0, keepdims=True),
                jnp.sum(d_normed, axis=0, keepdims=True),
                gate_sum,
                bias_sum,
                rest_sum,
                jnp.zeros((3, features), F32),
            ],
            axis=0,
        )

    return queue.call(body, operands, outs, "ln_back")


def attn_forward(queue, query, merged, proj_weight, block):
    _, rows, width = query.shape
    local = width // 3
    heads = local // HEAD_DIM
    counts = [part.shape[1] for part in merged]
    total = 2 * sum(counts)
    features = proj_weight.shape[2]
    by_keys = rows < 128

    def body(*refs):
        q_ref, refs = refs[0], refs[1:]
        kv_refs, refs = refs[: len(merged)], refs[len(merged) :]
        proj_ref, lse_ref, own_out, other_out, att_far, q_s, k_s, v_s, o_s, l_s, att_ref, done = refs
        for head in range(heads):
            low = head * HEAD_DIM
            first = 0
            for part, count in zip(kv_refs, counts):
                for side in range(2):
                    at = pl.ds(first, count)
                    k_s[head, at, :] = part[side, :, local + low : local + low + HEAD_DIM]
                    v_s[head, at, :] = part[side, :, 2 * local + low : 2 * local + low + HEAD_DIM]
                    first += count
            for side in range(2):
                q_s[head, side] = q_ref[side, :, low : low + HEAD_DIM]
        for head in range(heads):
            for side in range(2):
                if by_keys:
                    scores = nt(k_s[head], q_s[head, side])
                    highest = jnp.max(scores, axis=0, keepdims=True)
                    raised = jnp.exp2((scores - highest) * EXPONENT)
                    total_row = jnp.sum(raised, axis=0, keepdims=True)
                    out = tn(v_s[head], raised.astype(BF16))
                    o_s[head, side] = (out / total_row).T.astype(BF16)
                    lse_ref[head, side] = highest * EXPONENT + jnp.log2(total_row)
                else:
                    scores = nt(q_s[head, side], k_s[head])
                    highest = jnp.max(scores, axis=1, keepdims=True)
                    raised = jnp.exp2((scores - highest) * EXPONENT)
                    total_row = jnp.sum(raised, axis=1, keepdims=True)
                    out = nn(raised.astype(BF16), v_s[head])
                    o_s[head, side] = (out / total_row).astype(BF16)
                    l_s[head, side] = jnp.broadcast_to(
                        highest * EXPONENT + jnp.log2(total_row), (rows, 128)
                    )
        if not by_keys:
            for head in range(heads):
                for side in range(2):
                    lse_ref[head, side] = l_s[head, side].T[:1]
        for side, out_ref in ((1, other_out), (0, own_out)):
            for head in range(heads):
                low = head * HEAD_DIM
                att_ref[side * rows : (side + 1) * rows, low : low + HEAD_DIM] = o_s[head, side]
            out_ref[...] = nn(
                att_ref[side * rows : (side + 1) * rows, :], proj_ref[block]
            ).astype(BF16)
        for copy in copy_rows([att_ref], att_far, done):
            copy.wait()

    return queue.call(
        body,
        [query, *merged, proj_weight],
        [
            shaped((heads, 2, 1, rows), F32),
            shaped((rows, features)),
            shaped((rows, features)),
        ],
        "attn_forward",
        far_outs=[shaped((2 * rows, local))],
        scratch=[
            pltpu.VMEM((heads, 2, rows, HEAD_DIM), BF16),
            pltpu.VMEM((heads, total, HEAD_DIM), BF16),
            pltpu.VMEM((heads, total, HEAD_DIM), BF16),
            pltpu.VMEM((heads, 2, rows, HEAD_DIM), BF16),
            pltpu.VMEM((heads, 2, 8 if by_keys else rows, 128), F32),
            pltpu.VMEM((2 * rows, local), BF16),
        ],
        copies=1,
        limit=13,
    )


def attn_backward(queue, merged, normers, grads, proj_weight, block):
    count = len(merged)
    width = merged[0].shape[2]
    local = width // 3
    heads = local // HEAD_DIM
    halves = [part.shape[1] for part in merged]
    total = 2 * sum(halves)
    features = proj_weight.shape[2]
    step = min(halves)
    steps = total // step
    unroll = 4 if step * steps > 512 else steps * heads

    def body(*refs):
        m_refs, refs = refs[:count], refs[count:]
        l_refs, refs = refs[:count], refs[count:]
        g_refs, refs = refs[: 2 * count], refs[2 * count :]
        proj_ref, refs = refs[0], refs[1:]
        out_refs, refs = refs[:count], refs[count:]
        row_refs, refs = refs[:count], refs[count:]
        qkv_refs, refs = refs[:count], refs[count:]
        q_s, k_s, kt_s, v_s, g_s, dq_s, dk_s, dv_s, l_s, done = refs
        copies = []
        for index in range(count):
            copies += copy_rows(
                g_refs[2 * index : 2 * index + 2], row_refs[index], done, 2 * index
            )
        first = 0
        for index in range(count):
            rows = halves[index]
            for side in range(2):
                at = pl.ds(first, rows)
                grad = nt(g_refs[2 * index + side][...], proj_ref[block]).astype(BF16)
                for head in range(heads):
                    low = head * HEAD_DIM
                    part = m_refs[index]
                    q_s[head, at, :] = part[side, :, low : low + HEAD_DIM]
                    keys = part[side, :, local + low : local + low + HEAD_DIM]
                    k_s[head, at, :] = keys
                    kt_s[head, :, at] = keys.T
                    v_s[head, at, :] = part[side, :, 2 * local + low : 2 * local + low + HEAD_DIM]
                    g_s[head, at, :] = grad[:, low : low + HEAD_DIM]
                    for piece in range(rows // step):
                        l_s[head, first // step + piece] = l_refs[index][
                            head, side, :, piece * step : (piece + 1) * step
                        ]
                first += rows
        dk_s[...] = jnp.zeros_like(dk_s)
        dv_s[...] = jnp.zeros_like(dv_s)

        def one(index, carry):
            head, piece = index // steps, lax.rem(index, steps)
            at = pl.ds(pl.multiple_of(piece * step, step), step)
            queries, grad = q_s[head, at, :], g_s[head, at, :]
            probs = jnp.exp2(nt(k_s[head], queries) * EXPONENT - l_s[head, piece])
            product = probs * nt(v_s[head], grad)
            delta = jnp.sum(product, axis=0, keepdims=True)
            d_scores = (product - probs * delta).astype(BF16)
            dv_s[head] += nn(probs.astype(BF16), grad)
            dk_s[head] += nn(d_scores, queries)
            dq_s[head, at, :] = (nn(kt_s[head], d_scores) * SCALING).T.astype(BF16)
            return carry

        lax.fori_loop(0, steps * heads, one, 0, unroll=unroll)
        first = 0
        for index in range(count):
            rows = halves[index]
            for side in range(2):
                at = pl.ds(first, rows)
                out = out_refs[index]
                for head in range(heads):
                    low = head * HEAD_DIM
                    out[side, :, low : low + HEAD_DIM] = dq_s[head, at, :]
                    out[side, :, local + low : local + low + HEAD_DIM] = (
                        dk_s[head, at, :] * SCALING
                    ).astype(BF16)
                    out[side, :, 2 * local + low : 2 * local + low + HEAD_DIM] = dv_s[
                        head, at, :
                    ].astype(BF16)
                first += rows
            copies += copy_rows(
                [out_refs[index].at[0], out_refs[index].at[1]],
                qkv_refs[index],
                done,
                2 * count + 2 * index,
            )
        for copy in copies:
            copy.wait()

    def lanes(dtype=BF16):
        return pltpu.VMEM((heads, total, HEAD_DIM), dtype)

    return queue.call(
        body,
        [*merged, *normers, *[half for pair in grads for half in pair], proj_weight],
        [shaped(part.shape) for part in merged],
        "attn_backward",
        far_outs=[shaped((2 * rows, features)) for rows in halves]
        + [shaped((2 * rows, width)) for rows in halves],
        copies=4 * count,
        scratch=[
            lanes(),
            lanes(),
            pltpu.VMEM((heads, HEAD_DIM, total), BF16),
            lanes(),
            lanes(),
            lanes(),
            lanes(F32),
            lanes(F32),
            pltpu.VMEM((heads, steps, 1, step), F32),
        ],
        limit=16,
    )


def split_at(bits, bit):
    place = len(bits) - 1 - bits.index(bit)
    stride = 1 << place
    return [index for index in range(1 << len(bits)) if not index & stride], stride


def weight_grads(queue, pairs, bits, cuts):
    blocks = 1 << len(bits)
    features = pairs[0][0][0].shape[1]
    widths = [rights[0].shape[1] for _, rights in pairs]
    each = features // blocks
    rows = sum(part.shape[0] for part in pairs[0][0])
    far, plan, scratch = [], [], []
    for number, (lefts, rights) in enumerate(pairs):
        for place, parts in enumerate((lefts, rights)):
            first = 0
            for part in parts:
                plan.append((len(far), 2 * number + place, first, part.shape[0]))
                far.append(part)
                first += part.shape[0]
            scratch.append(pltpu.VMEM((rows, parts[0].shape[1]), BF16))
    buffers = len(scratch)
    scratch.append(pltpu.VMEM((blocks, each, sum(widths)), BF16))
    outs, far_outs = [], []
    for columns, _, _ in cuts:
        outs += [shaped((blocks // 2, each, columns))] * 2
    if not cuts:
        far_outs.append(shaped((blocks, each, sum(widths))))

    def body(*refs):
        mine_refs, refs = refs[: len(cuts)], refs[len(cuts) :]
        sources, refs = refs[: len(far)], refs[len(far) :]
        out_refs, refs = refs[: len(outs)], refs[len(outs) :]
        sums_ref, *held = refs
        whole_ref = None if cuts else held.pop(0)
        full, done = held[buffers], held[buffers + 1]
        copies = [
            pltpu.make_async_copy(
                sources[source], held[buffer].at[pl.ds(first, count)], done.at[index]
            )
            for index, (source, buffer, first, count) in enumerate(plan)
        ]
        for copy in copies:
            copy.start()
        low = 0
        ones = jnp.ones((8, rows), BF16)
        for number, width in enumerate(widths):
            for copy, (_, buffer, _, _) in zip(copies, plan):
                if buffer // 2 == number:
                    copy.wait()
            left, right = held[2 * number][...], held[2 * number + 1][...]
            total = tn(left, right).astype(BF16)
            columns = slice(low, low + width)
            for block in range(blocks):
                full[block, :, columns] = total[block * each : (block + 1) * each]
            sums_ref[:, columns] = nn(ones, right)
            low += width
        low = 0
        for index, (width, bit, _) in enumerate(cuts):
            starts, stride = split_at(bits, bit)
            at = mine_refs[index][0] * stride
            for place, start in enumerate(starts):
                out_refs[2 * index][place] = full[start + at, :, low : low + width]
                out_refs[2 * index + 1][place] = full[start + stride - at, :, low : low + width]
            low += width
        if not cuts:
            whole = pltpu.make_async_copy(full, whole_ref, done.at[len(plan)])
            whole.start()
            whole.wait()

    found = queue.call(
        body,
        [],
        [*outs, shaped((8, sum(widths)), F32)],
        "weight_grads",
        scalars=[mine for _, _, mine in cuts],
        far=far,
        far_outs=far_outs,
        scratch=scratch,
        copies=len(plan) + 1,
        limit=20 if len(pairs) == 1 else 28,
    )
    if not cuts:
        return found[1], found[0]
    return list(zip(found[:-1:2], found[1:-1:2])), found[-1]


def halve(queue, kept, moved, mine, bits, bit):
    blocks, each, width = kept.shape
    out = shaped((blocks // 2, each, width))
    starts, stride = split_at(bits, bit)

    def body(mine_ref, kept_ref, moved_ref, next_ref, away_ref):
        at = mine_ref[0] * stride
        for place, out_ref in ((stride - at, away_ref), (at, next_ref)):
            for index, start in enumerate(starts):
                total = kept_ref[start + place].astype(F32) + moved_ref[start + place].astype(F32)
                out_ref[index] = total.astype(BF16)

    return queue.call(body, [kept, moved], [out, out], "halve", scalars=[mine])


def spread_mods(queue, me, columns, features):
    size, latents, blocks, each = columns.shape

    def body(me_ref, in_ref, out_ref, flat):
        for device in range(size):
            block = in_ref[jnp.bitwise_xor(device, me_ref[0])].astype(F32)
            for latent in range(latents):
                flat[latent, :, device * each : (device + 1) * each] = block[latent]
        for latent in range(latents):
            for part in range(6):
                rows = flat[latent, :, part * features : (part + 1) * features]
                for index in range(blocks):
                    out_ref[index, latent, part : part + 1, :] = rows[index : index + 1]

    return queue.call(
        body,
        [columns],
        [shaped((blocks, latents, 6, features), F32)],
        "spread_mods",
        scalars=[me],
        scratch=[pltpu.VMEM((latents, blocks, size * each), F32)],
    )[0]


def collect_sums(queue, sources, recipe, parts):
    features = sources[0].shape[1]
    count = -(-len(recipe) // 8) * 8
    counts = [part.shape[0] for part in parts]

    def body(*refs):
        part_refs, refs = refs[: len(parts)], refs[len(parts) :]
        out_ref, joined_ref = refs[-2:]
        for index, terms in enumerate(recipe):
            total = None
            for source, row in terms:
                term = refs[source][row : row + 1, :]
                total = term if total is None else total + term
            out_ref[index : index + 1, :] = total
        if count > len(recipe):
            out_ref[len(recipe) :, :] = jnp.zeros((count - len(recipe), features), F32)
        first = 0
        for part_ref, rows in zip(part_refs, counts):
            joined_ref[first : first + rows, :] = part_ref[...]
            first += rows

    outs = [shaped((count, features), F32), shaped((sum(counts), features))]
    return queue.call(body, [*parts, *sources], outs, "collect_sums")


def pack_mods(queue, me, own, moved, latents, blocks, size, features):
    each = 6 * features // size
    rows = own.shape[0]

    def body(me_ref, own_ref, moved_ref, out_ref, total_ref, flat):
        total = own_ref[...] + moved_ref[...]
        total_ref[...] = total
        for latent in range(latents):
            for index in range(blocks):
                for part in range(6):
                    row = (index * latents + latent) * 6 + part
                    flat[latent, index : index + 1, part * features : (part + 1) * features] = total[
                        row : row + 1
                    ]
        for device in range(size):
            for latent in range(latents):
                out_ref[jnp.bitwise_xor(device, me_ref[0]), latent] = flat[
                    latent, :, device * each : (device + 1) * each
                ].astype(BF16)

    return queue.call(
        body,
        [own, moved],
        [shaped((size, latents, blocks, each)), shaped((rows, features), F32)],
        "pack_mods",
        scalars=[me],
        scratch=[pltpu.VMEM((latents, blocks, 6 * features), F32)],
    )


def partners(size, bit):
    return [(index, index ^ bit) for index in range(size)]


def bits_of(size):
    bits = []
    while (1 << len(bits)) < size:
        bits.append(1 << len(bits))
    assert (1 << len(bits)) == size
    return bits


class Links:
    def __init__(self, dp_size, tensor_size):
        self.dp_size = dp_size
        self.tensor_size = tensor_size
        self.dp_bits = bits_of(dp_size)
        me = lax.axis_index("dp")
        self.me = me.reshape(1)
        self.core = lax.rem(lax.axis_index("tensor"), 2).reshape(1)
        self.mine = {bit: lax.rem(me // bit, 2).reshape(1) for bit in self.dp_bits}

    def swap(self, value):
        return lax.ppermute(value, "tensor", partners(self.tensor_size, 1))

    def cross(self, value):
        return lax.ppermute(value, "tensor", partners(self.tensor_size, 2))

    def dp_move(self, value, bit):
        return lax.ppermute(value, "dp", partners(self.dp_size, bit))

    def gather_relative(self, value):
        held = value[None]
        for bit in self.dp_bits:
            held = jnp.concatenate([held, self.dp_move(held, bit)], axis=0)
        return held

    def exchange_relative(self, value, total=None):
        held = value
        for bit in reversed(self.dp_bits):
            split = held.reshape((self.dp_size // (2 * bit), 2, bit) + held.shape[1:])
            away = split[:, 1]
            if total is None:
                moved = self.dp_move(away, bit)
            else:
                sent = jnp.concatenate([away.astype(F32).reshape(-1), total])
                came = self.dp_move(sent, bit)
                moved = came[: away.size].reshape(away.shape).astype(held.dtype)
                total = total + came[away.size :]
            held = jnp.stack([split[:, 0], moved], axis=1).reshape(held.shape)
        return held if total is None else (held, total)

    def sum_relative(self, value):
        held = value
        for bit in reversed(self.dp_bits):
            moved = self.dp_move(held[bit:].astype(BF16), bit)
            held = held[:bit].astype(F32) + moved.astype(F32)
        return held[0]


class ScatterSum:
    def __init__(self, queue, links, kept, away, order):
        self.queue, self.links, self.kept = queue, links, kept
        self.order = list(order)
        self.open = sorted(self.order, reverse=True)
        self.send(away)

    def send(self, away):
        bit = self.order.pop(0)
        self.open.remove(bit)
        self.moved = self.links.dp_move(away, bit)

    def step(self):
        if self.order:
            bit = self.order[0]
            self.kept, away = halve(
                self.queue, self.kept, self.moved, self.links.mine[bit], self.open, bit
            )
            self.send(away)


def last_sums(queue, parts):
    shapes = [part.kept.shape[1:] for part in parts]

    def body(*refs):
        for index in range(len(parts)):
            kept_ref, moved_ref = refs[2 * index : 2 * index + 2]
            total = kept_ref[0].astype(F32) + moved_ref[0].astype(F32)
            refs[2 * len(parts) + index][...] = total

    operands = [value for part in parts for value in (part.kept, part.moved)]
    return queue.call(body, operands, [shaped(shape, F32) for shape in shapes], "last_sums")


def emit_wide(queue, parts, wide):
    each = parts[0].shape[0]

    def body(up_ref, down_ref, both_ref, up_out, down_out):
        up_out[0] = up_ref[...]
        down_out[0] = down_ref[...]
        up_out[1] = both_ref[:, :wide].astype(F32)
        down_out[1] = both_ref[:, wide:].astype(F32)

    features = parts[1].shape[1]
    outs = [shaped((2, each, wide), F32), shaped((2, each, features), F32)]
    return queue.call(body, parts, outs, "emit_wide")


def emit_attention(queue, encoder, decoder, local):
    each = decoder.shape[0]

    def body(kept_ref, moved_ref, dec_ref, proj_ref, qkv_ref):
        total = kept_ref[0].astype(F32) + moved_ref[0].astype(F32)
        for index, value in enumerate((total, dec_ref[...])):
            proj_ref[index] = value[:, :local]
            for part in range(3):
                qkv_ref[index, part] = value[:, (part + 1) * local : (part + 2) * local]

    outs = [shaped((2, each, local), F32), shaped((2, 3, each, local), F32)]
    return queue.call(body, [encoder.kept, encoder.moved, decoder], outs, "emit_attention")


def reduced(queue, links, pairs):
    whole, sums = weight_grads(queue, pairs, sorted(links.dp_bits, reverse=True), [])
    flat = whole.reshape(-1, whole.shape[-1])
    return lax.psum_scatter(flat, "dp", scatter_dimension=0, tiled=True), sums


def scatter_sums(queue, links, pairs, cuts):
    bits = sorted(links.dp_bits, reverse=True)
    found, sums = weight_grads(
        queue, pairs, bits, [(columns, order[0], links.mine[order[0]]) for columns, order in cuts]
    )
    pieces = [
        ScatterSum(queue, links, kept, away, order)
        for (kept, away), (_, order) in zip(found, cuts)
    ]
    return pieces, sums


class Weights:
    def __init__(self, qkv, proj, up, down, small, mods):
        self.qkv, self.proj, self.up, self.down = qkv, proj, up, down
        self.small, self.mods = small, mods


class Chunk:
    def __init__(self, queue, links, weights, block, latent, family):
        self.queue, self.links, self.weights = queue, links, weights
        self.block, self.latent, self.at = block, latent, (block, latent)
        self.family = family
        family.append(self)

    def enter(self, stream, normed):
        self.x = stream
        self.normed_attn = (normed, self.links.swap(normed))

    def qkv(self):
        w = self.weights
        self.merged, self.normed_attn_rows = qkv_forward(
            self.queue, *self.normed_attn, w.qkv, w.small, self.block
        )

    def attention(self):
        merged = [chunk.merged for chunk in self.family]
        self.normer, own, other, self.attended_rows = attn_forward(
            self.queue, self.merged, merged, self.weights.proj, self.block
        )
        self.part = (own, self.links.swap(other))

    def near(self):
        near = near_sum(self.queue, *self.part)
        self.sum = (near, self.links.cross(near))

    def merge(self):
        w = self.weights
        self.branch_attn = self.sum
        self.middle, normed = merge_attn(
            self.queue, self.x, *self.branch_attn, w.small, w.mods, self.at
        )
        self.normed_mlp = (normed, self.links.swap(normed))

    def mlp(self):
        w = self.weights
        own, other, self.slope, self.normed_mlp_rows, self.active_rows = mlp_forward(
            self.queue, *self.normed_mlp, w.up, w.down, w.small, self.block
        )
        self.part = (own, self.links.swap(other))

    def start_back(self, d_out, d_branch):
        self.d_out = d_out
        self.d_branch_mlp = (d_branch, self.links.swap(d_branch))

    def mlp_back(self):
        w = self.weights
        own, other, self.d_branch_mlp_rows, self.d_hidden_rows = mlp_backward(
            self.queue, *self.d_branch_mlp, self.slope, w.up, w.down, self.block
        )
        self.part = (own, self.links.swap(other))

    def merge_back(self):
        w = self.weights
        branch = ([self.branch_attn], w.small, PROJ_BIAS + self.block, self.at, GATE_ATTN)
        self.mlp_sums, self.d_middle, grad = ln_back(
            self.queue, *self.sum, self.middle, self.d_out, w.mods, self.at, SCALE_MLP, branch
        )
        self.d_branch_attn = (grad, self.links.swap(grad))

    def attention_back(self):
        family = self.family
        grads = attn_backward(
            self.queue,
            [chunk.merged for chunk in family],
            [chunk.normer for chunk in family],
            [chunk.d_branch_attn for chunk in family],
            self.weights.proj,
            self.block,
        )
        count = len(family)
        for index, chunk in enumerate(family):
            chunk.d_qkv, chunk.d_branch_attn_rows, chunk.d_qkv_rows = grads[index::count]

    def qkv_back(self):
        own, other = qkv_backward(self.queue, self.d_qkv, self.weights.qkv, self.block)
        self.part = (own, self.links.swap(other))

    def leave_back(self, branch=None, narrow=False):
        w = self.weights
        self.attn_sums, *rest = ln_back(
            self.queue,
            *self.sum,
            self.x,
            self.d_middle,
            w.mods,
            self.at,
            SCALE_ATTN,
            branch,
            narrow,
        )
        return rest


def rows_of(chunks, name):
    return [getattr(chunk, name + "_rows") for chunk in chunks]


def on_device(dp_size, tensor_size, *arguments):
    (
        tokens_long,
        tokens_short,
        cond_long,
        cond_short,
        perm_long,
        perm_short,
        ada_weight,
        ada_bias,
        qkv_weight,
        qv_bias,
        proj_weight,
        proj_bias,
        up_weight,
        up_bias,
        down_weight,
        down_bias,
        mask_token,
        cot_long,
        cot_short,
    ) = arguments
    assert tokens_long.shape[0] == 1 and tokens_short.shape[0] == 1
    queue = Queue()
    links = Links(dp_size, tensor_size)
    core = links.core
    features = tokens_long.shape[2]
    wide = up_weight.shape[2]
    local = qv_bias.shape[2]
    tokens = (tokens_long[0], tokens_short[0])
    cots = (cot_long[0], cot_short[0])
    perms = (perm_long, perm_short)
    lengths = tuple(rows.shape[0] for rows in tokens)
    kept = tuple(length // 2 for length in lengths)

    cond = jnp.concatenate([cond_long, cond_short]).astype(F32)
    acts = links.gather_relative(jax.nn.silu(cond).astype(BF16))
    flat_acts = acts.reshape(-1, features)
    columns = jnp.einsum("nd,ldm->nlm", flat_acts, ada_weight, preferred_element_type=F32)
    columns = (columns + ada_bias.astype(F32)[None]).astype(BF16)
    columns = links.exchange_relative(columns.reshape((dp_size, 2) + columns.shape[1:]))

    table_width = max(features, wide, 3 * local)

    def padded(rows):
        return jnp.pad(rows.astype(F32), ((0, 0), (0, table_width - rows.shape[1])))

    qkv_bias = jnp.concatenate(
        [qv_bias[:, 0], jnp.zeros_like(qv_bias[:, 0]), qv_bias[:, 1]], axis=1
    )
    small = jnp.concatenate([padded(proj_bias), padded(down_bias), padded(up_bias), padded(qkv_bias)])

    long_half, short_half = kept[0] // 2, kept[1] // 2
    quarter = long_half // 2
    enc_rows = [
        Rows((0, long_half, quarter)),
        Rows((quarter, long_half, quarter)),
        Rows((0, short_half, short_half)),
    ]
    table_places = [Rows((0, long_half, long_half)), Rows((0, short_half, short_half))]
    masked_places = [
        Rows((kept[0], long_half, long_half)),
        Rows((kept[1], short_half, short_half)),
    ]
    dec_rows = [
        table_places[0],
        masked_places[0],
        Rows((0, short_half, short_half), (kept[1], short_half, short_half)),
    ]
    enc_latents, dec_latents = (0, 0, 1), (0, 0, 1)

    streams = [
        gather_rows(queue, core, perms[latent], tokens[latent], rows, F32)
        for latent, rows in zip(enc_latents, enc_rows)
    ]
    mods = spread_mods(queue, links.me, columns, features)
    weights = Weights(
        jnp.transpose(qkv_weight, (0, 2, 3, 1)).reshape(2, 3 * local, features),
        proj_weight,
        up_weight,
        down_weight,
        small,
        mods,
    )
    families = {(block, latent): [] for block in (0, 1) for latent in (0, 1)}

    def chunks_of(block, latents):
        return [
            Chunk(queue, links, weights, block, latent, families[block, latent])
            for latent in latents
        ]

    encoder = chunks_of(0, enc_latents)
    decoder = chunks_of(1, dec_latents)
    ea, eb, es = encoder
    dk, dm, dt = decoder

    for chunk, stream in zip(encoder, streams):
        chunk.enter(stream, ln_open(queue, stream, mods, chunk.at))
    for chunk in encoder:
        chunk.qkv()
    ea.attention()
    eb.attention()
    ea.near()
    es.attention()
    eb.near()
    es.near()
    perms_later, filler, cots_later = queue.tie(perms, mask_token, cots)
    filler = filler.astype(F32)[None]
    waves = []
    for length in lengths:
        side = math.isqrt(length)
        quarter_wave = features // 4
        frequency = 1.0 / 10000.0 ** (jnp.arange(quarter_wave, dtype=F32) / quarter_wave)
        angle = jnp.arange(side, dtype=jnp.int32).astype(F32)[:, None] * frequency[None, :]
        waves.append(jnp.concatenate([jnp.sin(angle), jnp.cos(angle)], axis=1))
    masked = table_rows(queue, core, perms_later[0], waves[0], masked_places[0], filler)
    dm.enter(masked, ln_open(queue, masked, mods, dm.at))
    ea.merge()
    dm.qkv()
    ea.mlp()
    eb.merge()
    ea.near()
    es.merge()
    eb.mlp()
    es.mlp()
    eb.near()
    es.near()
    table_long = table_rows(queue, core, perms_later[0], waves[0], table_places[0])
    table_short = table_rows(queue, core, perms_later[1], waves[1], table_places[1])
    masked_short = table_rows(queue, core, perms_later[1], waves[1], masked_places[1], filler)
    d_out = [
        gather_rows(queue, core, perms_later[latent], cots_later[latent], rows, BF16)
        for latent, rows in zip(dec_latents, dec_rows)
    ]
    first_sums = []
    for chunk, grad in zip(decoder, d_out):
        d_branch, sums = first_grad(queue, grad, mods, chunk.at)
        first_sums.append(sums)
        chunk.start_back(grad, d_branch)

    pieces = [(chunk.middle, *chunk.sum) for chunk in encoder]
    for chunk in encoder:
        chunk.branch_mlp = chunk.sum
    dk.enter(*merge_mlp(queue, pieces[:2], small, mods, (0, 0), table_long, None))
    dt.enter(*merge_mlp(queue, pieces[2:], small, mods, (0, 1), table_short, masked_short))
    dk.qkv()
    dk.attention()
    dt.qkv()
    dk.near()
    dm.attention()
    dt.attention()
    dm.near()
    dt.near()
    dk.merge()
    dk.mlp()
    dm.merge()
    forward = {dk: dk.part}
    dk.mlp_back()
    dm.mlp()
    dk.near()
    forward[dm] = dm.part
    dm.mlp_back()
    dt.merge()
    dm.near()
    dt.mlp()
    forward[dt] = dt.part
    dt.mlp_back()
    dt.near()

    y_first, z_first = list(links.dp_bits), list(links.dp_bits)
    if len(z_first) > 1:
        z_first[0], z_first[1] = z_first[1], z_first[0]

    def wide_pairs(chunks):
        return [
            (rows_of(chunks, "normed_mlp"), rows_of(chunks, "d_hidden")),
            (rows_of(chunks, "d_branch_mlp"), rows_of(chunks, "active")),
        ]

    def attention_pairs(chunks):
        return [
            (rows_of(chunks, "d_branch_attn"), rows_of(chunks, "attended")),
            (rows_of(chunks, "normed_attn"), rows_of(chunks, "d_qkv")),
        ]

    sums_there = {}

    def forward_sum(chunk):
        near = near_sum(queue, *forward[chunk])
        sums_there[chunk] = (near, links.cross(near))

    def finished(*chunks):
        return finish(
            queue,
            [
                (chunk.middle, *sums_there[chunk], d_out[decoder.index(chunk)], chunk.at)
                for chunk in chunks
            ],
            small,
            mods,
        )

    dk.merge_back()
    dec_wide, dec_wide_sums = reduced(queue, links, wide_pairs(decoder))
    dm.merge_back()
    forward_sum(dk)
    forward_sum(dm)
    dm.attention_back()
    decoded_long, long_sums = finished(dk, dm)
    decoded_other = links.swap(decoded_long)
    dk.qkv_back()
    dm.qkv_back()
    dk.near()
    dm.near()
    dt.merge_back()
    dt.attention_back()
    dt.qkv_back()
    dt.near()
    result_long = place_rows(
        queue, core, perms_later[0], decoded_long, decoded_other, dec_rows[:2], 0
    )
    enc_branch = (small, DOWN_BIAS, (0, 0), GATE_MLP)
    short_branch = (small, DOWN_BIAS, (0, 1), GATE_MLP)
    d_a, d_b, grad_a, grad_b = dk.leave_back(([ea.branch_mlp, eb.branch_mlp], *enc_branch))
    ea.start_back(d_a, grad_a)
    eb.start_back(d_b, grad_b)

    ea.mlp_back()
    eb.mlp_back()
    ea.near()
    eb.near()
    (dec_attn,), dec_attn_sums = scatter_sums(
        queue, links, attention_pairs(decoder), [(4 * local, y_first)]
    )
    dm.leave_back()
    d_short, grad_short = dt.leave_back(([es.branch_mlp], *short_branch))
    es.start_back(d_short, grad_short)
    es.mlp_back()
    es.near()
    ea.merge_back()
    (enc_up, enc_down), enc_wide_sums = scatter_sums(
        queue, links, wide_pairs(encoder), [(wide, y_first), (wide, z_first)]
    )
    dec_attn.step()
    eb.merge_back()
    forward_sum(dt)
    ea.attention_back()
    ea.qkv_back()
    eb.qkv_back()
    ea.near()
    eb.near()
    enc_up.step()
    enc_down.step()
    es.merge_back()
    es.attention_back()
    es.qkv_back()
    es.near()
    (enc_attn,), enc_attn_sums = scatter_sums(
        queue, links, attention_pairs(encoder), [(4 * local, y_first)]
    )
    enc_up.step()
    enc_down.step()
    own_tokens = []
    for chunk in (ea, eb, es):
        own_tokens += chunk.leave_back(narrow=True)
    decoded_short, short_sums = finished(dt)
    decoded_other = links.swap(decoded_short)
    dec_attn.step()

    sources, recipe = [], []

    def row(array, index):
        for place, source in enumerate(sources):
            if source is array:
                return place, index
        sources.append(array)
        return len(sources) - 1, index

    for block, chunks in ((0, encoder), (1, decoder)):
        for latent in (0, 1):
            members = [chunk for chunk in chunks if chunk.latent == latent]
            if block == 0:
                gates = [row((dk, dt)[latent].attn_sums, 2)]
            else:
                gates = [row((long_sums, short_sums)[latent], latent)]
            recipe += [
                [row(chunk.attn_sums, 1) for chunk in members],
                [row(chunk.attn_sums, 0) for chunk in members],
                [row(chunk.mlp_sums, 2) for chunk in members],
                [row(chunk.mlp_sums, 1) for chunk in members],
                [row(chunk.mlp_sums, 0) for chunk in members],
                gates,
            ]
    recipe += [
        [row(chunk.mlp_sums, 3) for chunk in encoder],
        [row(chunk.mlp_sums, 3) for chunk in decoder],
        [row(chunk.attn_sums, 3) for chunk in (dk, dt)],
        [row(sums, 0) for sums in first_sums],
        [row(chunk.attn_sums, 4) for chunk in (dm, dt)],
    ]
    own_sums, joined = collect_sums(queue, sources, recipe, own_tokens)
    enc_attn.step()
    enc_up, enc_down = last_sums(queue, [enc_up, enc_down])
    up_grad, down_grad = emit_wide(queue, [enc_up, enc_down, dec_wide], wide)
    packed, all_sums = pack_mods(
        queue, links.me, own_sums, links.swap(own_sums), 2, 2, dp_size, features
    )
    totals = jnp.concatenate(
        [all_sums[24:29].reshape(-1), enc_wide_sums[0, :wide], dec_wide_sums[0, :wide]]
        + [
            sums[0, first : first + local]
            for sums in (enc_attn_sums, dec_attn_sums)
            for first in (local, 3 * local)
        ]
    )
    mine, totals = links.exchange_relative(packed, totals)
    mine, totals, enc_attn.moved = lax.optimization_barrier((mine, totals, enc_attn.moved))
    enc_attn.step()
    mine = queue.tie(mine)
    result_short = place_rows(
        queue, core, perms_later[1], decoded_short, decoded_other, dec_rows[2:], 0
    )
    flat_mine = mine.reshape((-1,) + mine.shape[2:])
    grad_ada = jnp.einsum("nd,nlm->ldm", flat_acts, flat_mine, preferred_element_type=F32)
    grad_ada_bias = jnp.sum(flat_mine.astype(F32), axis=0)
    d_acts = jnp.einsum("nlm,ldm->nd", flat_mine, ada_weight, preferred_element_type=F32)
    d_act = links.sum_relative(d_acts.reshape(dp_size, 2, features))
    gate = jax.nn.sigmoid(cond)
    d_cond = (d_act * gate * (1.0 + cond * (1.0 - gate))).astype(BF16)

    proj_out = totals[: 2 * features].reshape(2, features)
    down_out = totals[2 * features : 4 * features].reshape(2, features)
    mask_out = totals[4 * features : 5 * features]
    first = 5 * features
    up_out = totals[first : first + 2 * wide].reshape(2, wide)
    first += 2 * wide
    qv_out = totals[first : first + 4 * local].reshape(2, 2, local)

    joined_other = links.swap(joined)
    d_tokens = (
        place_rows(queue, core, perms_later[0], joined, joined_other, enc_rows[:2], 0),
        place_rows(queue, core, perms_later[1], joined, joined_other, enc_rows[2:], long_half),
    )
    (dec_attn,) = last_sums(queue, [dec_attn])
    proj_grad, qkv_grad = emit_attention(queue, enc_attn, dec_attn, local)

    return (
        result_long[None],
        result_short[None],
        d_tokens[0][None],
        d_tokens[1][None],
        d_cond[:1],
        d_cond[1:],
        grad_ada,
        grad_ada_bias,
        jnp.transpose(qkv_grad, (0, 2, 1, 3)),
        qv_out,
        jnp.transpose(proj_grad, (0, 2, 1)),
        proj_out,
        up_grad,
        up_out,
        jnp.transpose(down_grad, (0, 2, 1)),
        down_out,
        mask_out,
    )


def solution(mesh):
    in_specs = (
        P("dp", None, None),
        P("dp", None, None),
        P("dp", None),
        P("dp", None),
        P("dp", None),
        P("dp", None),
        P(None, None, "dp"),
        P(None, "dp"),
        P(None, None, None, "tensor"),
        P(None, None, "tensor"),
        P(None, "tensor", None),
        P(),
        P(None, None, "tensor"),
        P(None, "tensor"),
        P(None, "tensor", None),
        P(),
        P(),
        P("dp", None, None),
        P("dp", None, None),
    )
    out_specs = (
        P("dp", None, None),
        P("dp", None, None),
        P("dp", None, None),
        P("dp", None, None),
        P("dp", None),
        P("dp", None),
        P(None, None, "dp"),
        P(None, "dp"),
        P(None, "dp", None, "tensor"),
        P(None, None, "tensor"),
        P(None, "tensor", "dp"),
        P(),
        P(None, "dp", "tensor"),
        P(None, "tensor"),
        P(None, "tensor", "dp"),
        P(),
        P(),
    )

    def step(*arguments):
        return on_device(mesh.shape["dp"], mesh.shape["tensor"], *arguments)

    return jax.shard_map(
        step, mesh=mesh, in_specs=in_specs, out_specs=out_specs, check_vma=False
    )
```
